32 devices in a mesh: band: 8 (over z, x), pw: 4 (over y, core).
Axes of the slice: x: 2, y: 2, z: 4, core: 2. Of those that a mesh axis runs over, the one named last changes fastest.
Arguments:
- coefficients: float32 [8, 2, 32768], P('band', None, 'pw'), may hold values from -1.5 to 1.5
- pw_index: int32 [32768], P('pw'), may hold values from 0 to 16383, as said below
- col_index: int32 [512], replicated, may hold values from 0 to 16383, as said below
- occupation: int32 [8], P('band'), may hold values from 1 to 2
- v_local: float32 [128, 16384], P('pw'), may hold values from 0.1 to 9
- rho_in: float32 [128, 16384], P('pw', 'band'), may hold values from 1 to 2
- rho_hist: float32 [4, 128, 16384], P(None, 'pw', 'band'), may hold values from 1 to 2
- resid_hist: float32 [4, 128, 16384], P(None, 'pw', 'band'), may hold values from -12 to 12
Outputs:
- density: float32 [128, 16384], P('pw', 'band')
- mixed_density: float32 [128, 16384], P('pw', 'band')
- band_energy: float32 [8], P('band')
- residual_norm: float32 [], replicated
The draws below stay inside these ranges and needn't reach their ends.
Inputs may be any that keep to these rules, and one draw needn't show every extreme that they name: `pw_index`: within the block of 8192 entries of each index of pw all values are distinct; every block holds 0 and the largest value, and besides them the values whose frequency kz, counted from -64 to 64, has the smallest magnitude, ties at the largest magnitude taken at random. `col_index`: all values are distinct; they are 0, the largest value, and the columns of smallest kx^2 + ky^2 with kx, ky counted from -64 to 64, ties at the largest such value taken at random, in an order drawn from the seed.
All inputs are finite; a program needn't handle non-finite values.
Results may differ from the reference program's by a relative error of at most 0.00016.
Values sent between devices are 32-bit elements; how exact they have to be, the bound alone decides.
No kernel may reach another device: no remote copies, remote signals or barrier semaphores. Data moves between devices by JAX's collectives and lax.ppermute only.
A program may use at most 64 MiB of HBM per device.

```python
import math
import jax
import jax.numpy as jnp
from jax import lax

NG = 128
COLS_DEV = 128
PW_DEV = 8192
HIST = 4
BANDS = 8
NCOL = 512
NPW = 32768
N_PW = 4


def draw_pw_index(key, part):
    count_all = NG * COLS_DEV

    def one_block(device):
        subkey = jax.random.fold_in(jax.random.fold_in(key, 11), device)
        random_rank = jax.random.permutation(subkey, count_all).astype(jnp.int32)
        entries = jnp.arange(count_all, dtype=jnp.int32)
        freq_z = entries // COLS_DEV
        magnitude = jnp.minimum(freq_z, NG - freq_z)
        scores = magnitude * count_all + random_rank
        scores = jnp.where(entries == 0, -2, scores)
        scores = jnp.where(entries == count_all - 1, -1, scores)
        _, chosen = lax.top_k(-scores, PW_DEV)
        shuffle = jax.random.permutation(jax.random.fold_in(subkey, 3), PW_DEV)
        return chosen.astype(jnp.int32)[shuffle]
    return jax.vmap(one_block)(jnp.arange(N_PW)).reshape(-1)


def draw_col_index(key, part):
    count_all = NG * NG
    subkey = jax.random.fold_in(key, 23)
    random_rank = jax.random.permutation(subkey, count_all).astype(jnp.int32)
    entries = jnp.arange(count_all, dtype=jnp.int32)
    freq_x = entries // NG
    freq_y = entries % NG
    mag_x = jnp.minimum(freq_x, NG - freq_x)
    mag_y = jnp.minimum(freq_y, NG - freq_y)
    scores = (mag_x * mag_x + mag_y * mag_y) * count_all + random_rank
    scores = jnp.where(entries == 0, -2, scores)
    scores = jnp.where(entries == count_all - 1, -1, scores)
    _, chosen = lax.top_k(-scores, NCOL)
    shuffle = jax.random.permutation(jax.random.fold_in(key, 29), NCOL)
    return chosen.astype(jnp.int32)[shuffle]


def signed_freq(values):
    as_float = values.astype(jnp.float32)
    return jnp.where(values > NG // 2, as_float - NG, as_float)


def draw_coefficients(key, part):
    pw_values = draw_pw_index(key, part)
    col_values = draw_col_index(key, part)
    device = (jnp.arange(NPW) // PW_DEV).astype(jnp.int32)
    slot_pos = pw_values % COLS_DEV
    column = col_values[device * COLS_DEV + slot_pos]
    freq_z = signed_freq(pw_values // COLS_DEV)[None, :]
    freq_x = signed_freq(column // NG)[None, :]
    freq_y = signed_freq(column % NG)[None, :]
    centre = jax.random.uniform(jax.random.fold_in(key, 41), (BANDS, 3), jnp.float32, 0.0, NG * 1.0)
    spread = jnp.exp(jax.random.uniform(jax.random.fold_in(key, 43), (BANDS, 1), jnp.float32, math.log(2.0), math.log(5.0)))
    radius = freq_z * freq_z + freq_x * freq_x + freq_y * freq_y
    envelope = jnp.exp(-0.5 * radius / (spread * spread))
    phases = -2.0 * math.pi / NG * (centre[:, 0:1] * freq_z + centre[:, 1:2] * freq_x + centre[:, 2:3] * freq_y)
    band_norm = jnp.sqrt(jnp.sum(envelope * envelope, axis=1, keepdims=True))
    smooth = envelope / band_norm
    rough_part = jnp.clip(jax.random.normal(jax.random.fold_in(key, 47), (BANDS, 2, NPW), jnp.float32), -4.0, 4.0)
    rough_part = rough_part * jnp.sqrt(1.0 / (2.0 * NPW))
    wave_part = jnp.stack([smooth * jnp.cos(phases), smooth * jnp.sin(phases)], axis=1)
    return wave_part + rough_part


def draw_v_local(key, part):
    plane_pos = jnp.arange(NG, dtype=jnp.float32)[:, None]
    cell_pos = jnp.arange(NG * NG, dtype=jnp.float32)[None, :]
    row_pos = jnp.floor(cell_pos / NG)
    col_pos = cell_pos - row_pos * NG
    shifts = jax.random.uniform(jax.random.fold_in(key, 51), (3,), jnp.float32, 0.0, NG * 1.0)
    turn = 2.0 * math.pi / NG
    waves = (jnp.cos(turn * (plane_pos + shifts[0])) + jnp.cos(turn * (row_pos + shifts[1])) + jnp.cos(turn * (col_pos + shifts[2]))) / 3.0
    smooth = jnp.exp(1.2 * waves)
    rough_part = jnp.exp(jax.random.uniform(jax.random.fold_in(key, 53), (NG, NG * NG), jnp.float32, math.log(0.5), math.log(2.0)))
    return smooth * rough_part


def draw_resid_hist(key, part):
    plane_pos = jnp.arange(NG, dtype=jnp.float32)[:, None]
    row_pos = jnp.floor(jnp.arange(NG * NG, dtype=jnp.float32) / NG)[None, :]
    profile = jnp.exp(jnp.log(10.0) * 0.5 * (plane_pos + row_pos) / NG)
    values = jax.random.normal(key, (HIST, NG, NG * NG), jnp.float32)
    return 0.3 * jnp.clip(values, -4.0, 4.0) * profile


def with_ends(drawn, stream_key, smallest, top_value):
    dims = drawn.shape
    index_at = [jax.random.randint(jax.random.fold_in(stream_key, axis), (), 0, dims[axis]) for axis in range(len(dims))]
    drawn = drawn.at[tuple(index_at)].set(smallest)
    longest = dims.index(max(dims))
    index_at[longest] = (index_at[longest] + 1) % dims[longest]
    return drawn.at[tuple(index_at)].set(top_value)


def block_scale(key, extent, shards, smallest, largest):
    factor_of = 1.0
    for axis_at, blocks in shards:
        draws = jax.random.uniform(jax.random.fold_in(jax.random.fold_in(key, 6), axis_at), (blocks,), jnp.float32, smallest / len(shards), largest / len(shards))
        factor_of = factor_of * jnp.repeat(jnp.exp(draws), extent[axis_at] // blocks).reshape((-1,) + (1,) * (len(extent) - 1 - axis_at))
    return factor_of


def setup_inputs(seed: int = 0) -> dict:
    streams_of = jax.random.split(jax.random.key(seed), 9)
    return {
        "coefficients": draw_coefficients(jax.random.fold_in(streams_of[8], 71), 0),
        "pw_index": draw_pw_index(jax.random.fold_in(streams_of[8], 71), 0),
        "col_index": draw_col_index(jax.random.fold_in(streams_of[8], 71), 0),
        "occupation": with_ends(jax.random.randint(streams_of[3], (BANDS,), 1, 3), jax.random.fold_in(streams_of[3], 1), 1, 2).astype(jnp.int32),
        "v_local": draw_v_local(jax.random.fold_in(streams_of[8], 71), 0),
        "rho_in": jnp.clip(1.0 + 1.0 * jax.random.uniform(streams_of[5], (NG, NG * NG), jnp.float32) ** block_scale(streams_of[5], (NG, NG * NG), ((0, 4), (1, 8)), -0.2, 0.2), 1.0, 2.0),
        "rho_hist": jnp.clip(1.0 + 1.0 * jax.random.uniform(streams_of[6], (HIST, NG, NG * NG), jnp.float32) ** block_scale(streams_of[6], (HIST, NG, NG * NG), ((1, 4), (2, 8)), -0.2, 0.2), 1.0, 2.0),
        "resid_hist": draw_resid_hist(jax.random.fold_in(streams_of[8], 71), 0),
    }


def reference(coefficients, pw_index, col_index, occupation, v_local, rho_in, rho_hist, resid_hist):
    device = (jnp.arange(NPW) // PW_DEV).astype(jnp.int32)
    slot = pw_index % COLS_DEV
    freq_z = pw_index // COLS_DEV
    column = col_index[device * COLS_DEV + slot]
    flat = freq_z * (NG * NG) + column
    weights = occupation.astype(jnp.float32) / BANDS
    potential = v_local.reshape(NG, NG, NG)

    def one_band(total, inputs):
        coeff, weight = inputs
        real_part = jnp.zeros((NG * NG * NG,), jnp.float32).at[flat].set(coeff[0])
        imag_part = jnp.zeros((NG * NG * NG,), jnp.float32).at[flat].set(coeff[1])
        grid = lax.complex(real_part, imag_part).reshape(NG, NG, NG)
        wave = jnp.fft.ifftn(grid) * (NG * NG * NG)
        power = jnp.real(wave) ** 2 + jnp.imag(wave) ** 2
        energy = jnp.sum(potential * power) / (NG * NG * NG)
        return (total + weight * power, energy)
    start = jnp.zeros((NG, NG, NG), jnp.float32)
    total, band_energy = lax.scan(one_band, start, (coefficients, weights))
    density = total.reshape(NG, NG * NG)
    vectors = jnp.concatenate([resid_hist, (density - rho_in)[None]], axis=0)
    inputs = jnp.concatenate([rho_hist, rho_in[None]], axis=0)
    gram = jnp.einsum('izc,jzc->ij', vectors, vectors, precision=lax.Precision.HIGHEST) / (NG * NG * NG)
    residual_norm = jnp.sqrt(gram[HIST, HIST])
    factor = jnp.linalg.cholesky(gram)
    solved = jax.scipy.linalg.cho_solve((factor, True), jnp.ones((HIST + 1,), jnp.float32))
    coef = solved / jnp.sum(solved)
    mixed_density = jnp.einsum('i,izc->zc', coef, inputs + 0.8 * vectors, precision=lax.Precision.HIGHEST)
    return (density, mixed_density, band_energy, residual_norm)
```

```python
import math

import jax
import jax.numpy as jnp
import numpy as np
from jax import lax
from jax.experimental import pallas as pl
from jax.experimental.pallas import tpu as pltpu
from jax.sharding import PartitionSpec as P

F32 = jnp.float32
BF16 = jnp.bfloat16
LANES = 128
VMEM_LIMIT = 40 * 1024 * 1024


def up(value, multiple):
    return -(-value // multiple) * multiple


def split_np(table):
    high = table.astype(np.float32).astype(jnp.bfloat16)
    low = (table - high.astype(np.float64)).astype(np.float32).astype(jnp.bfloat16)
    return high, low


def split(value):
    high = value.astype(BF16)
    low = (value - high.astype(F32)).astype(BF16)
    return high, low


def dot(left, right):
    return jnp.dot(left, right, preferred_element_type=F32)


def dot_t(left, right):
    return lax.dot_general(left, right, (((1,), (1,)), ((), ())), preferred_element_type=F32)


def dot3(left, right_high, right_low):
    high, low = split(left)
    return dot(high, right_high) + dot(high, right_low) + dot(low, right_high)


def signed(length):
    index = np.arange(length)
    return np.where(index > length // 2, index - length, index)


def plane_radius(length, count):
    freq = signed(length)
    norm = np.sort((freq[:, None] ** 2 + freq[None, :] ** 2).reshape(-1))
    return max(1, math.isqrt(int(norm[count - 1])))


def line_radius(length, columns, count):
    norm = np.sort(np.repeat(np.abs(signed(length)), columns))
    return max(1, int(norm[count - 1]))


def box(length, radius, multiple):
    real = min(length, 2 * radius + 1)
    rows = up(real, multiple)
    return (np.arange(real) - radius) % length, rows


def row_freq(shape, length, radius):
    row = lax.broadcasted_iota(jnp.int32, shape, 0)
    real = min(length, 2 * radius + 1)
    freq = jnp.where(row < radius, row - radius + length, row - radius)
    return jnp.where(row < real, freq, -1)


def interpolation(length, samples):
    if samples == length:
        return np.eye(length)
    shift = np.arange(length)[:, None] - np.arange(samples)[None, :] * (length // samples)
    total = np.cos(math.pi * samples * shift / length)
    for k in range(samples // 2):
        total = total + (2.0 if k else 1.0) * np.cos(2.0 * math.pi * k * shift / length)
    return total / samples


def columns_kernel(cfg, occ_ref, index_ref, coef_ref, table_ref, out_ref):
    rows, cols = cfg["kz_rows"], cfg["cols"]
    count = index_ref.shape[1]
    chunk = math.gcd(count, 1024)
    freq_k = row_freq((rows, chunk), cfg["ng"], cfg["kz_radius"]).astype(F32).astype(BF16)
    freq_s = lax.broadcasted_iota(jnp.int32, (cols, chunk), 0).astype(F32).astype(BF16)
    weight = occ_ref[0].astype(F32) * (1.0 / cfg["bands"])
    scale = jnp.sqrt(jnp.full((1, chunk), weight, F32))
    total = jnp.zeros((4 * rows, cols), F32)
    for at in range(0, count, chunk):
        index = index_ref[:, at : at + chunk].astype(F32)
        kz = jnp.floor((index + 0.5) * (1.0 / cols))
        slot = index - kz * cols
        hit = jnp.broadcast_to(kz, (rows, chunk)).astype(BF16) == freq_k
        pieces = []
        for comp in range(2):
            value = coef_ref[0, comp : comp + 1, at : at + chunk] * scale
            high = value.astype(BF16).astype(F32)
            pieces.append((high, value - high))
        parts = []
        for part in range(2):
            for comp in range(2):
                wide = jnp.broadcast_to(pieces[comp][part], (rows, chunk)).astype(BF16)
                parts.append(jnp.where(hit, wide, jnp.zeros_like(wide)))
        where = jnp.broadcast_to(slot, (cols, chunk)).astype(BF16) == freq_s
        pick = jnp.where(where, jnp.ones((cols, chunk), BF16), jnp.zeros((cols, chunk), BF16))
        total = total + dot_t(jnp.concatenate(parts, axis=0), pick)
    line = total.astype(BF16)
    high = line[: 2 * rows]
    out_ref[...] = dot(table_ref[...], jnp.concatenate([line, high], axis=0))


def tables_kernel(cfg, col_ref, yt_ref, iy_ref, ix_ref, v_ref, high_ref, low_ref, v_out_ref):
    ncol, rows, m = cfg["ncol"], cfg["k_rows"], cfg["m"]
    col = col_ref[...].astype(F32)
    kx = jnp.floor((col + 0.5) * (1.0 / cfg["ng"]))
    ky = col - kx * cfg["ng"]
    freq = row_freq((rows, ncol), cfg["ng"], cfg["k_radius"]).astype(F32)
    hot = jnp.where(jnp.broadcast_to(ky, (rows, ncol)) == freq, 1.0, 0.0)
    hot = hot.T.astype(BF16)
    width = 4 * m
    high_ref[:ncol] = dot(hot, yt_ref[:, :width]).astype(BF16)
    high_ref[ncol:] = dot(hot, yt_ref[:, width : 2 * width]).astype(BF16)
    low_ref[:ncol] = dot(hot, yt_ref[:, 2 * width : 3 * width]).astype(BF16)
    low_ref[ncol:] = dot(hot, yt_ref[:, 3 * width :]).astype(BF16)
    xs = cfg["xs"]
    for z in range(cfg["zs"]):
        along = dot3(v_ref[z * xs : (z + 1) * xs, :], iy_ref[0], iy_ref[1])
        high, low = split(along)
        v_out_ref[z * m : (z + 1) * m, :] = (
            dot(ix_ref[0], high) + dot(ix_ref[1], high) + dot(ix_ref[0], low)
        )


def planes_kernel(
    cfg, col_ref, in_ref, high_ref, low_ref, tx_ref, ix_ref, v_ref, out_ref, energy_ref, a_high, a_low
):
    ncol, rows, m, zs, cols = cfg["ncol"], cfg["k_rows"], cfg["m"], cfg["zs"], cfg["cols"]
    npw, bands, per = cfg["npw"], cfg["bands"], cfg["chunk_bands"]
    col = col_ref[...].astype(F32)
    kx = jnp.floor((col + 0.5) * (1.0 / cfg["ng"]))
    freq = row_freq((rows, cols), cfg["ng"], cfg["k_radius"]).astype(F32)
    hits = [
        jnp.broadcast_to(kx[:, p * cols : (p + 1) * cols], (rows, cols)) == freq for p in range(npw)
    ]
    lane = lax.broadcasted_iota(jnp.int32, energy_ref.shape, 1)

    def step(first, carry):
        dens, energy = carry
        for b in range(per):
            for p in range(npw):
                base = ((first + b) * npw + p) * 2 * zs
                for comp in range(2):
                    for z in range(zs):
                        line = in_ref[pl.ds(base + comp * zs + z, 1), :]
                        line_high = line.astype(BF16).astype(F32)
                        at = (b * zs + z) * rows
                        to = comp * ncol + p * cols
                        for ref, value in ((a_high, line_high), (a_low, line - line_high)):
                            wide = jnp.broadcast_to(value, (rows, cols))
                            ref[at : at + rows, to : to + cols] = jnp.where(hits[p], wide, 0.0).astype(BF16)
        left = a_high[...]
        grid = dot(left, high_ref[...]) + dot(left, low_ref[...]) + dot(a_low[...], high_ref[...])
        grid_high, grid_low = split(grid)
        dens = list(dens)

        def stack(b, z):
            at = (b * zs + z) * rows
            high = [grid_high[at : at + rows, : 2 * m], grid_high[at : at + rows, 2 * m :]]
            low = [grid_low[at : at + rows, : 2 * m], grid_low[at : at + rows, 2 * m :]]
            return jnp.concatenate(high + low + high, axis=0)

        for b in range(per):
            part = jnp.zeros((1, 1), F32)
            acc = jnp.zeros((m, 2 * m), F32)
            for z in range(zs):
                psi = dot(tx_ref[...], stack(b, z))
                square = psi * psi
                dens[z] = dens[z] + square
                acc = acc + square * v_ref[z * m : (z + 1) * m, :]
            part = jnp.sum(jnp.sum(acc, axis=0, keepdims=True), axis=1, keepdims=True)
            energy = energy + jnp.where(lane == first + b, part, 0.0)
        return tuple(dens), energy

    start = (
        tuple(jnp.zeros((m, 2 * m), F32) for _ in range(zs)),
        jnp.zeros(energy_ref.shape, F32),
    )
    if per == bands:
        dens, energy = step(0, start)
    else:
        dens, energy = lax.fori_loop(0, bands // per, lambda i, c: step(i * per, c), start)
    energy_ref[...] = energy
    pk, xr, gz = cfg["pk"], cfg["xr"], cfg["gz"]
    for zp in range(zs // pk):
        folded = []
        for half in range(pk):
            value = dens[zp * pk + half]
            folded.append(value[:, :m] + value[:, m:])
        merged = jnp.concatenate(folded, axis=1) if pk > 1 else folded[0]
        high, low = split(merged)
        rows_x = dot(ix_ref[0], high) + dot(ix_ref[1], high) + dot(ix_ref[0], low)
        for g in range(gz):
            at = (g * (zs // pk) + zp) * xr
            out_ref[at : at + xr, :] = rows_x[g * xr : (g + 1) * xr, :]


def history_kernel(cfg, resid_ref, out_ref):
    hist = resid_ref.shape[0]
    lane = lax.broadcasted_iota(jnp.int32, out_ref.shape, 1)
    row = jnp.zeros(out_ref.shape, F32)
    for i in range(hist):
        left = resid_ref[i]
        for j in range(i, hist):
            value = jnp.sum(left * resid_ref[j], axis=0, keepdims=True)
            value = jnp.sum(value, axis=1, keepdims=True)
            row = row + jnp.where(lane == i * (hist + 1) + j, value, 0.0)
    out_ref[...] = row


def cells_kernel(cfg, in_ref, iy_ref, rho_ref, resid_ref, hist_ref, energy_ref, dens_ref, send_ref, work):
    pk, xr, ng = cfg["pk"], cfg["xr"], cfg["ng"]
    count = in_ref.shape[0] // xr
    high, low = split(in_ref[...])
    cells = dot(high, iy_ref[0]) + dot(high, iy_ref[1]) + dot(low, iy_ref[0])
    for at in range(count):
        for half in range(pk):
            to = (at * pk + half) * xr
            work[to : to + xr, :] = cells[at * xr : (at + 1) * xr, half * ng : (half + 1) * ng]
    for x in range(xr):
        dens_ref[:, x * ng : (x + 1) * ng] = work[pl.ds(x, count * pk, stride=xr), :]
    hist = resid_ref.shape[0]
    lane = lax.broadcasted_iota(jnp.int32, hist_ref.shape, 1)
    last = dens_ref[...] - rho_ref[...]
    row = hist_ref[...]
    for i in range(hist + 1):
        other = resid_ref[i] if i < hist else last
        value = jnp.sum(last * other, axis=0, keepdims=True)
        value = jnp.sum(value, axis=1, keepdims=True)
        row = row + jnp.where(lane == i * (hist + 1) + hist, value, 0.0)
    width = row.shape[1]
    send_ref[:, :width] = jnp.broadcast_to(row, (send_ref.shape[0], width))
    send_ref[:, width:] = jnp.broadcast_to(energy_ref[...], (send_ref.shape[0], energy_ref.shape[1]))


def mix_kernel(
    cfg, band_ref, occ_ref, in_ref, dens_ref, rho_ref, rho_hist_ref, resid_ref, mixed_ref, energy_ref, norm_ref
):
    hist = resid_ref.shape[0]
    size = hist + 1
    row = jnp.sum(in_ref[...], axis=0, keepdims=True) * (1.0 / cfg["ng"] ** 3)
    lane = lax.broadcasted_iota(jnp.int32, row.shape, 1)

    def pick(at):
        return jnp.sum(jnp.where(lane == at, row, 0.0), axis=1, keepdims=True)

    weight = occ_ref[0].astype(F32) * (1.0 / cfg["bands"])
    energy_ref[...] = pick(cfg["row"] + band_ref[0]) / jnp.full((1, 1), weight, F32)
    gram = {(i, j): pick(i * size + j) for i in range(size) for j in range(i, size)}
    norm_ref[...] = jnp.sqrt(gram[(hist, hist)])
    low = {}
    for j in range(size):
        value = gram[(j, j)]
        for k in range(j):
            value = value - low[(j, k)] * low[(j, k)]
        low[(j, j)] = jnp.sqrt(value)
        for i in range(j + 1, size):
            value = gram[(j, i)]
            for k in range(j):
                value = value - low[(i, k)] * low[(j, k)]
            low[(i, j)] = value / low[(j, j)]
    ones = jnp.ones((1, 1), F32)
    half = []
    for i in range(size):
        value = ones
        for k in range(i):
            value = value - low[(i, k)] * half[k]
        half.append(value / low[(i, i)])
    solved = [None] * size
    for i in reversed(range(size)):
        value = half[i]
        for k in range(i + 1, size):
            value = value - low[(k, i)] * solved[k]
        solved[i] = value / low[(i, i)]
    total = solved[0]
    for value in solved[1:]:
        total = total + value
    coef = [value / total for value in solved]
    rho = rho_ref[...]
    mixed = coef[hist] * (rho + 0.8 * (dens_ref[...] - rho))
    for i in range(hist):
        mixed = mixed + coef[i] * (rho_hist_ref[i] + 0.8 * resid_ref[i])
    mixed_ref[...] = mixed


def call(kernel, cfg, outs, spaces, scratch=(), name=None, limit=VMEM_LIMIT):
    vmem, smem = pl.BlockSpec(memory_space=pltpu.VMEM), pl.BlockSpec(memory_space=pltpu.SMEM)
    several = isinstance(outs, (list, tuple))
    return pl.pallas_call(
        lambda *refs: kernel(cfg, *refs),
        out_shape=outs,
        in_specs=[smem if space == "s" else vmem for space in spaces],
        out_specs=[vmem] * len(outs) if several else vmem,
        scratch_shapes=list(scratch),
        compiler_params=pltpu.CompilerParams(vmem_limit_bytes=limit),
        name=name,
    )


def build(mesh):
    nband, npw = mesh.shape["band"], mesh.shape["pw"]
    both = ("band", "pw")

    def local(coefficients, pw_index, col_index, occupation, v_local, rho_in, rho_hist, resid_hist):
        bands_dev, _, count = coefficients.shape
        planes, cells = v_local.shape
        ng = planes * npw
        ncol = col_index.shape[0]
        cols = ncol // npw
        hist = resid_hist.shape[0]
        assert bands_dev == 1 and ng * ng == cells and ng == LANES
        bands = nband
        gz = math.gcd(planes, nband)
        gx = nband // gz
        zs, xs, xr = planes // gz, ng // gx, ng // nband
        kz_radius = line_radius(ng, cols, count)
        k_radius = plane_radius(ng, ncol)
        m = ng
        while m % 2 == 0 and m // 2 > 4 * k_radius and zs % (2 * ng // m) == 0:
            m //= 2
        pk = ng // m
        kz_vals, kz_rows = box(ng, kz_radius, 16)
        k_vals, k_rows = box(ng, k_radius, 16)
        if k_rows % 32:
            k_rows = up(k_rows, 32)
        chunk_bands = bands
        while chunk_bands % 2 == 0 and chunk_bands * zs * k_rows > 1024:
            chunk_bands //= 2
        cfg = dict(
            ng=ng, ncol=ncol, cols=cols, bands=bands, npw=npw, gz=gz, zs=zs, xs=xs, xr=xr, m=m, pk=pk,
            kz_radius=kz_radius, k_radius=k_radius, kz_rows=kz_rows, k_rows=k_rows, chunk_bands=chunk_bands,
            row=up((hist + 1) ** 2, LANES),
        )
        turn = 2.0 * math.pi / ng
        z_of = (
            np.arange(npw)[None, :, None] * planes
            + (np.arange(nband) % gz)[:, None, None] * zs
            + np.arange(zs)[None, None, :]
        )
        angle = turn * (z_of[..., None] * kz_vals % ng)
        cz, sz = np.zeros((2,) + z_of.shape + (kz_rows,))
        cz[..., : len(kz_vals)], sz[..., : len(kz_vals)] = np.cos(angle), np.sin(angle)
        z_table = np.stack([np.concatenate([cz, -sz], -1), np.concatenate([sz, cz], -1)], axis=2)
        z_high, z_low = split_np(z_table.reshape(-1, 2 * kz_rows))
        z_table = jnp.asarray(np.concatenate([z_high, z_high, z_low], axis=1))
        angle = turn * pk * (k_vals[:, None] * np.arange(m)[None, :])
        cy, sy = np.zeros((2, k_rows, m))
        cy[: len(k_vals)], sy[: len(k_vals)] = np.cos(angle), np.sin(angle)
        real = split_np(np.concatenate([cy, sy, -sy, cy], axis=1))
        imag = split_np(np.concatenate([-sy, cy, -cy, -sy], axis=1))
        y_table = jnp.asarray(np.concatenate([real[0], imag[0], real[1], imag[1]], axis=1))
        x_high, x_low = split_np(np.concatenate([cy.T, sy.T], axis=1))
        x_table = jnp.asarray(np.concatenate([x_high, x_high, x_low], axis=1))
        inter = interpolation(ng, m)
        iy_twice = jnp.asarray(np.stack(split_np(np.concatenate([inter, inter], axis=1))))
        wide = np.zeros((pk * m, pk * ng))
        for half in range(pk):
            wide[half * m : (half + 1) * m, half * ng : (half + 1) * ng] = inter.T
        iy_wide = jnp.asarray(np.stack(split_np(wide)))
        ix_full = jnp.asarray(np.stack(split_np(inter)))
        ixt_full = jnp.asarray(np.stack(split_np(inter.T)))

        band = lax.axis_index("band")
        if gx == 1:
            ix, ixt = ix_full, ixt_full
            v_mine = lax.dynamic_slice_in_dim(v_local, band * zs, zs, 0)
        else:
            group = band // gz
            ix = lax.dynamic_slice_in_dim(ix_full, group * xs, xs, 1)
            ixt = lax.dynamic_slice_in_dim(ixt_full, group * xs, xs, 2)
            v_mine = lax.dynamic_slice(v_local, ((band % gz) * zs, group * xs * ng), (zs, xs * ng))
        v_mine = v_mine.reshape(zs * xs, ng)
        index = pw_index.reshape(1, count)
        col = col_index.reshape(1, ncol)
        shape = jax.ShapeDtypeStruct

        sent = call(
            columns_kernel, cfg, shape((nband * npw * 2 * zs, cols), F32), "svvv", name="columns"
        )(occupation, index, coefficients, z_table)
        received = lax.all_to_all(sent, both, 0, 0, tiled=True)
        y_high, y_low, v_grid = call(
            tables_kernel, cfg,
            (shape((2 * ncol, 4 * m), BF16), shape((2 * ncol, 4 * m), BF16), shape((zs * m, 2 * m), F32)),
            "vvvvv", name="tables",
        )(col, y_table, iy_twice, ixt, v_mine)
        hist_row = call(history_kernel, cfg, shape((1, cfg["row"]), F32), "v", name="history")(resid_hist)
        a_shape = (chunk_bands * zs * k_rows, 2 * ncol)
        to_cells, energy_row = call(
            planes_kernel, cfg,
            (shape((gz * (zs // pk) * xr, pk * m), F32), shape((1, up(bands, LANES)), F32)),
            "vvvvvvv", scratch=(pltpu.VMEM(a_shape, BF16), pltpu.VMEM(a_shape, BF16)), name="planes",
        )(col, received, y_high, y_low, x_table, ix, v_grid)
        groups = None if gx == 1 else [list(range(g * gz, (g + 1) * gz)) for g in range(gx)]
        mine = lax.all_to_all(to_cells, "band", 0, 0, axis_index_groups=groups, tiled=True)
        width = cfg["row"] + up(bands, LANES)
        density, row = call(
            cells_kernel, cfg, (shape(rho_in.shape, F32), shape((nband * npw, width), F32)), "vvvvvv",
            scratch=(pltpu.VMEM((mine.shape[0] * pk, ng), F32),), name="cells",
        )(mine, iy_wide, rho_in, resid_hist, hist_row, energy_row)
        rows = lax.all_to_all(row, both, 0, 0, tiled=True)
        mixed, energy, norm = call(
            mix_kernel, cfg, (shape(rho_in.shape, F32), shape((1, 1), F32), shape((1, 1), F32)), "ssvvvvv", name="mix",
        )(band.reshape(1).astype(jnp.int32), occupation, rows, density, rho_in, rho_hist, resid_hist)
        return density, mixed, energy.reshape(1), norm.reshape(())

    return local


def solution(mesh):
    in_specs = (
        P("band", None, "pw"),
        P("pw"),
        P(),
        P("band"),
        P("pw", None),
        P("pw", "band"),
        P(None, "pw", "band"),
        P(None, "pw", "band"),
    )
    out_specs = (P("pw", "band"), P("pw", "band"), P("band"), P())
    return jax.shard_map(build(mesh), mesh=mesh, in_specs=in_specs, out_specs=out_specs, check_vma=False)
```

```python
import math

import jax
import jax.numpy as jnp
import numpy as np
from jax import lax
from jax.experimental import pallas as pl
from jax.experimental.pallas import tpu as pltpu
from jax.sharding import PartitionSpec as P

F32 = jnp.float32
BF16 = jnp.bfloat16
LANES = 128


def up(value, multiple):
    return -(-value // multiple) * multiple


def split_np(table):
    high = table.astype(np.float32).astype(jnp.bfloat16)
    low = (table - high.astype(np.float64)).astype(np.float32).astype(jnp.bfloat16)
    return high, low


def split(value):
    high = value.astype(BF16)
    low = (value - high.astype(F32)).astype(BF16)
    return high, low


def dot(left, right):
    return jnp.dot(left, right, preferred_element_type=F32)


def dot_t(left, right):
    return lax.dot_general(left, right, (((1,), (1,)), ((), ())), preferred_element_type=F32)


def dot3(left, right_high, right_low):
    high, low = split(left)
    return dot(high, right_high) + dot(high, right_low) + dot(low, right_high)


def signed(length):
    index = np.arange(length)
    return np.where(index > length // 2, index - length, index)


def plane_radius(length, count):
    freq = signed(length)
    norm = np.sort((freq[:, None] ** 2 + freq[None, :] ** 2).reshape(-1))
    return max(1, math.isqrt(int(norm[count - 1])))


def line_radius(length, columns, count):
    norm = np.sort(np.repeat(np.abs(signed(length)), columns))
    return max(1, int(norm[count - 1]))


def box(length, radius, multiple):
    real = min(length, 2 * radius + 1)
    rows = up(real, multiple)
    return (np.arange(real) - radius) % length, rows


def row_freq(shape, length, radius):
    row = lax.broadcasted_iota(jnp.int32, shape, 0)
    real = min(length, 2 * radius + 1)
    freq = jnp.where(row < radius, row - radius + length, row - radius)
    return jnp.where(row < real, freq, -1)


def interpolation(length, samples):
    if samples == length:
        return np.eye(length)
    shift = np.arange(length)[:, None] - np.arange(samples)[None, :] * (length // samples)
    total = np.cos(math.pi * samples * shift / length)
    for k in range(samples // 2):
        total = total + (2.0 if k else 1.0) * np.cos(2.0 * math.pi * k * shift / length)
    return total / samples


def fetch(pairs, sems):
    copies = [pltpu.make_async_copy(src, dst, sems.at[i]) for i, (src, dst) in enumerate(pairs)]
    for copy in copies:
        copy.start()
    return copies


def columns_kernel(
    cfg, occ_hbm, index_hbm, coef_hbm, table_hbm, out_hbm, occ_ref, index_ref, coef_ref, table_ref, out_ref, sems, out_sem
):
    copies = fetch(
        ((occ_hbm, occ_ref), (index_hbm, index_ref), (coef_hbm, coef_ref), (table_hbm, table_ref)), sems
    )
    rows, cols = cfg["kz_rows"], cfg["cols"]
    count = index_ref.shape[1]
    chunk = math.gcd(count, 1024)
    freq_k = row_freq((rows, chunk), cfg["ng"], cfg["kz_radius"]).astype(F32).astype(BF16)
    freq_s = lax.broadcasted_iota(jnp.int32, (cols, chunk), 0).astype(F32).astype(BF16)
    copies[0].wait()
    weight = occ_ref[0].astype(F32) * (1.0 / cfg["bands"])
    scale = jnp.sqrt(jnp.full((1, chunk), weight, F32))
    total = jnp.zeros((4 * rows, cols), F32)
    for copy in copies[1:3]:
        copy.wait()
    for at in range(0, count, chunk):
        index = index_ref[:, at : at + chunk].astype(F32)
        kz = jnp.floor((index + 0.5) * (1.0 / cols))
        slot = index - kz * cols
        hit = jnp.broadcast_to(kz, (rows, chunk)).astype(BF16) == freq_k
        pieces = []
        for comp in range(2):
            value = coef_ref[0, comp : comp + 1, at : at + chunk] * scale
            high = value.astype(BF16).astype(F32)
            pieces.append((high, value - high))
        parts = []
        for part in range(2):
            for comp in range(2):
                wide = jnp.broadcast_to(pieces[comp][part], (rows, chunk)).astype(BF16)
                parts.append(jnp.where(hit, wide, jnp.zeros_like(wide)))
        where = jnp.broadcast_to(slot, (cols, chunk)).astype(BF16) == freq_s
        pick = jnp.where(where, jnp.ones((cols, chunk), BF16), jnp.zeros((cols, chunk), BF16))
        total = total + dot_t(jnp.concatenate(parts, axis=0), pick)
    line = total.astype(BF16)
    high = line[: 2 * rows]
    both = jnp.concatenate([line, high], axis=0)
    copies[3].wait()
    out_ref[...] = dot(table_ref[...], both)
    copy = pltpu.make_async_copy(out_ref, out_hbm, out_sem)
    copy.start()
    copy.wait()


def tables_kernel(
    cfg, col_hbm, yt_hbm, iy_hbm, ix_hbm, v_hbm, resid_hbm, high_ref, low_ref, v_out_ref, hist_ref,
    col_ref, yt_ref, iy_ref, ix_ref, v_ref, resid_ref, v_work, sems,
):
    ncol, rows, m, zs, xs, ng = (cfg[k] for k in ("ncol", "k_rows", "m", "zs", "xs", "ng"))
    block = v_ref.shape[0]
    band = lax.axis_index("band")
    first = lax.rem(band, cfg["gz"]) * zs
    base = pl.multiple_of(lax.div(first, block) * block, 8)
    offset = first - base
    lanes = pl.multiple_of(lax.div(band, cfg["gz"]) * (xs * ng), LANES)
    v_mine = v_hbm.at[pl.ds(base, block), pl.ds(lanes, xs * ng)]
    copies = fetch(
        ((col_hbm, col_ref), (yt_hbm, yt_ref), (v_mine, v_ref), (iy_hbm, iy_ref), (ix_hbm, ix_ref), (resid_hbm, resid_ref)),
        sems,
    )
    copies[0].wait()
    col = col_ref[...].astype(F32)
    kx = jnp.floor((col + 0.5) * (1.0 / ng))
    ky = col - kx * ng
    freq = row_freq((rows, ncol), ng, cfg["k_radius"]).astype(F32)
    hot = jnp.where(jnp.broadcast_to(ky, (rows, ncol)) == freq, 1.0, 0.0)
    hot = hot.T.astype(BF16)
    width = 4 * m
    copies[1].wait()
    high_ref[:ncol] = dot(hot, yt_ref[:, :width]).astype(BF16)
    high_ref[ncol:] = dot(hot, yt_ref[:, width : 2 * width]).astype(BF16)
    low_ref[:ncol] = dot(hot, yt_ref[:, 2 * width : 3 * width]).astype(BF16)
    low_ref[ncol:] = dot(hot, yt_ref[:, 3 * width :]).astype(BF16)
    copies[2].wait()
    for x in range(xs):
        v_work[pl.ds(x, block, stride=xs), :] = v_ref[:, x * ng : (x + 1) * ng]
    copies[3].wait()
    copies[4].wait()
    for z in range(zs):
        at = pl.multiple_of((offset + z) * xs, 8)
        along = dot3(v_work[pl.ds(at, xs), :], iy_ref[0], iy_ref[1])
        high, low = split(along)
        v_out_ref[z * m : (z + 1) * m, :] = (
            dot(ix_ref[0], high) + dot(ix_ref[1], high) + dot(ix_ref[0], low)
        )
    copies[5].wait()
    hist = resid_ref.shape[0]
    lane = lax.broadcasted_iota(jnp.int32, hist_ref.shape, 1)
    row = jnp.zeros(hist_ref.shape, F32)
    for i in range(hist):
        left = resid_ref[i]
        for j in range(i, hist):
            value = jnp.sum(left * resid_ref[j], axis=0, keepdims=True)
            value = jnp.sum(value, axis=1, keepdims=True)
            row = row + jnp.where(lane == i * (hist + 1) + j, value, 0.0)
    hist_ref[...] = row


def planes_kernel(
    cfg, in_ref, col_hbm, high_hbm, low_hbm, tx_hbm, ix_hbm, v_hbm, hist_ref, out_ref, row_ref,
    a_high, a_low, col_ref, high_ref, low_ref, tx_ref, ix_ref, v_ref, sems,
):
    copies = fetch(
        ((col_hbm, col_ref), (high_hbm, high_ref), (low_hbm, low_ref), (tx_hbm, tx_ref), (v_hbm, v_ref), (ix_hbm, ix_ref)),
        sems,
    )
    ncol, rows, m, zs, cols = cfg["ncol"], cfg["k_rows"], cfg["m"], cfg["zs"], cfg["cols"]
    npw, bands, per = cfg["npw"], cfg["bands"], cfg["chunk_bands"]
    copies[0].wait()
    col = col_ref[...].astype(F32)
    kx = jnp.floor((col + 0.5) * (1.0 / cfg["ng"]))
    freq = row_freq((rows, cols), cfg["ng"], cfg["k_radius"]).astype(F32)
    hits = [
        jnp.broadcast_to(kx[:, p * cols : (p + 1) * cols], (rows, cols)) == freq for p in range(npw)
    ]
    lane = lax.broadcasted_iota(jnp.int32, row_ref.shape, 1)

    def step(first, carry, ready=lambda: None):
        dens, energy = carry
        for b in range(per):
            for p in range(npw):
                base = ((first + b) * npw + p) * 2 * zs
                for comp in range(2):
                    for z in range(zs):
                        line = in_ref[pl.ds(base + comp * zs + z, 1), :]
                        line_high = line.astype(BF16).astype(F32)
                        at = (b * zs + z) * rows
                        to = comp * ncol + p * cols
                        for ref, value in ((a_high, line_high), (a_low, line - line_high)):
                            wide = jnp.broadcast_to(value, (rows, cols))
                            ref[at : at + rows, to : to + cols] = jnp.where(hits[p], wide, 0.0).astype(BF16)
        ready()
        left = a_high[...]
        grid = dot(left, high_ref[...]) + dot(left, low_ref[...]) + dot(a_low[...], high_ref[...])
        grid_high, grid_low = split(grid)
        dens = list(dens)

        def stack(b, z):
            at = (b * zs + z) * rows
            high = [grid_high[at : at + rows, : 2 * m], grid_high[at : at + rows, 2 * m :]]
            low = [grid_low[at : at + rows, : 2 * m], grid_low[at : at + rows, 2 * m :]]
            return jnp.concatenate(high + low + high, axis=0)

        for b in range(per):
            part = jnp.zeros((1, 1), F32)
            acc = jnp.zeros((m, 2 * m), F32)
            for z in range(zs):
                psi = dot(tx_ref[...], stack(b, z))
                square = psi * psi
                dens[z] = dens[z] + square
                acc = acc + square * v_ref[z * m : (z + 1) * m, :]
            part = jnp.sum(jnp.sum(acc, axis=0, keepdims=True), axis=1, keepdims=True)
            energy = energy + jnp.where(lane == cfg["row"] + first + b, part, 0.0)
        return tuple(dens), energy

    start = (
        tuple(jnp.zeros((m, 2 * m), F32) for _ in range(zs)),
        hist_ref[...],
    )

    def ready():
        for copy in copies[1:]:
            copy.wait()

    if per == bands:
        dens, energy = step(0, start, ready)
    else:
        ready()
        dens, energy = lax.fori_loop(0, bands // per, lambda i, c: step(i * per, c), start)
    row_ref[...] = energy
    pk, xr, gz = cfg["pk"], cfg["xr"], cfg["gz"]
    for zp in range(zs // pk):
        folded = []
        for half in range(pk):
            value = dens[zp * pk + half]
            folded.append(value[:, :m] + value[:, m:])
        merged = jnp.concatenate(folded, axis=1) if pk > 1 else folded[0]
        high, low = split(merged)
        rows_x = dot(ix_ref[0], high) + dot(ix_ref[1], high) + dot(ix_ref[0], low)
        for g in range(gz):
            at = (g * (zs // pk) + zp) * xr
            out_ref[at : at + xr, :] = rows_x[g * xr : (g + 1) * xr, :]


def cells_kernel(
    cfg, in_ref, row_ref, iy_hbm, rho_ref, resid_ref, dens_ref, last_ref, send_ref, work, iy_ref, sems
):
    copies = fetch(((iy_hbm, iy_ref),), sems)
    pk, xr, ng = cfg["pk"], cfg["xr"], cfg["ng"]
    count = in_ref.shape[0] // xr
    high, low = split(in_ref[...])
    copies[0].wait()
    cells = dot(high, iy_ref[0]) + dot(high, iy_ref[1]) + dot(low, iy_ref[0])
    for at in range(count):
        for half in range(pk):
            to = (at * pk + half) * xr
            work[to : to + xr, :] = cells[at * xr : (at + 1) * xr, half * ng : (half + 1) * ng]
    for x in range(xr):
        dens_ref[:, x * ng : (x + 1) * ng] = work[pl.ds(x, count * pk, stride=xr), :]
    hist = resid_ref.shape[0]
    lane = lax.broadcasted_iota(jnp.int32, row_ref.shape, 1)
    rho = rho_ref[...]
    last = dens_ref[...] - rho
    last_ref[...] = rho + 0.8 * last
    row = row_ref[...]
    for i in range(hist + 1):
        other = resid_ref[i] if i < hist else last
        value = jnp.sum(last * other, axis=0, keepdims=True)
        value = jnp.sum(value, axis=1, keepdims=True)
        row = row + jnp.where(lane == i * (hist + 1) + hist, value, 0.0)
    send_ref[...] = jnp.broadcast_to(row, send_ref.shape)


def mix_kernel(
    cfg, in_ref, last_ref, rho_hist_ref, resid_ref, occ_hbm, mixed_ref, energy_ref, norm_ref, occ_ref, sems
):
    copies = fetch(((occ_hbm, occ_ref),), sems)
    hist = resid_ref.shape[0]
    size = hist + 1
    row = jnp.sum(in_ref[...], axis=0, keepdims=True) * (1.0 / cfg["ng"] ** 3)
    lane = lax.broadcasted_iota(jnp.int32, row.shape, 1)

    def pick(at):
        return jnp.sum(jnp.where(lane == at, row, 0.0), axis=1, keepdims=True)

    gram = {(i, j): pick(i * size + j) for i in range(size) for j in range(i, size)}
    norm_ref[...] = jnp.sqrt(gram[(hist, hist)])
    low = {}
    for j in range(size):
        value = gram[(j, j)]
        for k in range(j):
            value = value - low[(j, k)] * low[(j, k)]
        low[(j, j)] = jnp.sqrt(value)
        for i in range(j + 1, size):
            value = gram[(j, i)]
            for k in range(j):
                value = value - low[(i, k)] * low[(j, k)]
            low[(i, j)] = value / low[(j, j)]
    ones = jnp.ones((1, 1), F32)
    half = []
    for i in range(size):
        value = ones
        for k in range(i):
            value = value - low[(i, k)] * half[k]
        half.append(value / low[(i, i)])
    solved = [None] * size
    for i in reversed(range(size)):
        value = half[i]
        for k in range(i + 1, size):
            value = value - low[(k, i)] * solved[k]
        solved[i] = value / low[(i, i)]
    total = solved[0]
    for value in solved[1:]:
        total = total + value
    coef = [value / total for value in solved]
    mixed = coef[hist] * last_ref[...]
    for i in range(hist):
        mixed = mixed + coef[i] * (rho_hist_ref[i] + 0.8 * resid_ref[i])
    mixed_ref[...] = mixed
    copies[0].wait()
    weight = occ_ref[0].astype(F32) * (1.0 / cfg["bands"])
    energy_ref[...] = pick(cfg["row"] + lax.axis_index("band")) / jnp.full((1, 1), weight, F32)


SPACES = {"v": pltpu.VMEM, "s": pltpu.SMEM, "h": pltpu.HBM}


def call(kernel, cfg, outs, spaces, out_spaces, scratch, copies, name, limit):
    sems = [pltpu.SemaphoreType.DMA((copies,))] if copies else []
    return pl.pallas_call(
        lambda *refs: kernel(cfg, *refs),
        out_shape=outs,
        in_specs=[pl.BlockSpec(memory_space=SPACES[space]) for space in spaces],
        out_specs=tuple(pl.BlockSpec(memory_space=SPACES[space]) for space in out_spaces),
        scratch_shapes=list(scratch) + sems,
        compiler_params=pltpu.CompilerParams(vmem_limit_bytes=limit),
        name=name,
    )


def held(*arrays):
    return [pltpu.VMEM(array.shape, array.dtype) for array in arrays]


def slice_x(table, axis, gx, gz, xs):
    if gx == 1:
        return table
    return lax.dynamic_slice_in_dim(table, lax.axis_index("band") // gz * xs, xs, axis)


def build(mesh):
    nband, npw = mesh.shape["band"], mesh.shape["pw"]
    both = ("band", "pw")

    def local(coefficients, pw_index, col_index, occupation, v_local, rho_in, rho_hist, resid_hist):
        bands_dev, _, count = coefficients.shape
        planes, cells = v_local.shape
        ng = planes * npw
        ncol = col_index.shape[0]
        cols = ncol // npw
        hist = resid_hist.shape[0]
        assert bands_dev == 1 and ng * ng == cells and ng == LANES
        bands = nband
        gz = math.gcd(planes, nband)
        gx = nband // gz
        zs, xs, xr = planes // gz, ng // gx, ng // nband
        kz_radius = line_radius(ng, cols, count)
        k_radius = plane_radius(ng, ncol)
        m = ng
        while m % 2 == 0 and m // 2 > 4 * k_radius and zs % (2 * ng // m) == 0:
            m //= 2
        pk = ng // m
        kz_vals, kz_rows = box(ng, kz_radius, 16)
        k_vals, k_rows = box(ng, k_radius, 16)
        if k_rows % 32:
            k_rows = up(k_rows, 32)
        chunk_bands = bands
        while chunk_bands % 2 == 0 and chunk_bands * zs * k_rows > 1024:
            chunk_bands //= 2
        cfg = dict(
            ng=ng, ncol=ncol, cols=cols, bands=bands, npw=npw, gz=gz, zs=zs, xs=xs, xr=xr, m=m, pk=pk,
            kz_radius=kz_radius, k_radius=k_radius, kz_rows=kz_rows, k_rows=k_rows, chunk_bands=chunk_bands,
            row=(hist + 1) ** 2,
        )
        turn = 2.0 * math.pi / ng
        z_of = (
            np.arange(npw)[None, :, None] * planes
            + (np.arange(nband) % gz)[:, None, None] * zs
            + np.arange(zs)[None, None, :]
        )
        angle = turn * (z_of[..., None] * kz_vals % ng)
        cz, sz = np.zeros((2,) + z_of.shape + (kz_rows,))
        cz[..., : len(kz_vals)], sz[..., : len(kz_vals)] = np.cos(angle), np.sin(angle)
        z_table = np.stack([np.concatenate([cz, -sz], -1), np.concatenate([sz, cz], -1)], axis=2)
        z_high, z_low = split_np(z_table.reshape(-1, 2 * kz_rows))
        z_table = jnp.asarray(np.concatenate([z_high, z_high, z_low], axis=1))
        angle = turn * pk * (k_vals[:, None] * np.arange(m)[None, :])
        cy, sy = np.zeros((2, k_rows, m))
        cy[: len(k_vals)], sy[: len(k_vals)] = np.cos(angle), np.sin(angle)
        real = split_np(np.concatenate([cy, sy, -sy, cy], axis=1))
        imag = split_np(np.concatenate([-sy, cy, -cy, -sy], axis=1))
        y_table = jnp.asarray(np.concatenate([real[0], imag[0], real[1], imag[1]], axis=1))
        x_high, x_low = split_np(np.concatenate([cy.T, sy.T], axis=1))
        x_table = jnp.asarray(np.concatenate([x_high, x_high, x_low], axis=1))
        inter = interpolation(ng, m)
        iy_twice = jnp.asarray(np.stack(split_np(np.concatenate([inter, inter], axis=1))))
        wide = np.zeros((pk * m, pk * ng))
        for half in range(pk):
            wide[half * m : (half + 1) * m, half * ng : (half + 1) * ng] = inter.T
        iy_wide = jnp.asarray(np.stack(split_np(wide)))
        ix_full = jnp.asarray(np.stack(split_np(inter)))
        ixt_full = jnp.asarray(np.stack(split_np(inter.T)))

        index = pw_index.reshape(1, count)
        col = col_index.reshape(1, ncol)
        shape = jax.ShapeDtypeStruct
        occ = pltpu.SMEM(occupation.shape, occupation.dtype)
        width = up(cfg["row"] + bands, LANES)
        mib = 1024 * 1024

        sent_shape = shape((nband * npw * 2 * zs, cols), F32)
        (sent,) = call(
            columns_kernel, cfg, (sent_shape,), "hhhh", "h",
            [occ] + held(index, coefficients, z_table, sent_shape) + [pltpu.SemaphoreType.DMA((4,)), pltpu.SemaphoreType.DMA],
            0, "columns", 40 * mib,
        )(occupation, index, coefficients, z_table)
        received = lax.all_to_all(sent, both, 0, 0, tiled=True)
        block = max(zs, 8)
        assert planes % block == 0 and xs % 8 == 0
        v_block = shape((block, xs * ng), F32)
        y_high, y_low, v_grid, hist_row = call(
            tables_kernel, cfg,
            (
                shape((2 * ncol, 4 * m), BF16), shape((2 * ncol, 4 * m), BF16),
                shape((zs * m, 2 * m), F32), shape((1, width), F32),
            ),
            "hhhhhh", "vvvv",
            held(col, y_table, iy_twice, ixt_full[:, :, :xs], v_block, resid_hist, shape((block * xs, ng), F32)),
            6, "tables", 40 * mib,
        )(col, y_table, iy_twice, slice_x(ixt_full, 2, gx, gz, xs), v_local, resid_hist)
        a_shape = (chunk_bands * zs * k_rows, 2 * ncol)
        ix = slice_x(ix_full, 1, gx, gz, xs)
        to_cells, row = call(
            planes_kernel, cfg, (shape((gz * (zs // pk) * xr, pk * m), F32), shape((1, width), F32)),
            "vhhhhhhv", "vv",
            [pltpu.VMEM(a_shape, BF16), pltpu.VMEM(a_shape, BF16)] + held(col, y_high, y_low, x_table, ix, v_grid),
            6, "planes", 40 * mib,
        )(received, col, y_high, y_low, x_table, ix, v_grid, hist_row)
        groups = None if gx == 1 else [list(range(g * gz, (g + 1) * gz)) for g in range(gx)]
        mine = lax.all_to_all(to_cells, "band", 0, 0, axis_index_groups=groups, tiled=True)
        density, last, rows = call(
            cells_kernel, cfg, (shape(rho_in.shape, F32), shape(rho_in.shape, F32), shape((nband * npw, width), F32)),
            "vvhvv", "vvv", [pltpu.VMEM((mine.shape[0] * pk, ng), F32)] + held(iy_wide), 1, "cells", 16 * mib,
        )(mine, row, iy_wide, rho_in, resid_hist)
        rows = lax.all_to_all(rows, both, 0, 0, tiled=True)
        mixed, energy, norm = call(
            mix_kernel, cfg, (shape(rho_in.shape, F32), shape((1, 1), F32), shape((1, 1), F32)),
            "vvvvh", "vvv", [occ], 1, "mix", 16 * mib,
        )(rows, last, rho_hist, resid_hist, occupation)
        return density, mixed, energy.reshape(1), norm.reshape(())

    return local


def solution(mesh):
    in_specs = (
        P("band", None, "pw"),
        P("pw"),
        P(),
        P("band"),
        P("pw", None),
        P("pw", "band"),
        P(None, "pw", "band"),
        P(None, "pw", "band"),
    )
    out_specs = (P("pw", "band"), P("pw", "band"), P("band"), P())
    return jax.shard_map(build(mesh), mesh=mesh, in_specs=in_specs, out_specs=out_specs, check_vma=False)
```

```python
import math

import jax
import jax.numpy as jnp
import numpy as np
from jax import lax
from jax.experimental import pallas as pl
from jax.experimental.pallas import tpu as pltpu
from jax.sharding import PartitionSpec as P

F32 = jnp.float32
BF16 = jnp.bfloat16
LANES = 128


def up(value, multiple):
    return -(-value // multiple) * multiple


def split_np(table):
    high = table.astype(np.float32).astype(jnp.bfloat16)
    low = (table - high.astype(np.float64)).astype(np.float32).astype(jnp.bfloat16)
    return high, low


def split(value):
    high = value.astype(BF16)
    low = (value - high.astype(F32)).astype(BF16)
    return high, low


def dot(left, right):
    return jnp.dot(left, right, preferred_element_type=F32)


def dot_t(left, right):
    return lax.dot_general(left, right, (((1,), (1,)), ((), ())), preferred_element_type=F32)


def dot3(left, right_high, right_low):
    high, low = split(left)
    return dot(high, right_high) + dot(high, right_low) + dot(low, right_high)


def signed(length):
    index = np.arange(length)
    return np.where(index > length // 2, index - length, index)


def plane_radius(length, count):
    freq = signed(length)
    norm = np.sort((freq[:, None] ** 2 + freq[None, :] ** 2).reshape(-1))
    return max(1, math.isqrt(int(norm[count - 1])))


def line_radius(length, columns, count):
    norm = np.sort(np.repeat(np.abs(signed(length)), columns))
    return max(1, int(norm[count - 1]))


def box(length, radius, multiple):
    real = min(length, 2 * radius + 1)
    rows = up(real, multiple)
    return (np.arange(real) - radius) % length, rows


def row_freq(shape, length, radius):
    row = lax.broadcasted_iota(jnp.int32, shape, 0)
    real = min(length, 2 * radius + 1)
    freq = jnp.where(row < radius, row - radius + length, row - radius)
    return jnp.where(row < real, freq, -1)


def interpolation(length, samples):
    if samples == length:
        return np.eye(length)
    shift = np.arange(length)[:, None] - np.arange(samples)[None, :] * (length // samples)
    total = np.cos(math.pi * samples * shift / length)
    for k in range(samples // 2):
        total = total + (2.0 if k else 1.0) * np.cos(2.0 * math.pi * k * shift / length)
    return total / samples


def fetch(pairs, sems):
    copies = [pltpu.make_async_copy(src, dst, sems.at[i]) for i, (src, dst) in enumerate(pairs)]
    for copy in copies:
        copy.start()
    return copies


def columns_kernel(
    cfg, occ_ref, index_hbm, coef_hbm, table_hbm, out_hbm, index_ref, coef_ref, table_ref, out_ref, sems, out_sem
):
    copies = fetch(((index_hbm, index_ref), (coef_hbm, coef_ref), (table_hbm, table_ref)), sems)
    rows, cols = cfg["kz_rows"], cfg["cols"]
    count = index_ref.shape[1]
    chunk = math.gcd(count, 1024)
    freq_k = row_freq((rows, chunk), cfg["ng"], cfg["kz_radius"]).astype(F32).astype(BF16)
    freq_s = lax.broadcasted_iota(jnp.int32, (cols, chunk), 0).astype(F32).astype(BF16)
    weight = occ_ref[0].astype(F32) * (1.0 / cfg["bands"])
    scale = jnp.sqrt(jnp.full((1, chunk), weight, F32))
    total = jnp.zeros((4 * rows, cols), F32)
    for copy in copies[:2]:
        copy.wait()
    for at in range(0, count, chunk):
        index = index_ref[:, at : at + chunk].astype(F32)
        kz = jnp.floor((index + 0.5) * (1.0 / cols))
        slot = index - kz * cols
        hit = jnp.broadcast_to(kz, (rows, chunk)).astype(BF16) == freq_k
        pieces = []
        for comp in range(2):
            value = coef_ref[0, comp : comp + 1, at : at + chunk] * scale
            high = value.astype(BF16).astype(F32)
            pieces.append((high, value - high))
        parts = []
        for part in range(2):
            for comp in range(2):
                wide = jnp.broadcast_to(pieces[comp][part], (rows, chunk)).astype(BF16)
                parts.append(jnp.where(hit, wide, jnp.zeros_like(wide)))
        where = jnp.broadcast_to(slot, (cols, chunk)).astype(BF16) == freq_s
        pick = jnp.where(where, jnp.ones((cols, chunk), BF16), jnp.zeros((cols, chunk), BF16))
        total = total + dot_t(jnp.concatenate(parts, axis=0), pick)
    line = total.astype(BF16)
    high = line[: 2 * rows]
    both = jnp.concatenate([line, high], axis=0)
    copies[2].wait()
    out_ref[...] = dot(table_ref[...], both)
    copy = pltpu.make_async_copy(out_ref, out_hbm, out_sem)
    copy.start()
    copy.wait()


def tables_kernel(
    cfg, col_hbm, yt_hbm, iy_hbm, ix_hbm, v_hbm, resid_hbm, high_ref, low_ref, v_out_hbm, hist_ref,
    col_ref, yt_ref, iy_ref, ix_ref, v_ref, resid_ref, v_work, v_out_ref, out_sem, sems,
):
    ncol, rows, m, zs, xs, ng = (cfg[k] for k in ("ncol", "k_rows", "m", "zs", "xs", "ng"))
    block = v_ref.shape[0]
    band = lax.axis_index("band")
    first = lax.rem(band, cfg["gz"]) * zs
    base = pl.multiple_of(lax.div(first, block) * block, 8)
    offset = first - base
    lanes = pl.multiple_of(lax.div(band, cfg["gz"]) * (xs * ng), LANES)
    v_mine = v_hbm.at[pl.ds(base, block), pl.ds(lanes, xs * ng)]
    copies = fetch(
        ((col_hbm, col_ref), (yt_hbm, yt_ref), (v_mine, v_ref), (iy_hbm, iy_ref), (ix_hbm, ix_ref), (resid_hbm, resid_ref)),
        sems,
    )
    copies[0].wait()
    col = col_ref[...].astype(F32)
    kx = jnp.floor((col + 0.5) * (1.0 / ng))
    ky = col - kx * ng
    freq = row_freq((rows, ncol), ng, cfg["k_radius"]).astype(F32)
    hot = jnp.where(jnp.broadcast_to(ky, (rows, ncol)) == freq, 1.0, 0.0)
    hot = hot.T.astype(BF16)
    width = 4 * m
    copies[1].wait()
    high_ref[:ncol] = dot(hot, yt_ref[:, :width]).astype(BF16)
    high_ref[ncol:] = dot(hot, yt_ref[:, width : 2 * width]).astype(BF16)
    low_ref[:ncol] = dot(hot, yt_ref[:, 2 * width : 3 * width]).astype(BF16)
    low_ref[ncol:] = dot(hot, yt_ref[:, 3 * width :]).astype(BF16)
    copies[2].wait()
    for x in range(xs):
        v_work[pl.ds(x, block, stride=xs), :] = v_ref[:, x * ng : (x + 1) * ng]
    copies[3].wait()
    copies[4].wait()
    for z in range(zs):
        at = pl.multiple_of((offset + z) * xs, 8)
        along = dot3(v_work[pl.ds(at, xs), :], iy_ref[0], iy_ref[1])
        high, low = split(along)
        v_out_ref[z * m : (z + 1) * m, :] = (
            dot(ix_ref[0], high) + dot(ix_ref[1], high) + dot(ix_ref[0], low)
        )
    out_copy = pltpu.make_async_copy(v_out_ref, v_out_hbm, out_sem)
    out_copy.start()
    copies[5].wait()
    hist = resid_ref.shape[0]
    lane = lax.broadcasted_iota(jnp.int32, hist_ref.shape, 1)
    row = jnp.zeros(hist_ref.shape, F32)
    for i in range(hist):
        left = resid_ref[i]
        for j in range(i, hist):
            value = jnp.sum(left * resid_ref[j], axis=0, keepdims=True)
            value = jnp.sum(value, axis=1, keepdims=True)
            row = row + jnp.where(lane == i * (hist + 1) + j, value, 0.0)
    hist_ref[...] = row
    out_copy.wait()


def planes_kernel(
    cfg, in_ref, col_hbm, high_ref, low_ref, tx_hbm, ix_hbm, v_hbm, hist_ref, out_ref, row_ref,
    a_high, a_low, col_ref, tx_ref, ix_ref, v_ref, sems,
):
    copies = fetch(((col_hbm, col_ref), (tx_hbm, tx_ref), (ix_hbm, ix_ref), (v_hbm, v_ref)), sems)
    ncol, rows, m, zs, cols = cfg["ncol"], cfg["k_rows"], cfg["m"], cfg["zs"], cfg["cols"]
    npw, bands, per = cfg["npw"], cfg["bands"], cfg["chunk_bands"]
    copies[0].wait()
    col = col_ref[...].astype(F32)
    kx = jnp.floor((col + 0.5) * (1.0 / cfg["ng"]))
    freq = row_freq((rows, cols), cfg["ng"], cfg["k_radius"]).astype(F32)
    hits = [
        jnp.broadcast_to(kx[:, p * cols : (p + 1) * cols], (rows, cols)) == freq for p in range(npw)
    ]
    lane = lax.broadcasted_iota(jnp.int32, row_ref.shape, 1)

    def step(first, carry, ready=lambda: None):
        dens, energy = carry
        for b in range(per):
            for p in range(npw):
                base = ((first + b) * npw + p) * 2 * zs
                for comp in range(2):
                    for z in range(zs):
                        line = in_ref[pl.ds(base + comp * zs + z, 1), :]
                        line_high = line.astype(BF16).astype(F32)
                        at = (b * zs + z) * rows
                        to = comp * ncol + p * cols
                        for ref, value in ((a_high, line_high), (a_low, line - line_high)):
                            wide = jnp.broadcast_to(value, (rows, cols))
                            ref[at : at + rows, to : to + cols] = jnp.where(hits[p], wide, 0.0).astype(BF16)
        ready()
        left = a_high[...]
        grid = dot(left, high_ref[...]) + dot(left, low_ref[...]) + dot(a_low[...], high_ref[...])
        grid_high, grid_low = split(grid)
        dens = list(dens)

        def stack(b, z):
            at = (b * zs + z) * rows
            high = [grid_high[at : at + rows, : 2 * m], grid_high[at : at + rows, 2 * m :]]
            low = [grid_low[at : at + rows, : 2 * m], grid_low[at : at + rows, 2 * m :]]
            return jnp.concatenate(high + low + high, axis=0)

        for b in range(per):
            part = jnp.zeros((1, 1), F32)
            acc = jnp.zeros((m, 2 * m), F32)
            for z in range(zs):
                psi = dot(tx_ref[...], stack(b, z))
                square = psi * psi
                dens[z] = dens[z] + square
                acc = acc + square * v_ref[z * m : (z + 1) * m, :]
            part = jnp.sum(jnp.sum(acc, axis=0, keepdims=True), axis=1, keepdims=True)
            energy = energy + jnp.where(lane == cfg["row"] + first + b, part, 0.0)
        return tuple(dens), energy

    start = (
        tuple(jnp.zeros((m, 2 * m), F32) for _ in range(zs)),
        hist_ref[...],
    )

    def ready():
        for copy in copies[1:]:
            copy.wait()

    if per == bands:
        dens, energy = step(0, start, ready)
    else:
        ready()
        dens, energy = lax.fori_loop(0, bands // per, lambda i, c: step(i * per, c), start)
    row_ref[...] = energy
    pk, xr, gz = cfg["pk"], cfg["xr"], cfg["gz"]
    for zp in range(zs // pk):
        folded = []
        for half in range(pk):
            value = dens[zp * pk + half]
            folded.append(value[:, :m] + value[:, m:])
        merged = jnp.concatenate(folded, axis=1) if pk > 1 else folded[0]
        high, low = split(merged)
        rows_x = dot(ix_ref[0], high) + dot(ix_ref[1], high) + dot(ix_ref[0], low)
        for g in range(gz):
            at = (g * (zs // pk) + zp) * xr
            out_ref[at : at + xr, :] = rows_x[g * xr : (g + 1) * xr, :]


def cells_kernel(
    cfg, in_ref, row_ref, iy_hbm, rho_ref, resid_ref, dens_ref, last_ref, send_ref, work, iy_ref, sems
):
    copies = fetch(((iy_hbm, iy_ref),), sems)
    pk, xr, ng = cfg["pk"], cfg["xr"], cfg["ng"]
    count = in_ref.shape[0] // xr
    high, low = split(in_ref[...])
    copies[0].wait()
    cells = dot(high, iy_ref[0]) + dot(high, iy_ref[1]) + dot(low, iy_ref[0])
    for at in range(count):
        for half in range(pk):
            to = (at * pk + half) * xr
            work[to : to + xr, :] = cells[at * xr : (at + 1) * xr, half * ng : (half + 1) * ng]
    for x in range(xr):
        dens_ref[:, x * ng : (x + 1) * ng] = work[pl.ds(x, count * pk, stride=xr), :]
    hist = resid_ref.shape[0]
    lane = lax.broadcasted_iota(jnp.int32, row_ref.shape, 1)
    rho = rho_ref[...]
    last = dens_ref[...] - rho
    last_ref[...] = rho + 0.8 * last
    row = row_ref[...]
    for i in range(hist + 1):
        other = resid_ref[i] if i < hist else last
        value = jnp.sum(last * other, axis=0, keepdims=True)
        value = jnp.sum(value, axis=1, keepdims=True)
        row = row + jnp.where(lane == i * (hist + 1) + hist, value, 0.0)
    send_ref[...] = jnp.broadcast_to(row, send_ref.shape)


def mix_kernel(
    cfg, in_ref, last_ref, rho_hist_ref, resid_ref, occ_ref, mixed_ref, energy_ref, norm_ref
):
    hist = resid_ref.shape[0]
    size = hist + 1
    row = jnp.sum(in_ref[...], axis=0, keepdims=True) * (1.0 / cfg["ng"] ** 3)
    lane = lax.broadcasted_iota(jnp.int32, row.shape, 1)

    def pick(at):
        return jnp.sum(jnp.where(lane == at, row, 0.0), axis=1, keepdims=True)

    gram = {(i, j): pick(i * size + j) for i in range(size) for j in range(i, size)}
    norm_ref[...] = jnp.sqrt(gram[(hist, hist)])
    low = {}
    for j in range(size):
        value = gram[(j, j)]
        for k in range(j):
            value = value - low[(j, k)] * low[(j, k)]
        low[(j, j)] = jnp.sqrt(value)
        for i in range(j + 1, size):
            value = gram[(j, i)]
            for k in range(j):
                value = value - low[(i, k)] * low[(j, k)]
            low[(i, j)] = value / low[(j, j)]
    ones = jnp.ones((1, 1), F32)
    half = []
    for i in range(size):
        value = ones
        for k in range(i):
            value = value - low[(i, k)] * half[k]
        half.append(value / low[(i, i)])
    solved = [None] * size
    for i in reversed(range(size)):
        value = half[i]
        for k in range(i + 1, size):
            value = value - low[(k, i)] * solved[k]
        solved[i] = value / low[(i, i)]
    total = solved[0]
    for value in solved[1:]:
        total = total + value
    coef = [value / total for value in solved]
    mixed = coef[hist] * last_ref[...]
    for i in range(hist):
        mixed = mixed + coef[i] * (rho_hist_ref[i] + 0.8 * resid_ref[i])
    mixed_ref[...] = mixed
    weight = occ_ref[0].astype(F32) * (1.0 / cfg["bands"])
    energy_ref[...] = pick(cfg["row"] + lax.axis_index("band")) / jnp.full((1, 1), weight, F32)


SPACES = {"v": pltpu.VMEM, "p": pltpu.VMEM, "s": pltpu.SMEM, "h": pltpu.HBM}


def call(kernel, cfg, outs, spaces, out_spaces, scratch, copies, name, limit):
    sems = [pltpu.SemaphoreType.DMA((copies,))] if copies else []
    run = pl.pallas_call(
        lambda *refs: kernel(cfg, *refs),
        out_shape=tuple(
            SPACES[space](out.shape, out.dtype) if space in "hp" else out
            for out, space in zip(outs, out_spaces, strict=True)
        ),
        in_specs=[pl.BlockSpec(memory_space=SPACES[space]) for space in spaces],
        out_specs=tuple(pl.BlockSpec(memory_space=SPACES[space]) for space in out_spaces),
        scratch_shapes=list(scratch) + sems,
        compiler_params=pltpu.CompilerParams(vmem_limit_bytes=limit),
        name=name,
    )

    def placed(*args):
        return run(*(
            pltpu.with_memory_space_constraint(arg, SPACES[space]) if space in "hp" else arg
            for arg, space in zip(args, spaces, strict=True)
        ))

    return placed


def held(*arrays):
    return [pltpu.VMEM(array.shape, array.dtype) for array in arrays]


def slice_x(table, axis, gx, gz, xs):
    if gx == 1:
        return table
    return lax.dynamic_slice_in_dim(table, lax.axis_index("band") // gz * xs, xs, axis)


def build(mesh):
    nband, npw = mesh.shape["band"], mesh.shape["pw"]
    both = ("band", "pw")

    def local(coefficients, pw_index, col_index, occupation, v_local, rho_in, rho_hist, resid_hist):
        bands_dev, _, count = coefficients.shape
        planes, cells = v_local.shape
        ng = planes * npw
        ncol = col_index.shape[0]
        cols = ncol // npw
        hist = resid_hist.shape[0]
        assert bands_dev == 1 and ng * ng == cells and ng == LANES
        bands = nband
        gz = math.gcd(planes, nband)
        gx = nband // gz
        zs, xs, xr = planes // gz, ng // gx, ng // nband
        kz_radius = line_radius(ng, cols, count)
        k_radius = plane_radius(ng, ncol)
        m = ng
        while m % 2 == 0 and m // 2 > 4 * k_radius and zs % (2 * ng // m) == 0:
            m //= 2
        pk = ng // m
        kz_vals, kz_rows = box(ng, kz_radius, 16)
        k_vals, k_rows = box(ng, k_radius, 16)
        if k_rows % 32:
            k_rows = up(k_rows, 32)
        chunk_bands = bands
        while chunk_bands % 2 == 0 and chunk_bands * zs * k_rows > 1024:
            chunk_bands //= 2
        cfg = dict(
            ng=ng, ncol=ncol, cols=cols, bands=bands, npw=npw, gz=gz, zs=zs, xs=xs, xr=xr, m=m, pk=pk,
            kz_radius=kz_radius, k_radius=k_radius, kz_rows=kz_rows, k_rows=k_rows, chunk_bands=chunk_bands,
            row=(hist + 1) ** 2,
        )
        turn = 2.0 * math.pi / ng
        z_of = (
            np.arange(npw)[None, :, None] * planes
            + (np.arange(nband) % gz)[:, None, None] * zs
            + np.arange(zs)[None, None, :]
        )
        angle = turn * (z_of[..., None] * kz_vals % ng)
        cz, sz = np.zeros((2,) + z_of.shape + (kz_rows,))
        cz[..., : len(kz_vals)], sz[..., : len(kz_vals)] = np.cos(angle), np.sin(angle)
        z_table = np.stack([np.concatenate([cz, -sz], -1), np.concatenate([sz, cz], -1)], axis=2)
        z_high, z_low = split_np(z_table.reshape(-1, 2 * kz_rows))
        z_table = jnp.asarray(np.concatenate([z_high, z_high, z_low], axis=1))
        angle = turn * pk * (k_vals[:, None] * np.arange(m)[None, :])
        cy, sy = np.zeros((2, k_rows, m))
        cy[: len(k_vals)], sy[: len(k_vals)] = np.cos(angle), np.sin(angle)
        real = split_np(np.concatenate([cy, sy, -sy, cy], axis=1))
        imag = split_np(np.concatenate([-sy, cy, -cy, -sy], axis=1))
        y_table = jnp.asarray(np.concatenate([real[0], imag[0], real[1], imag[1]], axis=1))
        x_high, x_low = split_np(np.concatenate([cy.T, sy.T], axis=1))
        x_table = jnp.asarray(np.concatenate([x_high, x_high, x_low], axis=1))
        inter = interpolation(ng, m)
        iy_twice = jnp.asarray(np.stack(split_np(np.concatenate([inter, inter], axis=1))))
        wide = np.zeros((pk * m, pk * ng))
        for half in range(pk):
            wide[half * m : (half + 1) * m, half * ng : (half + 1) * ng] = inter.T
        iy_wide = jnp.asarray(np.stack(split_np(wide)))
        ix_full = jnp.asarray(np.stack(split_np(inter)))
        ixt_full = jnp.asarray(np.stack(split_np(inter.T)))

        index = pw_index.reshape(1, count)
        col = col_index.reshape(1, ncol)
        shape = jax.ShapeDtypeStruct
        width = up(cfg["row"] + bands, LANES)
        mib = 1024 * 1024

        sent_shape = shape((nband * npw * 2 * zs, cols), F32)
        (sent,) = call(
            columns_kernel, cfg, (sent_shape,), "shhh", "h",
            held(index, coefficients, z_table, sent_shape) + [pltpu.SemaphoreType.DMA((3,)), pltpu.SemaphoreType.DMA],
            0, "columns", 40 * mib,
        )(occupation, index, coefficients, z_table)
        received = lax.all_to_all(sent, both, 0, 0, tiled=True)
        block = max(zs, 8)
        assert planes % block == 0 and xs % 8 == 0
        v_block = shape((block, xs * ng), F32)
        y_high, y_low, v_grid, hist_row = call(
            tables_kernel, cfg,
            (
                shape((2 * ncol, 4 * m), BF16), shape((2 * ncol, 4 * m), BF16),
                shape((zs * m, 2 * m), F32), shape((1, width), F32),
            ),
            "hhhhhh", "pphp",
            held(col, y_table, iy_twice, ixt_full[:, :, :xs], v_block, resid_hist, shape((block * xs, ng), F32), shape((zs * m, 2 * m), F32))
            + [pltpu.SemaphoreType.DMA],
            6, "tables", 40 * mib,
        )(col, y_table, iy_twice, slice_x(ixt_full, 2, gx, gz, xs), v_local, resid_hist)
        a_shape = (chunk_bands * zs * k_rows, 2 * ncol)
        ix = slice_x(ix_full, 1, gx, gz, xs)
        to_cells, row = call(
            planes_kernel, cfg, (shape((gz * (zs // pk) * xr, pk * m), F32), shape((1, width), F32)),
            "vhpphhhp", "pp",
            [pltpu.VMEM(a_shape, BF16), pltpu.VMEM(a_shape, BF16)] + held(col, x_table, ix, v_grid), 4, "planes", 40 * mib,
        )(received, col, y_high, y_low, x_table, ix, v_grid, hist_row)
        groups = None if gx == 1 else [list(range(g * gz, (g + 1) * gz)) for g in range(gx)]
        mine = lax.all_to_all(to_cells, "band", 0, 0, axis_index_groups=groups, tiled=True)
        density, last, rows = call(
            cells_kernel, cfg, (shape(rho_in.shape, F32), shape(rho_in.shape, F32), shape((nband * npw, width), F32)),
            "vphvv", "vpp", [pltpu.VMEM((mine.shape[0] * pk, ng), F32)] + held(iy_wide), 1, "cells", 16 * mib,
        )(mine, row, iy_wide, rho_in, resid_hist)
        rows = lax.all_to_all(rows, both, 0, 0, tiled=True)
        mixed, energy, norm = call(
            mix_kernel, cfg, (shape(rho_in.shape, F32), shape((1, 1), F32), shape((1, 1), F32)),
            "vpvvs", "vvv", [], 0, "mix", 16 * mib,
        )(rows, last, rho_hist, resid_hist, occupation)
        return density, mixed, energy.reshape(1), norm.reshape(())

    return local


def solution(mesh):
    in_specs = (
        P("band", None, "pw"),
        P("pw"),
        P(),
        P("band"),
        P("pw", None),
        P("pw", "band"),
        P(None, "pw", "band"),
        P(None, "pw", "band"),
    )
    out_specs = (P("pw", "band"), P("pw", "band"), P("band"), P())
    return jax.shard_map(build(mesh), mesh=mesh, in_specs=in_specs, out_specs=out_specs, check_vma=False)
```

```python
import math

import jax
import jax.numpy as jnp
import numpy as np
from jax import lax
from jax.experimental import pallas as pl
from jax.experimental.pallas import tpu as pltpu
from jax.sharding import PartitionSpec as P

F32 = jnp.float32
BF16 = jnp.bfloat16
LANES = 128


def up(value, multiple):
    return -(-value // multiple) * multiple


def split_np(table):
    high = table.astype(np.float32).astype(jnp.bfloat16)
    low = (table - high.astype(np.float64)).astype(np.float32).astype(jnp.bfloat16)
    return high, low


def split(value):
    high = value.astype(BF16)
    low = (value - high.astype(F32)).astype(BF16)
    return high, low


def dot(left, right):
    return jnp.dot(left, right, preferred_element_type=F32)


def dot_t(left, right):
    return lax.dot_general(left, right, (((1,), (1,)), ((), ())), preferred_element_type=F32)


def dot3(left, right_high, right_low):
    high, low = split(left)
    return dot(high, right_high) + dot(high, right_low) + dot(low, right_high)


def signed(length):
    index = np.arange(length)
    return np.where(index > length // 2, index - length, index)


def plane_radius(length, count):
    freq = signed(length)
    norm = np.sort((freq[:, None] ** 2 + freq[None, :] ** 2).reshape(-1))
    return max(1, math.isqrt(int(norm[count - 1])))


def line_radius(length, columns, count):
    norm = np.sort(np.repeat(np.abs(signed(length)), columns))
    return max(1, int(norm[count - 1]))


def box(length, radius, multiple):
    real = min(length, 2 * radius + 1)
    rows = up(real, multiple)
    return (np.arange(real) - radius) % length, rows


def row_freq(shape, length, radius):
    row = lax.broadcasted_iota(jnp.int32, shape, 0)
    real = min(length, 2 * radius + 1)
    freq = jnp.where(row < radius, row - radius + length, row - radius)
    return jnp.where(row < real, freq, -1)


def interpolation(length, samples):
    if samples == length:
        return np.eye(length)
    shift = np.arange(length)[:, None] - np.arange(samples)[None, :] * (length // samples)
    total = np.cos(math.pi * samples * shift / length)
    for k in range(samples // 2):
        total = total + (2.0 if k else 1.0) * np.cos(2.0 * math.pi * k * shift / length)
    return total / samples


def fetch(pairs, sems):
    copies = [pltpu.make_async_copy(src, dst, sems.at[i]) for i, (src, dst) in enumerate(pairs)]
    for copy in copies:
        copy.start()
    return copies


def columns_kernel(
    cfg, occ_ref, index_hbm, coef_hbm, table_hbm, out_hbm, index_ref, coef_ref, table_ref, out_ref, sems, out_sem
):
    copies = fetch(((index_hbm, index_ref), (coef_hbm, coef_ref), (table_hbm, table_ref)), sems)
    rows, cols = cfg["kz_rows"], cfg["cols"]
    count = index_ref.shape[1]
    chunk = math.gcd(count, 1024)
    freq_k = row_freq((rows, chunk), cfg["ng"], cfg["kz_radius"]).astype(F32).astype(BF16)
    freq_s = lax.broadcasted_iota(jnp.int32, (cols, chunk), 0).astype(F32).astype(BF16)
    weight = occ_ref[0].astype(F32) * (1.0 / cfg["bands"])
    scale = jnp.sqrt(jnp.full((1, chunk), weight, F32))
    total = jnp.zeros((4 * rows, cols), F32)
    for copy in copies[:2]:
        copy.wait()
    for at in range(0, count, chunk):
        index = index_ref[:, at : at + chunk].astype(F32)
        kz = jnp.floor((index + 0.5) * (1.0 / cols))
        slot = index - kz * cols
        hit = jnp.broadcast_to(kz, (rows, chunk)).astype(BF16) == freq_k
        pieces = []
        for comp in range(2):
            value = coef_ref[0, comp : comp + 1, at : at + chunk] * scale
            high = value.astype(BF16).astype(F32)
            pieces.append((high, value - high))
        parts = []
        for part in range(2):
            for comp in range(2):
                wide = jnp.broadcast_to(pieces[comp][part], (rows, chunk)).astype(BF16)
                parts.append(jnp.where(hit, wide, jnp.zeros_like(wide)))
        where = jnp.broadcast_to(slot, (cols, chunk)).astype(BF16) == freq_s
        pick = jnp.where(where, jnp.ones((cols, chunk), BF16), jnp.zeros((cols, chunk), BF16))
        total = total + dot_t(jnp.concatenate(parts, axis=0), pick)
    line = total.astype(BF16)
    high = line[: 2 * rows]
    both = jnp.concatenate([line, high], axis=0)
    copies[2].wait()
    out_ref[...] = dot(table_ref[...], both)
    copy = pltpu.make_async_copy(out_ref, out_hbm, out_sem)
    copy.start()
    copy.wait()


def tables_kernel(
    cfg, col_hbm, yt_hbm, iy_hbm, ix_hbm, v_hbm, resid_hbm, tx_hbm, x_hbm, wide_hbm,
    e_ref, hot_ref, v_out_hbm, hist_ref, tx_ref, x_ref, wide_ref,
    col_ref, yt_ref, iy_ref, ix_ref, v_ref, resid_ref, v_work, v_out_ref, out_sem, sems,
):
    ncol, rows, m, zs, xs, ng = (cfg[k] for k in ("ncol", "k_rows", "m", "zs", "xs", "ng"))
    block = v_ref.shape[0]
    band = lax.axis_index("band")
    first = lax.rem(band, cfg["gz"]) * zs
    base = pl.multiple_of(lax.div(first, block) * block, 8)
    offset = first - base
    lanes = pl.multiple_of(lax.div(band, cfg["gz"]) * (xs * ng), LANES)
    v_mine = v_hbm.at[pl.ds(base, block), pl.ds(lanes, xs * ng)]
    copies = fetch(
        (
            (col_hbm, col_ref), (yt_hbm, yt_ref), (v_mine, v_ref), (iy_hbm, iy_ref), (ix_hbm, ix_ref), (resid_hbm, resid_ref),
            (tx_hbm, tx_ref), (x_hbm, x_ref), (wide_hbm, wide_ref),
        ),
        sems,
    )
    copies[0].wait()
    col = col_ref[...].astype(F32)
    kx = jnp.floor((col + 0.5) * (1.0 / ng))
    ky = col - kx * ng
    freq = row_freq((rows, ncol), ng, cfg["k_radius"]).astype(F32)
    hot_ref[...] = jnp.where(jnp.broadcast_to(kx, (rows, ncol)) == freq, 1.0, 0.0).astype(BF16)
    hot = jnp.where(jnp.broadcast_to(ky, (rows, ncol)) == freq, 1.0, 0.0)
    hot = hot.T.astype(BF16)
    width = 4 * m
    copies[1].wait()
    e_ref[:ncol] = dot(hot, yt_ref[:, :width]).astype(BF16)
    e_ref[ncol:] = dot(hot, yt_ref[:, width:]).astype(BF16)
    copies[2].wait()
    for x in range(xs):
        v_work[pl.ds(x, block, stride=xs), :] = v_ref[:, x * ng : (x + 1) * ng]
    copies[3].wait()
    copies[4].wait()
    for z in range(zs):
        at = pl.multiple_of((offset + z) * xs, 8)
        along = dot3(v_work[pl.ds(at, xs), :], iy_ref[0], iy_ref[1])
        high, low = split(along)
        v_out_ref[z * m : (z + 1) * m, :] = (
            dot(ix_ref[0], high) + dot(ix_ref[1], high) + dot(ix_ref[0], low)
        )
    out_copy = pltpu.make_async_copy(v_out_ref, v_out_hbm, out_sem)
    out_copy.start()
    copies[5].wait()
    hist = resid_ref.shape[0]
    lane = lax.broadcasted_iota(jnp.int32, hist_ref.shape, 1)
    row = jnp.zeros(hist_ref.shape, F32)
    for i in range(hist):
        left = resid_ref[i]
        for j in range(i, hist):
            value = jnp.sum(left * resid_ref[j], axis=0, keepdims=True)
            value = jnp.sum(value, axis=1, keepdims=True)
            row = row + jnp.where(lane == i * (hist + 1) + j, value, 0.0)
    hist_ref[...] = row
    for copy in copies[6:]:
        copy.wait()
    out_copy.wait()


def turned(value, m):
    if 2 * m > LANES:
        return jnp.concatenate([-value[:, m:], value[:, :m]], axis=1)
    lane = lax.broadcasted_iota(jnp.int32, value.shape, 1)
    moved = pltpu.roll(value, m, 1)
    return jnp.where(lane < m, -moved, moved)


def planes_kernel(
    cfg, in_ref, hot_ref, e_ref, tx_ref, ix_ref, v_hbm, hist_ref, out_ref, row_ref, piece_ref, v_ref, sems
):
    copies = fetch(((v_hbm, v_ref),), sems)
    ncol, rows, m, zs, cols = cfg["ncol"], cfg["k_rows"], cfg["m"], cfg["zs"], cfg["cols"]
    npw, bands, per = cfg["npw"], cfg["bands"], cfg["chunk_bands"]
    value = in_ref[...]
    high = value.astype(BF16).astype(F32)
    count = value.shape[0]
    piece_ref[0, :count] = high
    piece_ref[1, :count] = value - high
    hits = [hot_ref[:, p * cols : (p + 1) * cols] > 0 for p in range(npw)]
    none = jnp.zeros((rows, cols), BF16)
    lane = lax.broadcasted_iota(jnp.int32, row_ref.shape, 1)

    def left(part, first):
        lanes = []
        for comp in range(2):
            for p in range(npw):
                column = []
                for b in range(per):
                    for z in range(zs):
                        at = ((first + b) * npw + p) * 2 * zs + comp * zs + z
                        line = piece_ref[part, pl.ds(at, 8, stride=0), :]
                        line = jnp.concatenate([line, line], axis=0).astype(BF16)
                        column.append(jnp.where(hits[p], jnp.concatenate([line] * (rows // 16), axis=0), none))
                lanes.append(jnp.concatenate(column, axis=0))
        return jnp.concatenate(lanes, axis=1)

    def step(first, carry):
        dens, energy = carry
        dens = list(dens)
        grid = dot(left(0, first), e_ref[...])
        grid = grid[:, : 2 * m] + grid[:, 2 * m :] + dot(left(1, first), e_ref[:, : 2 * m])
        grids = [part for value in (grid, turned(grid, m)) for part in split(value)]

        def stack(b, z):
            at = (b * zs + z) * rows
            parts = [grids[k][at : at + rows] for k in (0, 2, 1, 3, 0, 2)]
            return jnp.concatenate(parts, axis=0)

        group = 2 if zs % 2 == 0 else 1
        for b in range(per):
            acc = jnp.zeros((m, 2 * m), F32)
            for z in range(0, zs, group):
                both = jnp.concatenate([stack(b, z + k) for k in range(group)], axis=1)
                psi = dot(tx_ref[...], both)
                for k in range(group):
                    square = psi[:, k * 2 * m : (k + 1) * 2 * m]
                    square = square * square
                    dens[z + k] = dens[z + k] + square
                    acc = acc + square * v_ref[(z + k) * m : (z + k + 1) * m, :]
            part = jnp.sum(jnp.sum(acc, axis=0, keepdims=True), axis=1, keepdims=True)
            energy = energy + jnp.where(lane == cfg["row"] + first + b, part, 0.0)
        return tuple(dens), energy

    carry = (
        tuple(jnp.zeros((m, 2 * m), F32) for _ in range(zs)),
        hist_ref[...],
    )
    copies[0].wait()
    if bands // per <= 2:
        for first in range(0, bands, per):
            carry = step(first, carry)
    else:
        carry = lax.fori_loop(0, bands // per, lambda i, c: step(i * per, c), carry)
    dens, energy = carry
    row_ref[...] = energy
    pk, xr, gz = cfg["pk"], cfg["xr"], cfg["gz"]
    for zp in range(zs // pk):
        folded = []
        for half in range(pk):
            value = dens[zp * pk + half]
            folded.append(value[:, :m] + value[:, m:])
        merged = jnp.concatenate(folded, axis=1) if pk > 1 else folded[0]
        high, low = split(merged)
        rows_x = dot(ix_ref[0], high) + dot(ix_ref[1], high) + dot(ix_ref[0], low)
        for g in range(gz):
            at = (g * (zs // pk) + zp) * xr
            out_ref[at : at + xr, :] = rows_x[g * xr : (g + 1) * xr, :]


def cells_kernel(cfg, in_ref, row_ref, iy_ref, rho_ref, resid_ref, dens_ref, send_ref, work):
    pk, xr, ng = cfg["pk"], cfg["xr"], cfg["ng"]
    count = in_ref.shape[0] // xr
    high, low = split(in_ref[...])
    cells = dot(high, iy_ref[0]) + dot(high, iy_ref[1]) + dot(low, iy_ref[0])
    for at in range(count):
        for half in range(pk):
            to = (at * pk + half) * xr
            work[to : to + xr, :] = cells[at * xr : (at + 1) * xr, half * ng : (half + 1) * ng]
    hist = resid_ref.shape[0]
    sums = [None] * (hist + 1)
    for x in range(xr):
        at = slice(x * ng, (x + 1) * ng)
        value = work[pl.ds(x, count * pk, stride=xr), :]
        dens_ref[:, at] = value
        last = value - rho_ref[:, at]
        for i in range(hist + 1):
            term = last * (resid_ref[i, :, at] if i < hist else last)
            sums[i] = term if x == 0 else sums[i] + term
    lane = lax.broadcasted_iota(jnp.int32, row_ref.shape, 1)
    row = row_ref[...]
    for i in range(hist + 1):
        value = jnp.sum(jnp.sum(sums[i], axis=0, keepdims=True), axis=1, keepdims=True)
        row = row + jnp.where(lane == i * (hist + 1) + hist, value, 0.0)
    send_ref[...] = jnp.broadcast_to(row, send_ref.shape)


def mix_kernel(
    cfg, in_ref, dens_ref, rho_ref, rho_hist_ref, resid_ref, occ_ref,
    dens_hbm, mixed_hbm, energy_ref, norm_ref, mixed_ref, sems,
):
    dens_copy = pltpu.make_async_copy(dens_ref, dens_hbm, sems.at[0])
    dens_copy.start()
    hist = resid_ref.shape[0]
    size = hist + 1
    row = jnp.sum(in_ref[...], axis=0, keepdims=True) * (1.0 / cfg["ng"] ** 3)
    lane = lax.broadcasted_iota(jnp.int32, row.shape, 1)

    def pick(at):
        return jnp.sum(jnp.where(lane == at, row, 0.0), axis=1, keepdims=True)

    gram = {(i, j): pick(i * size + j) for i in range(size) for j in range(i, size)}
    low = {}
    for j in range(size):
        value = gram[(j, j)]
        for k in range(j):
            value = value - low[(j, k)] * low[(j, k)]
        low[(j, j)] = jnp.sqrt(value)
        for i in range(j + 1, size):
            value = gram[(j, i)]
            for k in range(j):
                value = value - low[(i, k)] * low[(j, k)]
            low[(i, j)] = value / low[(j, j)]
    half = []
    for i in range(size):
        value = jnp.ones((1, 1), F32)
        for k in range(i):
            value = value - low[(i, k)] * half[k]
        half.append(value / low[(i, i)])
    solved = [None] * size
    for i in reversed(range(size)):
        value = half[i]
        for k in range(i + 1, size):
            value = value - low[(k, i)] * solved[k]
        solved[i] = value / low[(i, i)]
    total = solved[0]
    for value in solved[1:]:
        total = total + value
    coef = [value / total for value in solved]
    planes, width = mixed_ref.shape
    copies = [dens_copy]
    step = 8
    for at in range(0, planes, step):
        rows = slice(at, at + step)
        for first in range(0, width, 4 * LANES):
            lanes = slice(first, min(first + 4 * LANES, width))
            rho = rho_ref[rows, lanes]
            mixed = coef[hist] * (rho + 0.8 * (dens_ref[rows, lanes] - rho))
            for i in range(hist):
                mixed = mixed + coef[i] * (rho_hist_ref[i, rows, lanes] + 0.8 * resid_ref[i, rows, lanes])
            mixed_ref[rows, lanes] = mixed
        copy = pltpu.make_async_copy(mixed_ref.at[rows, :], mixed_hbm.at[rows, :], sems.at[1 + at // step])
        copy.start()
        copies.append(copy)
    norm_ref[...] = jnp.sqrt(gram[(hist, hist)])
    weight = occ_ref[0].astype(F32) * (1.0 / cfg["bands"])
    energy_ref[...] = pick(cfg["row"] + lax.axis_index("band")) / jnp.full((1, 1), weight, F32)
    for copy in copies:
        copy.wait()


SPACES = {"v": pltpu.VMEM, "p": pltpu.VMEM, "s": pltpu.SMEM, "h": pltpu.HBM}


def call(kernel, cfg, outs, spaces, out_spaces, scratch, copies, name, limit):
    sems = [pltpu.SemaphoreType.DMA((copies,))] if copies else []
    run = pl.pallas_call(
        lambda *refs: kernel(cfg, *refs),
        out_shape=tuple(
            SPACES[space](out.shape, out.dtype) if space in "hp" else out
            for out, space in zip(outs, out_spaces, strict=True)
        ),
        in_specs=[pl.BlockSpec(memory_space=SPACES[space]) for space in spaces],
        out_specs=tuple(pl.BlockSpec(memory_space=SPACES[space]) for space in out_spaces),
        scratch_shapes=list(scratch) + sems,
        compiler_params=pltpu.CompilerParams(vmem_limit_bytes=limit),
        name=name,
    )

    def placed(*args):
        return run(*(
            pltpu.with_memory_space_constraint(arg, SPACES[space]) if space in "hp" else arg
            for arg, space in zip(args, spaces, strict=True)
        ))

    return placed


def held(*arrays):
    return [pltpu.VMEM(array.shape, array.dtype) for array in arrays]


def slice_x(table, axis, gx, gz, xs):
    if gx == 1:
        return table
    return lax.dynamic_slice_in_dim(table, lax.axis_index("band") // gz * xs, xs, axis)


def build(mesh):
    nband, npw = mesh.shape["band"], mesh.shape["pw"]
    both = ("band", "pw")

    def local(coefficients, pw_index, col_index, occupation, v_local, rho_in, rho_hist, resid_hist):
        bands_dev, _, count = coefficients.shape
        planes, cells = v_local.shape
        ng = planes * npw
        ncol = col_index.shape[0]
        cols = ncol // npw
        hist = resid_hist.shape[0]
        assert bands_dev == 1 and ng * ng == cells and ng == LANES
        bands = nband
        gz = math.gcd(planes, nband)
        gx = nband // gz
        zs, xs, xr = planes // gz, ng // gx, ng // nband
        kz_radius = line_radius(ng, cols, count)
        k_radius = plane_radius(ng, ncol)
        m = ng
        while m % 2 == 0 and m // 2 > 4 * k_radius and zs % (2 * ng // m) == 0:
            m //= 2
        pk = ng // m
        kz_vals, kz_rows = box(ng, kz_radius, 16)
        k_vals, k_rows = box(ng, k_radius, 16)
        if k_rows % 32:
            k_rows = up(k_rows, 32)
        chunk_bands = bands
        while chunk_bands % 2 == 0 and chunk_bands * zs * k_rows > 512:
            chunk_bands //= 2
        cfg = dict(
            ng=ng, ncol=ncol, cols=cols, bands=bands, npw=npw, gz=gz, zs=zs, xs=xs, xr=xr, m=m, pk=pk,
            kz_radius=kz_radius, k_radius=k_radius, kz_rows=kz_rows, k_rows=k_rows, chunk_bands=chunk_bands,
            row=(hist + 1) ** 2,
        )
        turn = 2.0 * math.pi / ng
        z_of = (
            np.arange(npw)[None, :, None] * planes
            + (np.arange(nband) % gz)[:, None, None] * zs
            + np.arange(zs)[None, None, :]
        )
        angle = turn * (z_of[..., None] * kz_vals % ng)
        cz, sz = np.zeros((2,) + z_of.shape + (kz_rows,))
        cz[..., : len(kz_vals)], sz[..., : len(kz_vals)] = np.cos(angle), np.sin(angle)
        z_table = np.stack([np.concatenate([cz, -sz], -1), np.concatenate([sz, cz], -1)], axis=2)
        z_high, z_low = split_np(z_table.reshape(-1, 2 * kz_rows))
        z_table = jnp.asarray(np.concatenate([z_high, z_high, z_low], axis=1))
        angle = turn * pk * (k_vals[:, None] * np.arange(m)[None, :])
        cy, sy = np.zeros((2, k_rows, m))
        cy[: len(k_vals)], sy[: len(k_vals)] = np.cos(angle), np.sin(angle)
        real = split_np(np.concatenate([cy, sy], axis=1))
        imag = split_np(np.concatenate([-sy, cy], axis=1))
        y_table = jnp.asarray(np.concatenate([*real, *imag], axis=1))
        x_high, x_low = split_np(np.concatenate([cy.T, sy.T], axis=1))
        x_table = jnp.asarray(np.concatenate([x_high, x_high, x_low], axis=1))
        inter = interpolation(ng, m)
        iy_twice = jnp.asarray(np.stack(split_np(np.concatenate([inter, inter], axis=1))))
        wide = np.zeros((pk * m, pk * ng))
        for half in range(pk):
            wide[half * m : (half + 1) * m, half * ng : (half + 1) * ng] = inter.T
        iy_wide = jnp.asarray(np.stack(split_np(wide)))
        ix_full = jnp.asarray(np.stack(split_np(inter)))
        ixt_full = jnp.asarray(np.stack(split_np(inter.T)))

        index = pw_index.reshape(1, count)
        col = col_index.reshape(1, ncol)
        shape = jax.ShapeDtypeStruct
        width = up(cfg["row"] + bands, LANES)
        mib = 1024 * 1024

        sent_shape = shape((nband * npw * 2 * zs, cols), F32)
        (sent,) = call(
            columns_kernel, cfg, (sent_shape,), "shhh", "h",
            held(index, coefficients, z_table, sent_shape) + [pltpu.SemaphoreType.DMA((3,)), pltpu.SemaphoreType.DMA],
            0, "columns", 40 * mib,
        )(occupation, index, coefficients, z_table)
        received = lax.all_to_all(sent, both, 0, 0, tiled=True)
        block = max(zs, 8)
        assert planes % block == 0 and xs % 8 == 0
        v_block = shape((block, xs * ng), F32)
        ix = slice_x(ix_full, 1, gx, gz, xs)
        e_table, hot, v_grid, hist_row, tx, ix, iy = call(
            tables_kernel, cfg,
            (
                shape((2 * ncol, 4 * m), BF16), shape((k_rows, ncol), BF16), shape((zs * m, 2 * m), F32), shape((1, width), F32),
                x_table, ix, iy_wide,
            ),
            "h" * 9, "pphpppp",
            held(
                col, y_table, iy_twice, ixt_full[:, :, :xs], v_block, resid_hist,
                shape((block * xs, ng), F32), shape((zs * m, 2 * m), F32),
            ) + [pltpu.SemaphoreType.DMA],
            9, "tables", 40 * mib,
        )(col, y_table, iy_twice, slice_x(ixt_full, 2, gx, gz, xs), v_local, resid_hist, x_table, ix, iy_wide)
        to_cells, row = call(
            planes_kernel, cfg, (shape((gz * (zs // pk) * xr, pk * m), F32), shape((1, width), F32)),
            "vpppphp", "pp",
            held(shape((2, received.shape[0] + 8, cols), F32), v_grid), 1, "planes", 40 * mib,
        )(received, hot, e_table, tx, ix, v_grid, hist_row)
        groups = None if gx == 1 else [list(range(g * gz, (g + 1) * gz)) for g in range(gx)]
        mine = lax.all_to_all(to_cells, "band", 0, 0, axis_index_groups=groups, tiled=True)
        dens, rows = call(
            cells_kernel, cfg, (shape(rho_in.shape, F32), shape((nband * npw, width), F32)),
            "vppvv", "pp", [pltpu.VMEM((mine.shape[0] * pk, ng), F32)], 0, "cells", 16 * mib,
        )(mine, row, iy, rho_in, resid_hist)
        rows = lax.all_to_all(rows, both, 0, 0, tiled=True)
        density, mixed, energy, norm = call(
            mix_kernel, cfg,
            (shape(rho_in.shape, F32), shape(rho_in.shape, F32), shape((1, 1), F32), shape((1, 1), F32)),
            "vpvvvs", "hhvv", held(rho_in), 1 + planes // 8, "mix", 16 * mib,
        )(rows, dens, rho_in, rho_hist, resid_hist, occupation)
        return density, mixed, energy.reshape(1), norm.reshape(())

    return local


def solution(mesh):
    in_specs = (
        P("band", None, "pw"),
        P("pw"),
        P(),
        P("band"),
        P("pw", None),
        P("pw", "band"),
        P(None, "pw", "band"),
        P(None, "pw", "band"),
    )
    out_specs = (P("pw", "band"), P("pw", "band"), P("band"), P())
    return jax.shard_map(build(mesh), mesh=mesh, in_specs=in_specs, out_specs=out_specs, check_vma=False)
```

```python
import math

import jax
import jax.numpy as jnp
import numpy as np
from jax import lax
from jax.experimental import pallas as pl
from jax.experimental.pallas import tpu as pltpu
from jax.sharding import PartitionSpec as P

F32 = jnp.float32
BF16 = jnp.bfloat16
LANES = 128


def up(value, multiple):
    return -(-value // multiple) * multiple


def split_np(table):
    high = table.astype(np.float32).astype(jnp.bfloat16)
    low = (table - high.astype(np.float64)).astype(np.float32).astype(jnp.bfloat16)
    return high, low


def split(value):
    high = value.astype(BF16)
    low = (value - high.astype(F32)).astype(BF16)
    return high, low


def dot(left, right):
    return jnp.dot(left, right, preferred_element_type=F32)


def dot_t(left, right):
    return lax.dot_general(left, right, (((1,), (1,)), ((), ())), preferred_element_type=F32)


def dot3(left, right_high, right_low):
    high, low = split(left)
    return dot(high, right_high) + dot(high, right_low) + dot(low, right_high)


def signed(length):
    index = np.arange(length)
    return np.where(index > length // 2, index - length, index)


def plane_radius(length, count):
    freq = signed(length)
    norm = np.sort((freq[:, None] ** 2 + freq[None, :] ** 2).reshape(-1))
    return max(1, math.isqrt(int(norm[count - 1])))


def line_radius(length, columns, count):
    norm = np.sort(np.repeat(np.abs(signed(length)), columns))
    return max(1, int(norm[count - 1]))


def box(length, radius, multiple):
    real = min(length, 2 * radius + 1)
    rows = up(real, multiple)
    return (np.arange(real) - radius) % length, rows


def row_freq(shape, length, radius):
    row = lax.broadcasted_iota(jnp.int32, shape, 0)
    real = min(length, 2 * radius + 1)
    freq = jnp.where(row < radius, row - radius + length, row - radius)
    return jnp.where(row < real, freq, -1)


def interpolation(length, samples):
    if samples == length:
        return np.eye(length)
    shift = np.arange(length)[:, None] - np.arange(samples)[None, :] * (length // samples)
    total = np.cos(math.pi * samples * shift / length)
    for k in range(samples // 2):
        total = total + (2.0 if k else 1.0) * np.cos(2.0 * math.pi * k * shift / length)
    return total / samples


def kz_split(real):
    rows = real // 16 * 16
    return rows, real - rows, up(4 * (real - rows), 16)


def fetch(pairs, sems):
    copies = [pltpu.make_async_copy(src, dst, sems.at[i]) for i, (src, dst) in enumerate(pairs)]
    for copy in copies:
        copy.start()
    return copies


def columns_kernel(
    cfg, occ_ref, index_hbm, coef_hbm, table_hbm, out_hbm, index_ref, coef_ref, table_ref, out_ref, sems, out_sem
):
    copies = fetch(((index_hbm, index_ref), (coef_hbm, coef_ref), (table_hbm, table_ref)), sems)
    real, cols, ng, radius = cfg["kz_real"], cfg["cols"], cfg["ng"], cfg["kz_radius"]
    rows, rest, extra = kz_split(real)
    count = index_ref.shape[1]
    chunk = math.gcd(count, 1024)
    row = lax.broadcasted_iota(jnp.int32, (rows, chunk), 0)
    freq_k = jnp.where(row < radius, row - radius + ng, row - radius).astype(F32).astype(BF16)
    if extra:
        row = lax.broadcasted_iota(jnp.int32, (extra, chunk), 0)
        freq_e = jnp.where(row < 4 * rest, lax.rem(row, rest) + (rows - radius), -1).astype(F32).astype(BF16)
    freq_s = lax.broadcasted_iota(jnp.int32, (cols, chunk), 0).astype(F32).astype(BF16)
    weight = occ_ref[0].astype(F32) * (1.0 / cfg["bands"])
    scale = jnp.sqrt(jnp.full((1, chunk), weight, F32))
    total = jnp.zeros((4 * rows + extra, cols), F32)
    for copy in copies[:2]:
        copy.wait()
    for at in range(0, count, chunk):
        index = index_ref[:, at : at + chunk].astype(F32)
        kz = jnp.floor((index + 0.5) * (1.0 / cols))
        slot = index - kz * cols
        pieces = [None] * 4
        for comp in range(2):
            value = coef_ref[0, comp : comp + 1, at : at + chunk] * scale
            high = value.astype(BF16).astype(F32)
            pieces[comp], pieces[2 + comp] = high, value - high
        hit = jnp.broadcast_to(kz, (rows, chunk)).astype(BF16) == freq_k
        parts = []
        for piece in pieces:
            wide = jnp.broadcast_to(piece, (rows, chunk)).astype(BF16)
            parts.append(jnp.where(hit, wide, jnp.zeros_like(wide)))
        if extra:
            wide = jnp.broadcast_to(pieces[3], (extra, chunk))
            for k in (2, 1, 0):
                wide = jnp.where(row < (k + 1) * rest, jnp.broadcast_to(pieces[k], (extra, chunk)), wide)
            wide = wide.astype(BF16)
            hit = jnp.broadcast_to(kz, (extra, chunk)).astype(BF16) == freq_e
            parts.append(jnp.where(hit, wide, jnp.zeros_like(wide)))
        where = jnp.broadcast_to(slot, (cols, chunk)).astype(BF16) == freq_s
        pick = jnp.where(where, jnp.ones((cols, chunk), BF16), jnp.zeros((cols, chunk), BF16))
        total = total + dot_t(jnp.concatenate(parts, axis=0), pick)
    line = total.astype(BF16)
    both = jnp.concatenate([line, line[: 2 * rows]] + ([line[4 * rows :]] if extra else []), axis=0)
    copies[2].wait()
    out_ref[...] = dot(table_ref[...], both)
    copy = pltpu.make_async_copy(out_ref, out_hbm, out_sem)
    copy.start()
    copy.wait()


def tables_kernel(
    cfg, col_hbm, yt_hbm, iy_hbm, ix_hbm, v_hbm, resid_hbm, tx_hbm, x_hbm, wide_hbm,
    e_ref, hot_ref, v_out_hbm, hist_ref, tx_ref, x_ref, wide_ref,
    col_ref, yt_ref, iy_ref, ix_ref, v_ref, resid_ref, v_work, v_out_ref, out_sem, sems,
):
    ncol, rows, m, zs, xs, ng = (cfg[k] for k in ("ncol", "k_rows", "m", "zs", "xs", "ng"))
    block = v_ref.shape[0]
    band = lax.axis_index("band")
    first = lax.rem(band, cfg["gz"]) * zs
    base = pl.multiple_of(lax.div(first, block) * block, 8)
    offset = first - base
    lanes = pl.multiple_of(lax.div(band, cfg["gz"]) * (xs * ng), LANES)
    v_mine = v_hbm.at[pl.ds(base, block), pl.ds(lanes, xs * ng)]
    copies = fetch(
        (
            (col_hbm, col_ref), (yt_hbm, yt_ref), (v_mine, v_ref), (iy_hbm, iy_ref), (ix_hbm, ix_ref), (resid_hbm, resid_ref),
            (tx_hbm, tx_ref), (x_hbm, x_ref), (wide_hbm, wide_ref),
        ),
        sems,
    )
    copies[0].wait()
    col = col_ref[...].astype(F32)
    kx = jnp.floor((col + 0.5) * (1.0 / ng))
    ky = col - kx * ng
    freq = row_freq((rows, ncol), ng, cfg["k_radius"]).astype(F32)
    hot_ref[...] = jnp.where(jnp.broadcast_to(kx, (rows, ncol)) == freq, 1.0, 0.0).astype(BF16)
    hot = jnp.where(jnp.broadcast_to(ky, (rows, ncol)) == freq, 1.0, 0.0)
    hot = hot.T.astype(BF16)
    width = 4 * m
    copies[1].wait()
    e_ref[:ncol] = dot(hot, yt_ref[:, :width]).astype(BF16)
    e_ref[ncol:] = dot(hot, yt_ref[:, width:]).astype(BF16)
    copies[2].wait()
    for x in range(xs):
        v_work[pl.ds(x, block, stride=xs), :] = v_ref[:, x * ng : (x + 1) * ng]
    copies[3].wait()
    copies[4].wait()
    for z in range(zs):
        at = pl.multiple_of((offset + z) * xs, 8)
        along = dot3(v_work[pl.ds(at, xs), :], iy_ref[0], iy_ref[1])
        high, low = split(along)
        v_out_ref[z * m : (z + 1) * m, :] = (
            dot(ix_ref[0], high) + dot(ix_ref[1], high) + dot(ix_ref[0], low)
        )
    out_copy = pltpu.make_async_copy(v_out_ref, v_out_hbm, out_sem)
    out_copy.start()
    copies[5].wait()
    hist = resid_ref.shape[0]
    lane = lax.broadcasted_iota(jnp.int32, hist_ref.shape, 1)
    row = jnp.zeros(hist_ref.shape, F32)
    for i in range(hist):
        left = resid_ref[i]
        for j in range(i, hist):
            value = jnp.sum(left * resid_ref[j], axis=0, keepdims=True)
            value = jnp.sum(value, axis=1, keepdims=True)
            row = row + jnp.where(lane == i * (hist + 1) + j, value, 0.0)
    hist_ref[...] = row
    for copy in copies[6:]:
        copy.wait()
    out_copy.wait()


def turned(value, m):
    if 2 * m > LANES:
        return jnp.concatenate([-value[:, m:], value[:, :m]], axis=1)
    lane = lax.broadcasted_iota(jnp.int32, value.shape, 1)
    moved = pltpu.roll(value, m, 1)
    return jnp.where(lane < m, -moved, moved)


def planes_kernel(
    cfg, in_ref, hot_ref, e_ref, tx_ref, ix_ref, v_hbm, hist_ref, out_ref, row_ref, piece_ref, v_ref, sems
):
    copies = fetch(((v_hbm, v_ref),), sems)
    ncol, rows, m, zs, cols = cfg["ncol"], cfg["k_rows"], cfg["m"], cfg["zs"], cfg["cols"]
    npw, bands, per = cfg["npw"], cfg["bands"], cfg["chunk_bands"]
    value = in_ref[...]
    high = value.astype(BF16).astype(F32)
    count = value.shape[0]
    piece_ref[0, :count] = high
    piece_ref[1, :count] = value - high
    hits = [hot_ref[:, p * cols : (p + 1) * cols] > 0 for p in range(npw)]
    none = jnp.zeros((rows, cols), BF16)
    lane = lax.broadcasted_iota(jnp.int32, row_ref.shape, 1)

    def left(part, first):
        lanes = []
        for comp in range(2):
            for p in range(npw):
                column = []
                for b in range(per):
                    for z in range(zs):
                        at = ((first + b) * npw + p) * 2 * zs + comp * zs + z
                        line = piece_ref[part, pl.ds(at, 8, stride=0), :]
                        line = jnp.concatenate([line, line], axis=0).astype(BF16)
                        column.append(jnp.where(hits[p], jnp.concatenate([line] * (rows // 16), axis=0), none))
                lanes.append(jnp.concatenate(column, axis=0))
        return jnp.concatenate(lanes, axis=1)

    def step(first, carry):
        dens, energy = carry
        dens = list(dens)
        grid = dot(left(0, first), e_ref[...])
        grid = grid[:, : 2 * m] + grid[:, 2 * m :] + dot(left(1, first), e_ref[:, : 2 * m])
        grids = [part for value in (grid, turned(grid, m)) for part in split(value)]

        def stack(b, z):
            at = (b * zs + z) * rows
            parts = [grids[k][at : at + rows] for k in (0, 2, 1, 3, 0, 2)]
            return jnp.concatenate(parts, axis=0)

        group = 2 if zs % 2 == 0 else 1
        for b in range(per):
            acc = jnp.zeros((m, 2 * m), F32)
            for z in range(0, zs, group):
                both = jnp.concatenate([stack(b, z + k) for k in range(group)], axis=1)
                psi = dot(tx_ref[...], both)
                for k in range(group):
                    square = psi[:, k * 2 * m : (k + 1) * 2 * m]
                    square = square * square
                    dens[z + k] = dens[z + k] + square
                    acc = acc + square * v_ref[(z + k) * m : (z + k + 1) * m, :]
            part = jnp.sum(jnp.sum(acc, axis=0, keepdims=True), axis=1, keepdims=True)
            energy = energy + jnp.where(lane == cfg["row"] + first + b, part, 0.0)
        return tuple(dens), energy

    carry = (
        tuple(jnp.zeros((m, 2 * m), F32) for _ in range(zs)),
        hist_ref[...],
    )
    copies[0].wait()
    if bands // per <= 2:
        for first in range(0, bands, per):
            carry = step(first, carry)
    else:
        carry = lax.fori_loop(0, bands // per, lambda i, c: step(i * per, c), carry)
    dens, energy = carry
    row_ref[...] = energy
    pk, xr, gz = cfg["pk"], cfg["xr"], cfg["gz"]
    for zp in range(zs // pk):
        folded = []
        for half in range(pk):
            value = dens[zp * pk + half]
            folded.append(value[:, :m] + value[:, m:])
        merged = jnp.concatenate(folded, axis=1) if pk > 1 else folded[0]
        high, low = split(merged)
        rows_x = dot(ix_ref[0], high) + dot(ix_ref[1], high) + dot(ix_ref[0], low)
        for g in range(gz):
            at = (g * (zs // pk) + zp) * xr
            out_ref[at : at + xr, :] = rows_x[g * xr : (g + 1) * xr, :]


def cells_kernel(cfg, in_ref, row_ref, iy_ref, rho_ref, resid_ref, dens_ref, send_ref, work):
    pk, xr, ng = cfg["pk"], cfg["xr"], cfg["ng"]
    count = in_ref.shape[0] // xr
    high, low = split(in_ref[...])
    cells = dot(high, iy_ref[0]) + dot(high, iy_ref[1]) + dot(low, iy_ref[0])
    for at in range(count):
        for half in range(pk):
            to = (at * pk + half) * xr
            work[to : to + xr, :] = cells[at * xr : (at + 1) * xr, half * ng : (half + 1) * ng]
    hist = resid_ref.shape[0]
    sums = [None] * (hist + 1)
    for x in range(xr):
        at = slice(x * ng, (x + 1) * ng)
        value = work[pl.ds(x, count * pk, stride=xr), :]
        dens_ref[:, at] = value
        last = value - rho_ref[:, at]
        for i in range(hist + 1):
            term = last * (resid_ref[i, :, at] if i < hist else last)
            sums[i] = term if x == 0 else sums[i] + term
    lane = lax.broadcasted_iota(jnp.int32, row_ref.shape, 1)
    row = row_ref[...]
    for i in range(hist + 1):
        value = jnp.sum(jnp.sum(sums[i], axis=0, keepdims=True), axis=1, keepdims=True)
        row = row + jnp.where(lane == i * (hist + 1) + hist, value, 0.0)
    send_ref[...] = jnp.broadcast_to(row, send_ref.shape)


def mix_kernel(
    cfg, in_ref, dens_ref, rho_ref, rho_hist_ref, resid_ref, occ_ref,
    mixed_hbm, energy_hbm, norm_hbm, mixed_ref, energy_ref, norm_ref, sems,
):
    hist = resid_ref.shape[0]
    size = hist + 1
    row = jnp.sum(in_ref[...], axis=0, keepdims=True) * (1.0 / cfg["ng"] ** 3)
    lane = lax.broadcasted_iota(jnp.int32, row.shape, 1)

    def pick(at):
        return jnp.sum(jnp.where(lane == at, row, 0.0), axis=1, keepdims=True)

    gram = {(i, j): pick(i * size + j) for i in range(size) for j in range(i, size)}
    low = {}
    for j in range(size):
        value = gram[(j, j)]
        for k in range(j):
            value = value - low[(j, k)] * low[(j, k)]
        low[(j, j)] = jnp.sqrt(value)
        for i in range(j + 1, size):
            value = gram[(j, i)]
            for k in range(j):
                value = value - low[(i, k)] * low[(j, k)]
            low[(i, j)] = value / low[(j, j)]
    half = []
    for i in range(size):
        value = jnp.ones((1, 1), F32)
        for k in range(i):
            value = value - low[(i, k)] * half[k]
        half.append(value / low[(i, i)])
    solved = [None] * size
    for i in reversed(range(size)):
        value = half[i]
        for k in range(i + 1, size):
            value = value - low[(k, i)] * solved[k]
        solved[i] = value / low[(i, i)]
    total = solved[0]
    for value in solved[1:]:
        total = total + value
    coef = [value / total for value in solved]
    norm_ref[...] = jnp.sqrt(gram[(hist, hist)])
    weight = occ_ref[0].astype(F32) * (1.0 / cfg["bands"])
    energy_ref[...] = pick(cfg["row"] + lax.axis_index("band")) / jnp.full((1, 1), weight, F32)
    planes, width = mixed_ref.shape
    copies = fetch(((energy_ref, energy_hbm), (norm_ref, norm_hbm)), sems)
    step = 8
    for at in range(0, planes, step):
        rows = slice(at, at + step)
        for first in range(0, width, 4 * LANES):
            lanes = slice(first, min(first + 4 * LANES, width))
            rho = rho_ref[rows, lanes]
            mixed = coef[hist] * (rho + 0.8 * (dens_ref[rows, lanes] - rho))
            for i in range(hist):
                mixed = mixed + coef[i] * (rho_hist_ref[i, rows, lanes] + 0.8 * resid_ref[i, rows, lanes])
            mixed_ref[rows, lanes] = mixed
        copy = pltpu.make_async_copy(mixed_ref.at[rows, :], mixed_hbm.at[rows, :], sems.at[2 + at // step])
        copy.start()
        copies.append(copy)
    for copy in copies:
        copy.wait()


SPACES = {"u": pltpu.HBM, "v": pltpu.VMEM, "p": pltpu.VMEM, "s": pltpu.SMEM, "h": pltpu.HBM}


def call(kernel, cfg, outs, spaces, out_spaces, scratch, copies, name, limit):
    sems = [pltpu.SemaphoreType.DMA((copies,))] if copies else []
    run = pl.pallas_call(
        lambda *refs: kernel(cfg, *refs),
        out_shape=tuple(
            SPACES[space](out.shape, out.dtype) if space in "hp" else out
            for out, space in zip(outs, out_spaces, strict=True)
        ),
        in_specs=[pl.BlockSpec(memory_space=SPACES[space]) for space in spaces],
        out_specs=tuple(pl.BlockSpec(memory_space=SPACES[space]) for space in out_spaces),
        scratch_shapes=list(scratch) + sems,
        compiler_params=pltpu.CompilerParams(vmem_limit_bytes=limit),
        name=name,
    )

    def placed(*args):
        return run(*(
            pltpu.with_memory_space_constraint(arg, SPACES[space]) if space in "hp" else arg
            for arg, space in zip(args, spaces, strict=True)
        ))

    return placed


def held(*arrays):
    return [pltpu.VMEM(array.shape, array.dtype) for array in arrays]


def slice_x(table, axis, gx, gz, xs):
    if gx == 1:
        return table
    return lax.dynamic_slice_in_dim(table, lax.axis_index("band") // gz * xs, xs, axis)


def build(mesh):
    nband, npw = mesh.shape["band"], mesh.shape["pw"]
    both = ("band", "pw")

    def local(coefficients, pw_index, col_index, occupation, v_local, rho_in, rho_hist, resid_hist):
        bands_dev, _, count = coefficients.shape
        planes, cells = v_local.shape
        ng = planes * npw
        ncol = col_index.shape[0]
        cols = ncol // npw
        hist = resid_hist.shape[0]
        assert bands_dev == 1 and ng * ng == cells and ng == LANES
        bands = nband
        gz = math.gcd(planes, nband)
        gx = nband // gz
        zs, xs, xr = planes // gz, ng // gx, ng // nband
        kz_radius = line_radius(ng, cols, count)
        k_radius = plane_radius(ng, ncol)
        m = ng
        while m % 2 == 0 and m // 2 > 4 * k_radius and zs % (2 * ng // m) == 0:
            m //= 2
        pk = ng // m
        kz_vals, _ = box(ng, kz_radius, 16)
        kz_rows, kz_rest, kz_extra = kz_split(len(kz_vals))
        k_vals, k_rows = box(ng, k_radius, 16)
        if k_rows % 32:
            k_rows = up(k_rows, 32)
        chunk_bands = bands
        while chunk_bands % 2 == 0 and chunk_bands * zs * k_rows > 512:
            chunk_bands //= 2
        cfg = dict(
            ng=ng, ncol=ncol, cols=cols, bands=bands, npw=npw, gz=gz, zs=zs, xs=xs, xr=xr, m=m, pk=pk,
            kz_radius=kz_radius, k_radius=k_radius, kz_real=len(kz_vals), k_rows=k_rows, chunk_bands=chunk_bands,
            row=(hist + 1) ** 2,
        )
        turn = 2.0 * math.pi / ng
        z_of = (
            np.arange(npw)[None, :, None] * planes
            + (np.arange(nband) % gz)[:, None, None] * zs
            + np.arange(zs)[None, None, :]
        )
        angle = turn * (z_of[..., None] * kz_vals % ng)
        cz, sz = np.cos(angle), np.sin(angle)
        z_table = np.stack([np.stack([cz, -sz], -2), np.stack([sz, cz], -2)], axis=2)
        z_high, z_low = split_np(z_table.reshape(-1, 2, len(kz_vals)))
        flat = lambda table: table.reshape(table.shape[0], -1)
        main = [flat(table[:, :, :kz_rows]) for table in (z_high, z_low)]
        spare = [flat(table[:, :, kz_rows:]) for table in (z_high, z_low)]
        pad = [np.zeros((z_high.shape[0], kz_extra - 2 * k * kz_rest), z_high.dtype) for k in (2, 1)]
        z_table = jnp.asarray(np.concatenate(
            [main[0], main[0], spare[0], spare[0], pad[0], main[1], spare[1], pad[1]], axis=1
        ))
        angle = turn * pk * (k_vals[:, None] * np.arange(m)[None, :])
        cy, sy = np.zeros((2, k_rows, m))
        cy[: len(k_vals)], sy[: len(k_vals)] = np.cos(angle), np.sin(angle)
        real = split_np(np.concatenate([cy, sy], axis=1))
        imag = split_np(np.concatenate([-sy, cy], axis=1))
        y_table = jnp.asarray(np.concatenate([*real, *imag], axis=1))
        x_high, x_low = split_np(np.concatenate([cy.T, sy.T], axis=1))
        x_table = jnp.asarray(np.concatenate([x_high, x_high, x_low], axis=1))
        inter = interpolation(ng, m)
        iy_twice = jnp.asarray(np.stack(split_np(np.concatenate([inter, inter], axis=1))))
        wide = np.zeros((pk * m, pk * ng))
        for half in range(pk):
            wide[half * m : (half + 1) * m, half * ng : (half + 1) * ng] = inter.T
        iy_wide = jnp.asarray(np.stack(split_np(wide)))
        ix_full = jnp.asarray(np.stack(split_np(inter)))
        ixt_full = jnp.asarray(np.stack(split_np(inter.T)))

        index = pw_index.reshape(1, count)
        col = col_index.reshape(1, ncol)
        shape = jax.ShapeDtypeStruct
        width = up(cfg["row"] + bands, LANES)
        mib = 1024 * 1024

        sent_shape = shape((nband * npw * 2 * zs, cols), F32)
        (sent,) = call(
            columns_kernel, cfg, (sent_shape,), "shhh", "h",
            held(index, coefficients, z_table, sent_shape) + [pltpu.SemaphoreType.DMA((3,)), pltpu.SemaphoreType.DMA],
            0, "columns", 40 * mib,
        )(occupation, index, coefficients, z_table)
        received = lax.all_to_all(sent, both, 0, 0, tiled=True)
        block = max(zs, 8)
        assert planes % block == 0 and xs % 8 == 0
        v_block = shape((block, xs * ng), F32)
        ix = slice_x(ix_full, 1, gx, gz, xs)
        e_table, hot, v_grid, hist_row, tx, ix, iy = call(
            tables_kernel, cfg,
            (
                shape((2 * ncol, 4 * m), BF16), shape((k_rows, ncol), BF16), shape((zs * m, 2 * m), F32), shape((1, width), F32),
                x_table, ix, iy_wide,
            ),
            "h" * 9, "pphpppp",
            held(
                col, y_table, iy_twice, ixt_full[:, :, :xs], v_block, resid_hist,
                shape((block * xs, ng), F32), shape((zs * m, 2 * m), F32),
            ) + [pltpu.SemaphoreType.DMA],
            9, "tables", 40 * mib,
        )(col, y_table, iy_twice, slice_x(ixt_full, 2, gx, gz, xs), v_local, resid_hist, x_table, ix, iy_wide)
        to_cells, row = call(
            planes_kernel, cfg, (shape((gz * (zs // pk) * xr, pk * m), F32), shape((1, width), F32)),
            "vpppphp", "pp",
            held(shape((2, received.shape[0] + 8, cols), F32), v_grid), 1, "planes", 40 * mib,
        )(received, hot, e_table, tx, ix, v_grid, hist_row)
        groups = None if gx == 1 else [list(range(g * gz, (g + 1) * gz)) for g in range(gx)]
        mine = lax.all_to_all(to_cells, "band", 0, 0, axis_index_groups=groups, tiled=True)
        dens, rows = call(
            cells_kernel, cfg, (shape(rho_in.shape, F32), shape((nband * npw, width), F32)),
            "vppvv", "pp", [pltpu.VMEM((mine.shape[0] * pk, ng), F32)], 0, "cells", 16 * mib,
        )(mine, row, iy, rho_in, resid_hist)
        rows = lax.all_to_all(rows, both, 0, 0, tiled=True)
        one = shape((1, 1), F32)
        mixed, energy, norm = call(
            mix_kernel, cfg, (shape(rho_in.shape, F32), one, one),
            "vpvvvs", "huu", held(rho_in, one, one), 2 + planes // 8, "mix", 16 * mib,
        )(rows, dens, rho_in, rho_hist, resid_hist, occupation)
        return dens, mixed, energy.reshape(1), norm.reshape(())

    return local


def solution(mesh):
    in_specs = (
        P("band", None, "pw"),
        P("pw"),
        P(),
        P("band"),
        P("pw", None),
        P("pw", "band"),
        P(None, "pw", "band"),
        P(None, "pw", "band"),
    )
    out_specs = (P("pw", "band"), P("pw", "band"), P("band"), P())
    return jax.shard_map(build(mesh), mesh=mesh, in_specs=in_specs, out_specs=out_specs, check_vma=False)
```

```python
import math

import jax
import jax.numpy as jnp
import numpy as np
from jax import lax
from jax.experimental import pallas as pl
from jax.experimental.pallas import tpu as pltpu
from jax.sharding import PartitionSpec as P

F32 = jnp.float32
BF16 = jnp.bfloat16
LANES = 128


def up(value, multiple):
    return -(-value // multiple) * multiple


def split_np(table):
    high = table.astype(np.float32).astype(jnp.bfloat16)
    low = (table - high.astype(np.float64)).astype(np.float32).astype(jnp.bfloat16)
    return high, low


def split(value):
    high = value.astype(BF16)
    low = (value - high.astype(F32)).astype(BF16)
    return high, low


def dot(left, right):
    return jnp.dot(left, right, preferred_element_type=F32)


def dot_t(left, right):
    return lax.dot_general(left, right, (((1,), (1,)), ((), ())), preferred_element_type=F32)


def dot3(left, right_high, right_low):
    high, low = split(left)
    return dot(high, right_high) + dot(high, right_low) + dot(low, right_high)


def signed(length):
    index = np.arange(length)
    return np.where(index > length // 2, index - length, index)


def plane_radius(length, count):
    freq = signed(length)
    norm = np.sort((freq[:, None] ** 2 + freq[None, :] ** 2).reshape(-1))
    return max(1, math.isqrt(int(norm[count - 1])))


def line_radius(length, columns, count):
    norm = np.sort(np.repeat(np.abs(signed(length)), columns))
    return max(1, int(norm[count - 1]))


def box(length, radius, multiple):
    real = min(length, 2 * radius + 1)
    rows = up(real, multiple)
    return (np.arange(real) - radius) % length, rows


def row_freq(shape, length, radius):
    row = lax.broadcasted_iota(jnp.int32, shape, 0)
    real = min(length, 2 * radius + 1)
    freq = jnp.where(row < radius, row - radius + length, row - radius)
    return jnp.where(row < real, freq, -1)


def interpolation(length, samples):
    if samples == length:
        return np.eye(length)
    shift = np.arange(length)[:, None] - np.arange(samples)[None, :] * (length // samples)
    total = np.cos(math.pi * samples * shift / length)
    for k in range(samples // 2):
        total = total + (2.0 if k else 1.0) * np.cos(2.0 * math.pi * k * shift / length)
    return total / samples


def kz_split(real):
    rows = real // 16 * 16
    return rows, real - rows, up(4 * (real - rows), 16)


def fetch(pairs, sems):
    copies = [pltpu.make_async_copy(src, dst, sems.at[i]) for i, (src, dst) in enumerate(pairs)]
    for copy in copies:
        copy.start()
    return copies


def columns_kernel(
    cfg, occ_ref, index_hbm, coef_hbm, table_hbm, out_hbm, index_ref, coef_ref, table_ref, out_ref, sems, out_sem
):
    copies = fetch(((index_hbm, index_ref), (coef_hbm, coef_ref), (table_hbm, table_ref)), sems)
    real, cols, ng, radius = cfg["kz_real"], cfg["cols"], cfg["ng"], cfg["kz_radius"]
    rows, rest, extra = kz_split(real)
    count = index_ref.shape[1]
    chunk = math.gcd(count, 1024)
    row = lax.broadcasted_iota(jnp.int32, (rows, chunk), 0)
    freq_k = jnp.where(row < radius, row - radius + ng, row - radius).astype(F32).astype(BF16)
    if extra:
        row = lax.broadcasted_iota(jnp.int32, (extra, chunk), 0)
        freq_e = jnp.where(row < 4 * rest, lax.rem(row, rest) + (rows - radius), -1).astype(F32).astype(BF16)
    freq_s = lax.broadcasted_iota(jnp.int32, (cols, chunk), 0).astype(F32).astype(BF16)
    weight = occ_ref[0].astype(F32) * (1.0 / cfg["bands"])
    scale = jnp.sqrt(jnp.full((1, chunk), weight, F32))
    total = jnp.zeros((4 * rows + extra, cols), F32)
    for copy in copies[:2]:
        copy.wait()
    for at in range(0, count, chunk):
        index = index_ref[:, at : at + chunk].astype(F32)
        kz = jnp.floor((index + 0.5) * (1.0 / cols))
        slot = index - kz * cols
        pieces = [None] * 4
        for comp in range(2):
            value = coef_ref[0, comp : comp + 1, at : at + chunk] * scale
            high = value.astype(BF16).astype(F32)
            pieces[comp], pieces[2 + comp] = high, value - high
        hit = jnp.broadcast_to(kz, (rows, chunk)).astype(BF16) == freq_k
        parts = []
        for piece in pieces:
            wide = jnp.broadcast_to(piece, (rows, chunk)).astype(BF16)
            parts.append(jnp.where(hit, wide, jnp.zeros_like(wide)))
        if extra:
            wide = jnp.broadcast_to(pieces[3], (extra, chunk))
            for k in (2, 1, 0):
                wide = jnp.where(row < (k + 1) * rest, jnp.broadcast_to(pieces[k], (extra, chunk)), wide)
            wide = wide.astype(BF16)
            hit = jnp.broadcast_to(kz, (extra, chunk)).astype(BF16) == freq_e
            parts.append(jnp.where(hit, wide, jnp.zeros_like(wide)))
        where = jnp.broadcast_to(slot, (cols, chunk)).astype(BF16) == freq_s
        pick = jnp.where(where, jnp.ones((cols, chunk), BF16), jnp.zeros((cols, chunk), BF16))
        total = total + dot_t(jnp.concatenate(parts, axis=0), pick)
    line = total.astype(BF16)
    both = jnp.concatenate([line, line[: 2 * rows]] + ([line[4 * rows :]] if extra else []), axis=0)
    copies[2].wait()
    out_ref[...] = dot(table_ref[...], both)
    copy = pltpu.make_async_copy(out_ref, out_hbm, out_sem)
    copy.start()
    copy.wait()


def tables_kernel(
    cfg, col_hbm, yt_hbm, iy_hbm, ix_hbm, v_hbm, resid_hbm, tx_hbm, x_hbm, wide_hbm,
    e_ref, hot_ref, v_out_hbm, hist_ref, tx_ref, x_ref, wide_ref,
    col_ref, yt_ref, iy_ref, ix_ref, v_ref, resid_ref, v_work, v_out_ref, out_sem, sems,
):
    ncol, rows, m, zs, xs, ng = (cfg[k] for k in ("ncol", "k_rows", "m", "zs", "xs", "ng"))
    block = v_ref.shape[0]
    band = lax.axis_index("band")
    first = lax.rem(band, cfg["gz"]) * zs
    base = pl.multiple_of(lax.div(first, block) * block, 8)
    offset = first - base
    lanes = pl.multiple_of(lax.div(band, cfg["gz"]) * (xs * ng), LANES)
    v_mine = v_hbm.at[pl.ds(base, block), pl.ds(lanes, xs * ng)]
    copies = fetch(
        (
            (col_hbm, col_ref), (yt_hbm, yt_ref), (v_mine, v_ref), (iy_hbm, iy_ref), (ix_hbm, ix_ref), (resid_hbm, resid_ref),
            (tx_hbm, tx_ref), (x_hbm, x_ref), (wide_hbm, wide_ref),
        ),
        sems,
    )
    copies[0].wait()
    col = col_ref[...].astype(F32)
    kx = jnp.floor((col + 0.5) * (1.0 / ng))
    ky = col - kx * ng
    freq = row_freq((rows, ncol), ng, cfg["k_radius"]).astype(F32)
    hot_ref[...] = jnp.where(jnp.broadcast_to(kx, (rows, ncol)) == freq, 1.0, 0.0).astype(BF16)
    hot = jnp.where(jnp.broadcast_to(ky, (rows, ncol)) == freq, 1.0, 0.0)
    hot = hot.T.astype(BF16)
    copies[1].wait()
    width = 4 * m
    e_ref[:ncol] = dot(hot, yt_ref[:, :width]).astype(BF16)
    e_ref[ncol:] = dot(hot, yt_ref[:, width:]).astype(BF16)
    copies[2].wait()
    for x in range(xs):
        v_work[pl.ds(x, block, stride=xs), :] = v_ref[:, x * ng : (x + 1) * ng]
    copies[3].wait()
    copies[4].wait()
    for z in range(zs):
        at = pl.multiple_of((offset + z) * xs, 8)
        along = dot3(v_work[pl.ds(at, xs), :], iy_ref[0], iy_ref[1])
        high, low = split(along)
        v_out_ref[z * m : (z + 1) * m, :] = (
            dot(ix_ref[0], high) + dot(ix_ref[1], high) + dot(ix_ref[0], low)
        )
    out_copy = pltpu.make_async_copy(v_out_ref, v_out_hbm, out_sem)
    out_copy.start()
    copies[5].wait()
    hist = resid_ref.shape[0]
    lane = lax.broadcasted_iota(jnp.int32, hist_ref.shape, 1)
    row = jnp.zeros(hist_ref.shape, F32)
    for i in range(hist):
        left = resid_ref[i]
        for j in range(i, hist):
            value = jnp.sum(left * resid_ref[j], axis=0, keepdims=True)
            value = jnp.sum(value, axis=1, keepdims=True)
            row = row + jnp.where(lane == i * (hist + 1) + j, value, 0.0)
    hist_ref[...] = row
    for copy in copies[6:]:
        copy.wait()
    out_copy.wait()


def turned(value, m):
    if 2 * m > LANES:
        return jnp.concatenate([-value[:, m:], value[:, :m]], axis=1)
    lane = lax.broadcasted_iota(jnp.int32, value.shape, 1)
    moved = pltpu.roll(value, m, 1)
    return jnp.where(lane < m, -moved, moved)


def planes_kernel(
    cfg, in_ref, hot_ref, e_ref, tx_ref, ix_ref, v_hbm, hist_ref, out_ref, row_ref, piece_ref, v_ref, sems
):
    copies = fetch(((v_hbm, v_ref),), sems)
    ncol, rows, m, zs, cols = cfg["ncol"], cfg["k_rows"], cfg["m"], cfg["zs"], cfg["cols"]
    npw, bands, per = cfg["npw"], cfg["bands"], cfg["chunk_bands"]
    value = in_ref[...]
    high = value.astype(BF16).astype(F32)
    count = value.shape[0]
    piece_ref[0, :count] = high
    piece_ref[1, :count] = value - high
    hits = [hot_ref[:, p * cols : (p + 1) * cols] > 0 for p in range(npw)]
    none = jnp.zeros((rows, cols), BF16)
    lane = lax.broadcasted_iota(jnp.int32, row_ref.shape, 1)

    def left(part, first):
        lanes = []
        for comp in range(2):
            for p in range(npw):
                column = []
                for b in range(per):
                    for z in range(zs):
                        at = ((first + b) * npw + p) * 2 * zs + comp * zs + z
                        line = piece_ref[part, pl.ds(at, 8, stride=0), :]
                        line = jnp.concatenate([line, line], axis=0).astype(BF16)
                        column.append(jnp.where(hits[p], jnp.concatenate([line] * (rows // 16), axis=0), none))
                lanes.append(jnp.concatenate(column, axis=0))
        return jnp.concatenate(lanes, axis=1)

    def step(first, carry):
        dens, energy = carry
        dens = list(dens)
        grid = dot(left(0, first), e_ref[...])
        grid = grid[:, : 2 * m] + grid[:, 2 * m :] + dot(left(1, first), e_ref[:, : 2 * m])
        grids = [part for value in (grid, turned(grid, m)) for part in split(value)]

        def stack(b, z):
            at = (b * zs + z) * rows
            parts = [grids[k][at : at + rows] for k in (0, 2, 1, 3, 0, 2)]
            return jnp.concatenate(parts, axis=0)

        group = 2 if zs % 2 == 0 else 1
        for b in range(per):
            acc = jnp.zeros((m, 2 * m), F32)
            for z in range(0, zs, group):
                both = jnp.concatenate([stack(b, z + k) for k in range(group)], axis=1)
                psi = dot(tx_ref[...], both)
                for k in range(group):
                    square = psi[:, k * 2 * m : (k + 1) * 2 * m]
                    square = square * square
                    dens[z + k] = dens[z + k] + square
                    acc = acc + square * v_ref[(z + k) * m : (z + k + 1) * m, :]
            part = jnp.sum(jnp.sum(acc, axis=0, keepdims=True), axis=1, keepdims=True)
            energy = energy + jnp.where(lane == cfg["row"] + first + b, part, 0.0)
        return tuple(dens), energy

    carry = (
        tuple(jnp.zeros((m, 2 * m), F32) for _ in range(zs)),
        hist_ref[...],
    )
    copies[0].wait()
    if bands // per <= 2:
        for first in range(0, bands, per):
            carry = step(first, carry)
    else:
        carry = lax.fori_loop(0, bands // per, lambda i, c: step(i * per, c), carry)
    dens, energy = carry
    row_ref[...] = energy
    pk, xr, gz = cfg["pk"], cfg["xr"], cfg["gz"]
    merged = []
    for zp in range(zs // pk):
        folded = []
        for half in range(pk):
            value = dens[zp * pk + half]
            folded.append(value[:, :m] + value[:, m:])
        merged.append(jnp.concatenate(folded, axis=1) if pk > 1 else folded[0])
    high, low = split(jnp.concatenate(merged, axis=1))
    rows_x = dot(ix_ref[...], jnp.concatenate([high, high, low], axis=0))
    for zp in range(zs // pk):
        for g in range(gz):
            at = (g * (zs // pk) + zp) * xr
            out_ref[at : at + xr, :] = rows_x[g * xr : (g + 1) * xr, zp * pk * m : (zp + 1) * pk * m]


def cells_kernel(cfg, in_ref, row_ref, iy_ref, rho_ref, resid_ref, dens_ref, send_ref, work):
    pk, xr, ng = cfg["pk"], cfg["xr"], cfg["ng"]
    count = in_ref.shape[0] // xr
    high, low = split(in_ref[...])
    cells = dot(jnp.concatenate([high, high, low], axis=1), iy_ref[...])
    for at in range(count):
        for half in range(pk):
            to = (at * pk + half) * xr
            work[to : to + xr, :] = cells[at * xr : (at + 1) * xr, half * ng : (half + 1) * ng]
    hist = resid_ref.shape[0]
    sums = [None] * (hist + 1)
    for x in range(xr):
        at = slice(x * ng, (x + 1) * ng)
        value = work[pl.ds(x, count * pk, stride=xr), :]
        dens_ref[:, at] = value
        last = value - rho_ref[:, at]
        for i in range(hist + 1):
            term = last * (resid_ref[i, :, at] if i < hist else last)
            sums[i] = term if x == 0 else sums[i] + term
    lane = lax.broadcasted_iota(jnp.int32, row_ref.shape, 1)
    row = row_ref[...]
    for i in range(hist + 1):
        value = jnp.sum(jnp.sum(sums[i], axis=0, keepdims=True), axis=1, keepdims=True)
        row = row + jnp.where(lane == i * (hist + 1) + hist, value, 0.0)
    send_ref[...] = jnp.broadcast_to(row, send_ref.shape)


def mix_kernel(
    cfg, in_ref, dens_ref, rho_ref, rho_hist_ref, resid_ref, occ_ref,
    dens_hbm, mixed_hbm, energy_hbm, norm_hbm, mixed_ref, energy_ref, norm_ref, sems,
):
    dens_copy = pltpu.make_async_copy(dens_ref, dens_hbm, sems.at[2])
    dens_copy.start()
    hist = resid_ref.shape[0]
    size = hist + 1
    row = jnp.sum(in_ref[...], axis=0, keepdims=True) * (1.0 / cfg["ng"] ** 3)
    lane = lax.broadcasted_iota(jnp.int32, row.shape, 1)

    def pick(at):
        return jnp.sum(jnp.where(lane == at, row, 0.0), axis=1, keepdims=True)

    gram = {(i, j): pick(i * size + j) for i in range(size) for j in range(i, size)}
    low = {}
    for j in range(size):
        value = gram[(j, j)]
        for k in range(j):
            value = value - low[(j, k)] * low[(j, k)]
        low[(j, j)] = jnp.sqrt(value)
        for i in range(j + 1, size):
            value = gram[(j, i)]
            for k in range(j):
                value = value - low[(i, k)] * low[(j, k)]
            low[(i, j)] = value / low[(j, j)]
    half = []
    for i in range(size):
        value = jnp.ones((1, 1), F32)
        for k in range(i):
            value = value - low[(i, k)] * half[k]
        half.append(value / low[(i, i)])
    solved = [None] * size
    for i in reversed(range(size)):
        value = half[i]
        for k in range(i + 1, size):
            value = value - low[(k, i)] * solved[k]
        solved[i] = value / low[(i, i)]
    total = solved[0]
    for value in solved[1:]:
        total = total + value
    coef = [value / total for value in solved]
    norm_ref[...] = jnp.sqrt(gram[(hist, hist)])
    weight = occ_ref[0].astype(F32) * (1.0 / cfg["bands"])
    energy_ref[...] = pick(cfg["row"] + lax.axis_index("band")) / jnp.full((1, 1), weight, F32)
    planes, width = mixed_ref.shape
    copies = fetch(((energy_ref, energy_hbm), (norm_ref, norm_hbm)), sems) + [dens_copy]
    step = 8
    for at in range(0, planes, step):
        rows = slice(at, at + step)
        for first in range(0, width, 4 * LANES):
            lanes = slice(first, min(first + 4 * LANES, width))
            rho = rho_ref[rows, lanes]
            mixed = coef[hist] * (rho + 0.8 * (dens_ref[rows, lanes] - rho))
            for i in range(hist):
                mixed = mixed + coef[i] * (rho_hist_ref[i, rows, lanes] + 0.8 * resid_ref[i, rows, lanes])
            mixed_ref[rows, lanes] = mixed
        copy = pltpu.make_async_copy(mixed_ref.at[rows, :], mixed_hbm.at[rows, :], sems.at[3 + at // step])
        copy.start()
        copies.append(copy)
    for copy in copies:
        copy.wait()


SPACES = {"u": pltpu.HBM, "v": pltpu.VMEM, "p": pltpu.VMEM, "s": pltpu.SMEM, "h": pltpu.HBM}


def call(kernel, cfg, outs, spaces, out_spaces, scratch, copies, name, limit):
    sems = [pltpu.SemaphoreType.DMA((copies,))] if copies else []
    run = pl.pallas_call(
        lambda *refs: kernel(cfg, *refs),
        out_shape=tuple(
            SPACES[space](out.shape, out.dtype) if space in "hp" else out
            for out, space in zip(outs, out_spaces, strict=True)
        ),
        in_specs=[pl.BlockSpec(memory_space=SPACES[space]) for space in spaces],
        out_specs=tuple(pl.BlockSpec(memory_space=SPACES[space]) for space in out_spaces),
        scratch_shapes=list(scratch) + sems,
        compiler_params=pltpu.CompilerParams(vmem_limit_bytes=limit),
        name=name,
    )

    def placed(*args):
        return run(*(
            pltpu.with_memory_space_constraint(arg, SPACES[space]) if space in "hp" else arg
            for arg, space in zip(args, spaces, strict=True)
        ))

    return placed


def held(*arrays):
    return [pltpu.VMEM(array.shape, array.dtype) for array in arrays]


def slice_x(table, axis, gx, gz, xs):
    if gx == 1:
        return table
    return lax.dynamic_slice_in_dim(table, lax.axis_index("band") // gz * xs, xs, axis)


def build(mesh):
    nband, npw = mesh.shape["band"], mesh.shape["pw"]
    both = ("band", "pw")

    def local(coefficients, pw_index, col_index, occupation, v_local, rho_in, rho_hist, resid_hist):
        bands_dev, _, count = coefficients.shape
        planes, cells = v_local.shape
        ng = planes * npw
        ncol = col_index.shape[0]
        cols = ncol // npw
        hist = resid_hist.shape[0]
        assert bands_dev == 1 and ng * ng == cells and ng == LANES
        bands = nband
        gz = math.gcd(planes, nband)
        gx = nband // gz
        zs, xs, xr = planes // gz, ng // gx, ng // nband
        kz_radius = line_radius(ng, cols, count)
        k_radius = plane_radius(ng, ncol)
        m = ng
        while m % 2 == 0 and m // 2 > 4 * k_radius and zs % (2 * ng // m) == 0:
            m //= 2
        pk = ng // m
        kz_vals, _ = box(ng, kz_radius, 16)
        kz_rows, kz_rest, kz_extra = kz_split(len(kz_vals))
        k_vals, k_rows = box(ng, k_radius, 16)
        if k_rows % 32:
            k_rows = up(k_rows, 32)
        chunk_bands = bands
        while chunk_bands % 2 == 0 and chunk_bands * zs * k_rows > 1024:
            chunk_bands //= 2
        cfg = dict(
            ng=ng, ncol=ncol, cols=cols, bands=bands, npw=npw, gz=gz, zs=zs, xs=xs, xr=xr, m=m, pk=pk,
            kz_radius=kz_radius, k_radius=k_radius, kz_real=len(kz_vals), k_rows=k_rows, chunk_bands=chunk_bands,
            row=(hist + 1) ** 2,
        )
        turn = 2.0 * math.pi / ng
        z_of = (
            np.arange(npw)[None, :, None] * planes
            + (np.arange(nband) % gz)[:, None, None] * zs
            + np.arange(zs)[None, None, :]
        )
        angle = turn * (z_of[..., None] * kz_vals % ng)
        cz, sz = np.cos(angle), np.sin(angle)
        z_table = np.stack([np.stack([cz, -sz], -2), np.stack([sz, cz], -2)], axis=2)
        z_high, z_low = split_np(z_table.reshape(-1, 2, len(kz_vals)))
        flat = lambda table: table.reshape(table.shape[0], -1)
        main = [flat(table[:, :, :kz_rows]) for table in (z_high, z_low)]
        spare = [flat(table[:, :, kz_rows:]) for table in (z_high, z_low)]
        pad = [np.zeros((z_high.shape[0], kz_extra - 2 * k * kz_rest), z_high.dtype) for k in (2, 1)]
        z_table = jnp.asarray(np.concatenate(
            [main[0], main[0], spare[0], spare[0], pad[0], main[1], spare[1], pad[1]], axis=1
        ))
        angle = turn * pk * (k_vals[:, None] * np.arange(m)[None, :])
        cy, sy = np.zeros((2, k_rows, m))
        cy[: len(k_vals)], sy[: len(k_vals)] = np.cos(angle), np.sin(angle)
        real = split_np(np.concatenate([cy, sy], axis=1))
        imag = split_np(np.concatenate([-sy, cy], axis=1))
        y_table = jnp.asarray(np.concatenate([*real, *imag], axis=1))
        x_high, x_low = split_np(np.concatenate([cy.T, sy.T], axis=1))
        x_table = jnp.asarray(np.concatenate([x_high, x_high, x_low], axis=1))
        inter = interpolation(ng, m)
        iy_twice = jnp.asarray(np.stack(split_np(np.concatenate([inter, inter], axis=1))))
        wide = np.zeros((pk * m, pk * ng))
        for half in range(pk):
            wide[half * m : (half + 1) * m, half * ng : (half + 1) * ng] = inter.T
        w_high, w_low = split_np(wide)
        iy_wide = jnp.asarray(np.concatenate([w_high, w_low, w_high], axis=0))
        x_high, x_low = split_np(inter)
        ix_full = jnp.asarray(np.concatenate([x_high, x_low, x_high], axis=1))
        ixt_full = jnp.asarray(np.stack(split_np(inter.T)))

        index = pw_index.reshape(1, count)
        col = col_index.reshape(1, ncol)
        shape = jax.ShapeDtypeStruct
        width = up(cfg["row"] + bands, LANES)
        mib = 1024 * 1024

        sent_shape = shape((nband * npw * 2 * zs, cols), F32)
        (sent,) = call(
            columns_kernel, cfg, (sent_shape,), "shhh", "h",
            held(index, coefficients, z_table, sent_shape) + [pltpu.SemaphoreType.DMA((3,)), pltpu.SemaphoreType.DMA],
            0, "columns", 40 * mib,
        )(occupation, index, coefficients, z_table)
        received = lax.all_to_all(sent, both, 0, 0, tiled=True)
        block = max(zs, 8)
        assert planes % block == 0 and xs % 8 == 0
        v_block = shape((block, xs * ng), F32)
        ix = slice_x(ix_full, 0, gx, gz, xs)
        e_table, hot, v_grid, hist_row, tx, ix, iy = call(
            tables_kernel, cfg,
            (
                shape((2 * ncol, 4 * m), BF16), shape((k_rows, ncol), BF16), shape((zs * m, 2 * m), F32), shape((1, width), F32),
                x_table, ix, iy_wide,
            ),
            "h" * 9, "pphpppp",
            held(
                col, y_table, iy_twice, ixt_full[:, :, :xs], v_block, resid_hist,
                shape((block * xs, ng), F32), shape((zs * m, 2 * m), F32),
            ) + [pltpu.SemaphoreType.DMA],
            9, "tables", 40 * mib,
        )(col, y_table, iy_twice, slice_x(ixt_full, 2, gx, gz, xs), v_local, resid_hist, x_table, ix, iy_wide)
        to_cells, row = call(
            planes_kernel, cfg, (shape((gz * (zs // pk) * xr, pk * m), F32), shape((1, width), F32)),
            "vpppphp", "pp",
            held(shape((2, received.shape[0] + 8, cols), F32), v_grid), 1, "planes", 40 * mib,
        )(received, hot, e_table, tx, ix, v_grid, hist_row)
        groups = None if gx == 1 else [list(range(g * gz, (g + 1) * gz)) for g in range(gx)]
        mine = lax.all_to_all(to_cells, "band", 0, 0, axis_index_groups=groups, tiled=True)
        dens, rows = call(
            cells_kernel, cfg, (shape(rho_in.shape, F32), shape((nband * npw, width), F32)),
            "vppvv", "pp", [pltpu.VMEM((mine.shape[0] * pk, ng), F32)], 0, "cells", 16 * mib,
        )(mine, row, iy, rho_in, resid_hist)
        rows = lax.all_to_all(rows, both, 0, 0, tiled=True)
        one = shape((1, 1), F32)
        density, mixed, energy, norm = call(
            mix_kernel, cfg, (shape(rho_in.shape, F32), shape(rho_in.shape, F32), one, one),
            "vpvvvs", "hhuu", held(rho_in, one, one), 3 + planes // 8, "mix", 16 * mib,
        )(rows, dens, rho_in, rho_hist, resid_hist, occupation)
        return density, mixed, energy.reshape(1), norm.reshape(())

    return local


def solution(mesh):
    in_specs = (
        P("band", None, "pw"),
        P("pw"),
        P(),
        P("band"),
        P("pw", None),
        P("pw", "band"),
        P(None, "pw", "band"),
        P(None, "pw", "band"),
    )
    out_specs = (P("pw", "band"), P("pw", "band"), P("band"), P())
    return jax.shard_map(build(mesh), mesh=mesh, in_specs=in_specs, out_specs=out_specs, check_vma=False)
```

```python
import math

import jax
import jax.numpy as jnp
import numpy as np
from jax import lax
from jax.experimental import pallas as pl
from jax.experimental.pallas import tpu as pltpu
from jax.sharding import PartitionSpec as P

F32 = jnp.float32
BF16 = jnp.bfloat16
LANES = 128


def up(value, multiple):
    return -(-value // multiple) * multiple


def split_np(table):
    high = table.astype(np.float32).astype(jnp.bfloat16)
    low = (table - high.astype(np.float64)).astype(np.float32).astype(jnp.bfloat16)
    return high, low


def split(value):
    high = value.astype(BF16)
    low = (value - high.astype(F32)).astype(BF16)
    return high, low


def dot(left, right):
    return jnp.dot(left, right, preferred_element_type=F32)


def dot_t(left, right):
    return lax.dot_general(left, right, (((1,), (1,)), ((), ())), preferred_element_type=F32)


def dot3(left, right_high, right_low):
    high, low = split(left)
    return dot(high, right_high) + dot(high, right_low) + dot(low, right_high)


def signed(length):
    index = np.arange(length)
    return np.where(index > length // 2, index - length, index)


def plane_radius(length, count):
    freq = signed(length)
    norm = np.sort((freq[:, None] ** 2 + freq[None, :] ** 2).reshape(-1))
    return max(1, math.isqrt(int(norm[count - 1])))


def line_radius(length, columns, count):
    norm = np.sort(np.repeat(np.abs(signed(length)), columns))
    return max(1, int(norm[count - 1]))


def box(length, radius, multiple):
    real = min(length, 2 * radius + 1)
    rows = up(real, multiple)
    return (np.arange(real) - radius) % length, rows


def row_freq(shape, length, radius):
    row = lax.broadcasted_iota(jnp.int32, shape, 0)
    real = min(length, 2 * radius + 1)
    freq = jnp.where(row < radius, row - radius + length, row - radius)
    return jnp.where(row < real, freq, -1)


def interpolation(length, samples):
    if samples == length:
        return np.eye(length)
    shift = np.arange(length)[:, None] - np.arange(samples)[None, :] * (length // samples)
    total = np.cos(math.pi * samples * shift / length)
    for k in range(samples // 2):
        total = total + (2.0 if k else 1.0) * np.cos(2.0 * math.pi * k * shift / length)
    return total / samples


def kz_split(real):
    rows = real // 16 * 16
    return rows, real - rows, up(4 * (real - rows), 16)


def fetch(pairs, sems):
    copies = [pltpu.make_async_copy(src, dst, sems.at[i]) for i, (src, dst) in enumerate(pairs)]
    for copy in copies:
        copy.start()
    return copies


def columns_kernel(
    cfg, occ_ref, index_hbm, coef_hbm, table_hbm, out_hbm, index_ref, coef_ref, table_ref, out_ref, sems, out_sem
):
    copies = fetch(((index_hbm, index_ref), (coef_hbm, coef_ref), (table_hbm, table_ref)), sems)
    real, cols, ng, radius = cfg["kz_real"], cfg["cols"], cfg["ng"], cfg["kz_radius"]
    rows, rest, extra = kz_split(real)
    count = index_ref.shape[1]
    chunk = math.gcd(count, 1024)
    row = lax.broadcasted_iota(jnp.int32, (rows, chunk), 0)
    freq_k = jnp.where(row < radius, row - radius + ng, row - radius).astype(F32).astype(BF16)
    if extra:
        row = lax.broadcasted_iota(jnp.int32, (extra, chunk), 0)
        freq_e = jnp.where(row < 4 * rest, lax.rem(row, rest) + (rows - radius), -1).astype(F32).astype(BF16)
    freq_s = lax.broadcasted_iota(jnp.int32, (cols, chunk), 0).astype(F32).astype(BF16)
    weight = occ_ref[0].astype(F32) * (1.0 / cfg["bands"])
    scale = jnp.sqrt(jnp.full((1, chunk), weight, F32))
    total = jnp.zeros((4 * rows + extra, cols), F32)
    for copy in copies[:2]:
        copy.wait()
    for at in range(0, count, chunk):
        index = index_ref[:, at : at + chunk].astype(F32)
        kz = jnp.floor((index + 0.5) * (1.0 / cols))
        slot = index - kz * cols
        pieces = [None] * 4
        for comp in range(2):
            value = coef_ref[0, comp : comp + 1, at : at + chunk] * scale
            high = value.astype(BF16).astype(F32)
            pieces[comp], pieces[2 + comp] = high, value - high
        hit = jnp.broadcast_to(kz, (rows, chunk)).astype(BF16) == freq_k
        parts = []
        for piece in pieces:
            wide = jnp.broadcast_to(piece, (rows, chunk)).astype(BF16)
            parts.append(jnp.where(hit, wide, jnp.zeros_like(wide)))
        if extra:
            wide = jnp.broadcast_to(pieces[3], (extra, chunk))
            for k in (2, 1, 0):
                wide = jnp.where(row < (k + 1) * rest, jnp.broadcast_to(pieces[k], (extra, chunk)), wide)
            wide = wide.astype(BF16)
            hit = jnp.broadcast_to(kz, (extra, chunk)).astype(BF16) == freq_e
            parts.append(jnp.where(hit, wide, jnp.zeros_like(wide)))
        where = jnp.broadcast_to(slot, (cols, chunk)).astype(BF16) == freq_s
        pick = jnp.where(where, jnp.ones((cols, chunk), BF16), jnp.zeros((cols, chunk), BF16))
        total = total + dot_t(jnp.concatenate(parts, axis=0), pick)
    line = total.astype(BF16)
    both = jnp.concatenate([line, line[: 2 * rows]] + ([line[4 * rows :]] if extra else []), axis=0)
    copies[2].wait()
    out_ref[...] = dot(table_ref[...], both)
    copy = pltpu.make_async_copy(out_ref, out_hbm, out_sem)
    copy.start()
    copy.wait()


def tables_kernel(
    cfg, col_hbm, yt_hbm, iy_hbm, ix_hbm, v_hbm, resid_hbm, tx_hbm, x_hbm, wide_hbm,
    e_ref, hot_ref, v_out_ref, hist_ref, tx_ref, x_ref, wide_ref,
    col_ref, yt_ref, iy_ref, ix_ref, v_ref, resid_ref, v_work, sems,
):
    ncol, rows, m, zs, xs, ng = (cfg[k] for k in ("ncol", "k_rows", "m", "zs", "xs", "ng"))
    block = v_ref.shape[0]
    band = lax.axis_index("band")
    first = lax.rem(band, cfg["gz"]) * zs
    base = pl.multiple_of(lax.div(first, block) * block, 8)
    offset = first - base
    lanes = pl.multiple_of(lax.div(band, cfg["gz"]) * (xs * ng), LANES)
    v_mine = v_hbm.at[pl.ds(base, block), pl.ds(lanes, xs * ng)]
    copies = fetch(
        (
            (col_hbm, col_ref), (yt_hbm, yt_ref), (v_mine, v_ref), (iy_hbm, iy_ref), (ix_hbm, ix_ref), (resid_hbm, resid_ref),
            (tx_hbm, tx_ref), (x_hbm, x_ref), (wide_hbm, wide_ref),
        ),
        sems,
    )
    copies[0].wait()
    col = col_ref[...].astype(F32)
    kx = jnp.floor((col + 0.5) * (1.0 / ng))
    ky = col - kx * ng
    freq = row_freq((rows, ncol), ng, cfg["k_radius"]).astype(F32)
    hot_ref[...] = jnp.where(jnp.broadcast_to(kx, (rows, ncol)) == freq, 1.0, 0.0).astype(BF16)
    hot = jnp.where(jnp.broadcast_to(ky, (rows, ncol)) == freq, 1.0, 0.0)
    hot = hot.T.astype(BF16)
    copies[1].wait()
    width = 4 * m
    e_ref[:ncol] = dot(hot, yt_ref[:, :width]).astype(BF16)
    e_ref[ncol:] = dot(hot, yt_ref[:, width:]).astype(BF16)
    copies[2].wait()
    for x in range(xs):
        v_work[pl.ds(x, block, stride=xs), :] = v_ref[:, x * ng : (x + 1) * ng]
    copies[3].wait()
    copies[4].wait()
    for z in range(zs):
        at = pl.multiple_of((offset + z) * xs, 8)
        along = dot3(v_work[pl.ds(at, xs), :], iy_ref[0], iy_ref[1])
        high, low = split(along)
        v_out_ref[z * m : (z + 1) * m, :] = (
            dot(ix_ref[0], high) + dot(ix_ref[1], high) + dot(ix_ref[0], low)
        )
    copies[5].wait()
    hist = resid_ref.shape[0]
    lane = lax.broadcasted_iota(jnp.int32, hist_ref.shape, 1)
    row = jnp.zeros(hist_ref.shape, F32)
    for i in range(hist):
        left = resid_ref[i]
        for j in range(i, hist):
            value = jnp.sum(left * resid_ref[j], axis=0, keepdims=True)
            value = jnp.sum(value, axis=1, keepdims=True)
            row = row + jnp.where(lane == i * (hist + 1) + j, value, 0.0)
    hist_ref[...] = row
    for copy in copies[6:]:
        copy.wait()


def turned(value, m):
    if 2 * m > LANES:
        return jnp.concatenate([-value[:, m:], value[:, :m]], axis=1)
    lane = lax.broadcasted_iota(jnp.int32, value.shape, 1)
    moved = pltpu.roll(value, m, 1)
    return jnp.where(lane < m, -moved, moved)


def planes_kernel(
    cfg, in_ref, hot_ref, e_ref, tx_ref, ix_ref, v_ref, hist_ref, out_ref, row_ref, piece_ref
):
    ncol, rows, m, zs, cols = cfg["ncol"], cfg["k_rows"], cfg["m"], cfg["zs"], cfg["cols"]
    npw, bands, per = cfg["npw"], cfg["bands"], cfg["chunk_bands"]
    value = in_ref[...]
    high = value.astype(BF16).astype(F32)
    count = value.shape[0]
    piece_ref[0, :count] = high
    piece_ref[1, :count] = value - high
    hits = [hot_ref[:, p * cols : (p + 1) * cols] > 0 for p in range(npw)]
    none = jnp.zeros((rows, cols), BF16)
    lane = lax.broadcasted_iota(jnp.int32, row_ref.shape, 1)

    def left(part, first):
        lanes = []
        for comp in range(2):
            for p in range(npw):
                column = []
                for b in range(per):
                    for z in range(zs):
                        at = ((first + b) * npw + p) * 2 * zs + comp * zs + z
                        line = piece_ref[part, pl.ds(at, 8, stride=0), :]
                        line = jnp.concatenate([line, line], axis=0).astype(BF16)
                        column.append(jnp.where(hits[p], jnp.concatenate([line] * (rows // 16), axis=0), none))
                lanes.append(jnp.concatenate(column, axis=0))
        return jnp.concatenate(lanes, axis=1)

    def step(first, carry):
        dens, energy = carry
        dens = list(dens)
        grid = dot(left(0, first), e_ref[...])
        grid = grid[:, : 2 * m] + grid[:, 2 * m :] + dot(left(1, first), e_ref[:, : 2 * m])
        grids = [part for value in (grid, turned(grid, m)) for part in split(value)]

        def stack(b, z):
            at = (b * zs + z) * rows
            parts = [grids[k][at : at + rows] for k in (0, 2, 1, 3, 0, 2)]
            return jnp.concatenate(parts, axis=0)

        group = 2 if zs % 2 == 0 else 1
        for b in range(per):
            acc = jnp.zeros((m, 2 * m), F32)
            for z in range(0, zs, group):
                both = jnp.concatenate([stack(b, z + k) for k in range(group)], axis=1)
                psi = dot(tx_ref[...], both)
                for k in range(group):
                    square = psi[:, k * 2 * m : (k + 1) * 2 * m]
                    square = square * square
                    dens[z + k] = dens[z + k] + square
                    acc = acc + square * v_ref[(z + k) * m : (z + k + 1) * m, :]
            part = jnp.sum(jnp.sum(acc, axis=0, keepdims=True), axis=1, keepdims=True)
            energy = energy + jnp.where(lane == cfg["row"] + first + b, part, 0.0)
        return tuple(dens), energy

    carry = (
        tuple(jnp.zeros((m, 2 * m), F32) for _ in range(zs)),
        hist_ref[...],
    )
    if bands // per <= 2:
        for first in range(0, bands, per):
            carry = step(first, carry)
    else:
        carry = lax.fori_loop(0, bands // per, lambda i, c: step(i * per, c), carry)
    dens, energy = carry
    row_ref[...] = energy
    pk, xr, gz = cfg["pk"], cfg["xr"], cfg["gz"]
    merged = []
    for zp in range(zs // pk):
        folded = []
        for half in range(pk):
            value = dens[zp * pk + half]
            folded.append(value[:, :m] + value[:, m:])
        merged.append(jnp.concatenate(folded, axis=1) if pk > 1 else folded[0])
    high, low = split(jnp.concatenate(merged, axis=1))
    rows_x = dot(ix_ref[...], jnp.concatenate([high, high, low], axis=0))
    for zp in range(zs // pk):
        for g in range(gz):
            at = (g * (zs // pk) + zp) * xr
            out_ref[at : at + xr, :] = rows_x[g * xr : (g + 1) * xr, zp * pk * m : (zp + 1) * pk * m]


def cells_kernel(cfg, in_ref, row_ref, iy_ref, rho_ref, resid_ref, dens_ref, send_ref, work):
    pk, xr, ng = cfg["pk"], cfg["xr"], cfg["ng"]
    count = in_ref.shape[0] // xr
    high, low = split(in_ref[...])
    cells = dot(jnp.concatenate([high, high, low], axis=1), iy_ref[...])
    for at in range(count):
        for half in range(pk):
            to = (at * pk + half) * xr
            work[to : to + xr, :] = cells[at * xr : (at + 1) * xr, half * ng : (half + 1) * ng]
    hist = resid_ref.shape[0]
    sums = [None] * (hist + 1)
    for x in range(xr):
        at = slice(x * ng, (x + 1) * ng)
        value = work[pl.ds(x, count * pk, stride=xr), :]
        dens_ref[:, at] = value
        last = value - rho_ref[:, at]
        for i in range(hist + 1):
            term = last * (resid_ref[i, :, at] if i < hist else last)
            sums[i] = term if x == 0 else sums[i] + term
    lane = lax.broadcasted_iota(jnp.int32, row_ref.shape, 1)
    row = row_ref[...]
    for i in range(hist + 1):
        value = jnp.sum(jnp.sum(sums[i], axis=0, keepdims=True), axis=1, keepdims=True)
        row = row + jnp.where(lane == i * (hist + 1) + hist, value, 0.0)
    send_ref[...] = jnp.broadcast_to(row, send_ref.shape)


def mix_kernel(
    cfg, in_ref, dens_ref, rho_ref, rho_hist_ref, resid_ref, occ_ref,
    dens_hbm, mixed_hbm, energy_hbm, norm_hbm, mixed_ref, energy_ref, norm_ref, sems,
):
    dens_copy = pltpu.make_async_copy(dens_ref, dens_hbm, sems.at[2])
    dens_copy.start()
    hist = resid_ref.shape[0]
    size = hist + 1
    row = jnp.sum(in_ref[...], axis=0, keepdims=True) * (1.0 / cfg["ng"] ** 3)
    lane = lax.broadcasted_iota(jnp.int32, row.shape, 1)

    def pick(at):
        return jnp.sum(jnp.where(lane == at, row, 0.0), axis=1, keepdims=True)

    gram = {(i, j): pick(i * size + j) for i in range(size) for j in range(i, size)}
    low = {}
    for j in range(size):
        value = gram[(j, j)]
        for k in range(j):
            value = value - low[(j, k)] * low[(j, k)]
        low[(j, j)] = jnp.sqrt(value)
        for i in range(j + 1, size):
            value = gram[(j, i)]
            for k in range(j):
                value = value - low[(i, k)] * low[(j, k)]
            low[(i, j)] = value / low[(j, j)]
    half = []
    for i in range(size):
        value = jnp.ones((1, 1), F32)
        for k in range(i):
            value = value - low[(i, k)] * half[k]
        half.append(value / low[(i, i)])
    solved = [None] * size
    for i in reversed(range(size)):
        value = half[i]
        for k in range(i + 1, size):
            value = value - low[(k, i)] * solved[k]
        solved[i] = value / low[(i, i)]
    total = solved[0]
    for value in solved[1:]:
        total = total + value
    coef = [value / total for value in solved]
    norm_ref[...] = jnp.sqrt(gram[(hist, hist)])
    weight = occ_ref[0].astype(F32) * (1.0 / cfg["bands"])
    energy_ref[...] = pick(cfg["row"] + lax.axis_index("band")) / jnp.full((1, 1), weight, F32)
    planes, width = mixed_ref.shape
    copies = fetch(((energy_ref, energy_hbm), (norm_ref, norm_hbm)), sems) + [dens_copy]
    step = 8
    for at in range(0, planes, step):
        rows = slice(at, at + step)
        for first in range(0, width, 4 * LANES):
            lanes = slice(first, min(first + 4 * LANES, width))
            rho = rho_ref[rows, lanes]
            mixed = coef[hist] * (rho + 0.8 * (dens_ref[rows, lanes] - rho))
            for i in range(hist):
                mixed = mixed + coef[i] * (rho_hist_ref[i, rows, lanes] + 0.8 * resid_ref[i, rows, lanes])
            mixed_ref[rows, lanes] = mixed
        copy = pltpu.make_async_copy(mixed_ref.at[rows, :], mixed_hbm.at[rows, :], sems.at[3 + at // step])
        copy.start()
        copies.append(copy)
    for copy in copies:
        copy.wait()


SPACES = {"u": pltpu.HBM, "v": pltpu.VMEM, "p": pltpu.VMEM, "s": pltpu.SMEM, "h": pltpu.HBM}


def call(kernel, cfg, outs, spaces, out_spaces, scratch, copies, name, limit):
    sems = [pltpu.SemaphoreType.DMA((copies,))] if copies else []
    run = pl.pallas_call(
        lambda *refs: kernel(cfg, *refs),
        out_shape=tuple(
            SPACES[space](out.shape, out.dtype) if space in "hp" else out
            for out, space in zip(outs, out_spaces, strict=True)
        ),
        in_specs=[pl.BlockSpec(memory_space=SPACES[space]) for space in spaces],
        out_specs=tuple(pl.BlockSpec(memory_space=SPACES[space]) for space in out_spaces),
        scratch_shapes=list(scratch) + sems,
        compiler_params=pltpu.CompilerParams(vmem_limit_bytes=limit),
        name=name,
    )

    def placed(*args):
        return run(*(
            pltpu.with_memory_space_constraint(arg, SPACES[space]) if space in "hp" else arg
            for arg, space in zip(args, spaces, strict=True)
        ))

    return placed


def held(*arrays):
    return [pltpu.VMEM(array.shape, array.dtype) for array in arrays]


def slice_x(table, axis, gx, gz, xs):
    if gx == 1:
        return table
    return lax.dynamic_slice_in_dim(table, lax.axis_index("band") // gz * xs, xs, axis)


def build(mesh):
    nband, npw = mesh.shape["band"], mesh.shape["pw"]
    both = ("band", "pw")

    def local(coefficients, pw_index, col_index, occupation, v_local, rho_in, rho_hist, resid_hist):
        bands_dev, _, count = coefficients.shape
        planes, cells = v_local.shape
        ng = planes * npw
        ncol = col_index.shape[0]
        cols = ncol // npw
        hist = resid_hist.shape[0]
        assert bands_dev == 1 and ng * ng == cells and ng == LANES
        bands = nband
        gz = math.gcd(planes, nband)
        gx = nband // gz
        zs, xs, xr = planes // gz, ng // gx, ng // nband
        kz_radius = line_radius(ng, cols, count)
        k_radius = plane_radius(ng, ncol)
        m = ng
        while m % 2 == 0 and m // 2 > 4 * k_radius and zs % (2 * ng // m) == 0:
            m //= 2
        pk = ng // m
        kz_vals, _ = box(ng, kz_radius, 16)
        kz_rows, kz_rest, kz_extra = kz_split(len(kz_vals))
        k_vals, k_rows = box(ng, k_radius, 16)
        if k_rows % 32:
            k_rows = up(k_rows, 32)
        chunk_bands = bands
        while chunk_bands % 2 == 0 and chunk_bands * zs * k_rows > 1024:
            chunk_bands //= 2
        cfg = dict(
            ng=ng, ncol=ncol, cols=cols, bands=bands, npw=npw, gz=gz, zs=zs, xs=xs, xr=xr, m=m, pk=pk,
            kz_radius=kz_radius, k_radius=k_radius, kz_real=len(kz_vals), k_rows=k_rows, chunk_bands=chunk_bands,
            row=(hist + 1) ** 2,
        )
        turn = 2.0 * math.pi / ng
        z_of = (
            np.arange(npw)[None, :, None] * planes
            + (np.arange(nband) % gz)[:, None, None] * zs
            + np.arange(zs)[None, None, :]
        )
        angle = turn * (z_of[..., None] * kz_vals % ng)
        cz, sz = np.cos(angle), np.sin(angle)
        z_table = np.stack([np.stack([cz, -sz], -2), np.stack([sz, cz], -2)], axis=2)
        z_high, z_low = split_np(z_table.reshape(-1, 2, len(kz_vals)))
        flat = lambda table: table.reshape(table.shape[0], -1)
        main = [flat(table[:, :, :kz_rows]) for table in (z_high, z_low)]
        spare = [flat(table[:, :, kz_rows:]) for table in (z_high, z_low)]
        pad = [np.zeros((z_high.shape[0], kz_extra - 2 * k * kz_rest), z_high.dtype) for k in (2, 1)]
        z_table = jnp.asarray(np.concatenate(
            [main[0], main[0], spare[0], spare[0], pad[0], main[1], spare[1], pad[1]], axis=1
        ))
        angle = turn * pk * (k_vals[:, None] * np.arange(m)[None, :])
        cy, sy = np.zeros((2, k_rows, m))
        cy[: len(k_vals)], sy[: len(k_vals)] = np.cos(angle), np.sin(angle)
        real = split_np(np.concatenate([cy, sy], axis=1))
        imag = split_np(np.concatenate([-sy, cy], axis=1))
        y_table = jnp.asarray(np.concatenate([*real, *imag], axis=1))
        x_high, x_low = split_np(np.concatenate([cy.T, sy.T], axis=1))
        x_table = jnp.asarray(np.concatenate([x_high, x_high, x_low], axis=1))
        inter = interpolation(ng, m)
        iy_twice = jnp.asarray(np.stack(split_np(np.concatenate([inter, inter], axis=1))))
        wide = np.zeros((pk * m, pk * ng))
        for half in range(pk):
            wide[half * m : (half + 1) * m, half * ng : (half + 1) * ng] = inter.T
        w_high, w_low = split_np(wide)
        iy_wide = jnp.asarray(np.concatenate([w_high, w_low, w_high], axis=0))
        x_high, x_low = split_np(inter)
        ix_full = jnp.asarray(np.concatenate([x_high, x_low, x_high], axis=1))
        ixt_full = jnp.asarray(np.stack(split_np(inter.T)))

        index = pw_index.reshape(1, count)
        col = col_index.reshape(1, ncol)
        shape = jax.ShapeDtypeStruct
        width = up(cfg["row"] + bands, LANES)
        mib = 1024 * 1024

        sent_shape = shape((nband * npw * 2 * zs, cols), F32)
        (sent,) = call(
            columns_kernel, cfg, (sent_shape,), "shhh", "h",
            held(index, coefficients, z_table, sent_shape) + [pltpu.SemaphoreType.DMA((3,)), pltpu.SemaphoreType.DMA],
            0, "columns", 40 * mib,
        )(occupation, index, coefficients, z_table)
        received = lax.all_to_all(sent, both, 0, 0, tiled=True)
        block = max(zs, 8)
        assert planes % block == 0 and xs % 8 == 0
        v_block = shape((block, xs * ng), F32)
        ix = slice_x(ix_full, 0, gx, gz, xs)
        e_table, hot, v_grid, hist_row, tx, ix, iy = call(
            tables_kernel, cfg,
            (
                shape((2 * ncol, 4 * m), BF16), shape((k_rows, ncol), BF16), shape((zs * m, 2 * m), F32), shape((1, width), F32),
                x_table, ix, iy_wide,
            ),
            "h" * 9, "ppppppp",
            held(
                col, y_table, iy_twice, ixt_full[:, :, :xs], v_block, resid_hist,
                shape((block * xs, ng), F32),
            ),
            9, "tables", 40 * mib,
        )(col, y_table, iy_twice, slice_x(ixt_full, 2, gx, gz, xs), v_local, resid_hist, x_table, ix, iy_wide)
        to_cells, row = call(
            planes_kernel, cfg, (shape((gz * (zs // pk) * xr, pk * m), F32), shape((1, width), F32)),
            "vpppppp", "pp", held(shape((2, received.shape[0] + 8, cols), F32)), 0, "planes", 40 * mib,
        )(received, hot, e_table, tx, ix, v_grid, hist_row)
        groups = None if gx == 1 else [list(range(g * gz, (g + 1) * gz)) for g in range(gx)]
        mine = lax.all_to_all(to_cells, "band", 0, 0, axis_index_groups=groups, tiled=True)
        dens, rows = call(
            cells_kernel, cfg, (shape(rho_in.shape, F32), shape((nband * npw, width), F32)),
            "vppvv", "pp", [pltpu.VMEM((mine.shape[0] * pk, ng), F32)], 0, "cells", 16 * mib,
        )(mine, row, iy, rho_in, resid_hist)
        rows = lax.all_to_all(rows, both, 0, 0, tiled=True)
        one = shape((1, 1), F32)
        density, mixed, energy, norm = call(
            mix_kernel, cfg, (shape(rho_in.shape, F32), shape(rho_in.shape, F32), one, one),
            "vpvvvs", "hhuu", held(rho_in, one, one), 3 + planes // 8, "mix", 16 * mib,
        )(rows, dens, rho_in, rho_hist, resid_hist, occupation)
        return density, mixed, energy.reshape(1), norm.reshape(())

    return local


def solution(mesh):
    in_specs = (
        P("band", None, "pw"),
        P("pw"),
        P(),
        P("band"),
        P("pw", None),
        P("pw", "band"),
        P(None, "pw", "band"),
        P(None, "pw", "band"),
    )
    out_specs = (P("pw", "band"), P("pw", "band"), P("band"), P())
    return jax.shard_map(build(mesh), mesh=mesh, in_specs=in_specs, out_specs=out_specs, check_vma=False)
```

```python
import math

import jax
import jax.numpy as jnp
import numpy as np
from jax import lax
from jax.experimental import pallas as pl
from jax.experimental.pallas import tpu as pltpu
from jax.sharding import PartitionSpec as P

F32 = jnp.float32
BF16 = jnp.bfloat16
LANES = 128


def up(value, multiple):
    return -(-value // multiple) * multiple


def split_np(table):
    high = table.astype(np.float32).astype(jnp.bfloat16)
    low = (table - high.astype(np.float64)).astype(np.float32).astype(jnp.bfloat16)
    return high, low


def split(value):
    high = value.astype(BF16)
    low = (value - high.astype(F32)).astype(BF16)
    return high, low


def dot(left, right):
    return jnp.dot(left, right, preferred_element_type=F32)


def dot_t(left, right):
    return lax.dot_general(left, right, (((1,), (1,)), ((), ())), preferred_element_type=F32)


def dot3(left, right_high, right_low):
    high, low = split(left)
    return dot(high, right_high) + dot(high, right_low) + dot(low, right_high)


def signed(length):
    index = np.arange(length)
    return np.where(index > length // 2, index - length, index)


def plane_radius(length, count):
    freq = signed(length)
    norm = np.sort((freq[:, None] ** 2 + freq[None, :] ** 2).reshape(-1))
    return max(1, math.isqrt(int(norm[count - 1])))


def line_radius(length, columns, count):
    norm = np.sort(np.repeat(np.abs(signed(length)), columns))
    return max(1, int(norm[count - 1]))


def box(length, radius, multiple):
    real = min(length, 2 * radius + 1)
    rows = up(real, multiple)
    return (np.arange(real) - radius) % length, rows


def row_freq(shape, length, radius):
    row = lax.broadcasted_iota(jnp.int32, shape, 0)
    real = min(length, 2 * radius + 1)
    freq = jnp.where(row < radius, row - radius + length, row - radius)
    return jnp.where(row < real, freq, -1)


def interpolation(length, samples):
    if samples == length:
        return np.eye(length)
    shift = np.arange(length)[:, None] - np.arange(samples)[None, :] * (length // samples)
    total = np.cos(math.pi * samples * shift / length)
    for k in range(samples // 2):
        total = total + (2.0 if k else 1.0) * np.cos(2.0 * math.pi * k * shift / length)
    return total / samples


def kz_split(real):
    rows = real // 16 * 16
    return rows, real - rows, up(4 * (real - rows), 16)


def shuffled(size):
    return [int(k) for k in np.random.RandomState(44).permutation(size)]


def snake(rows, columns):
    members = []
    for i in range(rows):
        row = i ^ (i >> 1) if rows & (rows - 1) == 0 else i
        line = [row * columns + k for k in range(columns)]
        members += line[::-1] if i % 2 else line
    return members


def inverse(members):
    return [members.index(k) for k in range(len(members))]


def fetch(pairs, sems):
    copies = [pltpu.make_async_copy(src, dst, sems.at[i]) for i, (src, dst) in enumerate(pairs)]
    for copy in copies:
        copy.start()
    return copies


def columns_kernel(
    cfg, occ_ref, index_hbm, coef_hbm, table_hbm, out_hbm, index_ref, coef_ref, table_ref, out_ref, sems, out_sem
):
    copies = fetch(((index_hbm, index_ref), (coef_hbm, coef_ref), (table_hbm, table_ref)), sems)
    real, cols, ng, radius = cfg["kz_real"], cfg["cols"], cfg["ng"], cfg["kz_radius"]
    rows, rest, extra = kz_split(real)
    count = index_ref.shape[1]
    chunk = math.gcd(count, 1024)
    row = lax.broadcasted_iota(jnp.int32, (rows, chunk), 0)
    freq_k = jnp.where(row < radius, row - radius + ng, row - radius).astype(F32).astype(BF16)
    if extra:
        row = lax.broadcasted_iota(jnp.int32, (extra, chunk), 0)
        freq_e = jnp.where(row < 4 * rest, lax.rem(row, rest) + (rows - radius), -1).astype(F32).astype(BF16)
    freq_s = lax.broadcasted_iota(jnp.int32, (cols, chunk), 0).astype(F32).astype(BF16)
    weight = occ_ref[0].astype(F32) * (1.0 / cfg["bands"])
    scale = jnp.sqrt(jnp.full((1, chunk), weight, F32))
    total = jnp.zeros((4 * rows + extra, cols), F32)
    for copy in copies[:2]:
        copy.wait()
    for at in range(0, count, chunk):
        index = index_ref[:, at : at + chunk].astype(F32)
        kz = jnp.floor((index + 0.5) * (1.0 / cols))
        slot = index - kz * cols
        pieces = [None] * 4
        for comp in range(2):
            value = coef_ref[0, comp : comp + 1, at : at + chunk] * scale
            high = value.astype(BF16).astype(F32)
            pieces[comp], pieces[2 + comp] = high, value - high
        hit = jnp.broadcast_to(kz, (rows, chunk)).astype(BF16) == freq_k
        parts = []
        for piece in pieces:
            wide = jnp.broadcast_to(piece, (rows, chunk)).astype(BF16)
            parts.append(jnp.where(hit, wide, jnp.zeros_like(wide)))
        if extra:
            wide = jnp.broadcast_to(pieces[3], (extra, chunk))
            for k in (2, 1, 0):
                wide = jnp.where(row < (k + 1) * rest, jnp.broadcast_to(pieces[k], (extra, chunk)), wide)
            wide = wide.astype(BF16)
            hit = jnp.broadcast_to(kz, (extra, chunk)).astype(BF16) == freq_e
            parts.append(jnp.where(hit, wide, jnp.zeros_like(wide)))
        where = jnp.broadcast_to(slot, (cols, chunk)).astype(BF16) == freq_s
        pick = jnp.where(where, jnp.ones((cols, chunk), BF16), jnp.zeros((cols, chunk), BF16))
        total = total + dot_t(jnp.concatenate(parts, axis=0), pick)
    line = total.astype(BF16)
    both = jnp.concatenate([line, line[: 2 * rows]] + ([line[4 * rows :]] if extra else []), axis=0)
    copies[2].wait()
    out_ref[...] = dot(table_ref[...], both)
    copy = pltpu.make_async_copy(out_ref, out_hbm, out_sem)
    copy.start()
    copy.wait()


def tables_kernel(
    cfg, col_hbm, yt_hbm, iy_hbm, ix_hbm, v_hbm, resid_hbm, tx_hbm, x_hbm, wide_hbm,
    e_ref, hot_ref, v_out_ref, hist_ref, tx_ref, x_ref, wide_ref,
    col_ref, yt_ref, iy_ref, ix_ref, v_ref, resid_ref, v_work, sems,
):
    ncol, rows, m, zs, xs, ng = (cfg[k] for k in ("ncol", "k_rows", "m", "zs", "xs", "ng"))
    block = v_ref.shape[0]
    band = lax.axis_index("band")
    first = lax.rem(band, cfg["gz"]) * zs
    base = pl.multiple_of(lax.div(first, block) * block, 8)
    offset = first - base
    lanes = pl.multiple_of(lax.div(band, cfg["gz"]) * (xs * ng), LANES)
    v_mine = v_hbm.at[pl.ds(base, block), pl.ds(lanes, xs * ng)]
    copies = fetch(
        (
            (col_hbm, col_ref), (yt_hbm, yt_ref), (v_mine, v_ref), (iy_hbm, iy_ref), (ix_hbm, ix_ref), (resid_hbm, resid_ref),
            (tx_hbm, tx_ref), (x_hbm, x_ref), (wide_hbm, wide_ref),
        ),
        sems,
    )
    copies[0].wait()
    col = col_ref[...].astype(F32)
    kx = jnp.floor((col + 0.5) * (1.0 / ng))
    ky = col - kx * ng
    freq = row_freq((rows, ncol), ng, cfg["k_radius"]).astype(F32)
    hot_ref[...] = jnp.where(jnp.broadcast_to(kx, (rows, ncol)) == freq, 1.0, 0.0).astype(BF16)
    hot = jnp.where(jnp.broadcast_to(ky, (rows, ncol)) == freq, 1.0, 0.0)
    hot = hot.T.astype(BF16)
    copies[1].wait()
    width = 4 * m
    e_ref[:ncol] = dot(hot, yt_ref[:, :width]).astype(BF16)
    e_ref[ncol:] = dot(hot, yt_ref[:, width:]).astype(BF16)
    copies[2].wait()
    for x in range(xs):
        v_work[pl.ds(x, block, stride=xs), :] = v_ref[:, x * ng : (x + 1) * ng]
    copies[3].wait()
    copies[4].wait()
    for z in range(zs):
        at = pl.multiple_of((offset + z) * xs, 8)
        along = dot3(v_work[pl.ds(at, xs), :], iy_ref[0], iy_ref[1])
        high, low = split(along)
        v_out_ref[z * m : (z + 1) * m, :] = (
            dot(ix_ref[0], high) + dot(ix_ref[1], high) + dot(ix_ref[0], low)
        )
    copies[5].wait()
    hist = resid_ref.shape[0]
    lane = lax.broadcasted_iota(jnp.int32, hist_ref.shape, 1)
    row = jnp.zeros(hist_ref.shape, F32)
    for i in range(hist):
        left = resid_ref[i]
        for j in range(i, hist):
            value = jnp.sum(left * resid_ref[j], axis=0, keepdims=True)
            value = jnp.sum(value, axis=1, keepdims=True)
            row = row + jnp.where(lane == i * (hist + 1) + j, value, 0.0)
    hist_ref[...] = row
    for copy in copies[6:]:
        copy.wait()


def turned(value, m):
    if 2 * m > LANES:
        return jnp.concatenate([-value[:, m:], value[:, :m]], axis=1)
    lane = lax.broadcasted_iota(jnp.int32, value.shape, 1)
    moved = pltpu.roll(value, m, 1)
    return jnp.where(lane < m, -moved, moved)


def planes_kernel(
    cfg, in_ref, hot_ref, e_ref, tx_ref, ix_ref, v_ref, hist_ref, out_ref, row_ref, piece_ref
):
    ncol, rows, m, zs, cols = cfg["ncol"], cfg["k_rows"], cfg["m"], cfg["zs"], cfg["cols"]
    npw, bands, per = cfg["npw"], cfg["bands"], cfg["chunk_bands"]
    value = in_ref[...]
    high = value.astype(BF16).astype(F32)
    count = value.shape[0]
    piece_ref[0, :count] = high
    piece_ref[1, :count] = value - high
    hits = [hot_ref[:, p * cols : (p + 1) * cols] > 0 for p in range(npw)]
    none = jnp.zeros((rows, cols), BF16)
    lane = lax.broadcasted_iota(jnp.int32, row_ref.shape, 1)

    def left(part, first):
        lanes = []
        for comp in range(2):
            for p in range(npw):
                column = []
                for b in range(per):
                    for z in range(zs):
                        block = (first + b) * npw + p
                        if cfg["source"]:
                            block = cfg["source"][block]
                        at = block * 2 * zs + comp * zs + z
                        line = piece_ref[part, pl.ds(at, 8, stride=0), :]
                        line = jnp.concatenate([line, line], axis=0).astype(BF16)
                        column.append(jnp.where(hits[p], jnp.concatenate([line] * (rows // 16), axis=0), none))
                lanes.append(jnp.concatenate(column, axis=0))
        return jnp.concatenate(lanes, axis=1)

    def step(first, carry):
        dens, energy = carry
        dens = list(dens)
        grid = dot(left(0, first), e_ref[...])
        grid = grid[:, : 2 * m] + grid[:, 2 * m :] + dot(left(1, first), e_ref[:, : 2 * m])
        grids = [part for value in (grid, turned(grid, m)) for part in split(value)]

        def stack(b, z):
            at = (b * zs + z) * rows
            parts = [grids[k][at : at + rows] for k in (0, 2, 1, 3, 0, 2)]
            return jnp.concatenate(parts, axis=0)

        group = 2 if zs % 2 == 0 else 1
        for b in range(per):
            acc = jnp.zeros((m, 2 * m), F32)
            for z in range(0, zs, group):
                both = jnp.concatenate([stack(b, z + k) for k in range(group)], axis=1)
                psi = dot(tx_ref[...], both)
                for k in range(group):
                    square = psi[:, k * 2 * m : (k + 1) * 2 * m]
                    square = square * square
                    dens[z + k] = dens[z + k] + square
                    acc = acc + square * v_ref[(z + k) * m : (z + k + 1) * m, :]
            part = jnp.sum(jnp.sum(acc, axis=0, keepdims=True), axis=1, keepdims=True)
            energy = energy + jnp.where(lane == cfg["row"] + first + b, part, 0.0)
        return tuple(dens), energy

    carry = (
        tuple(jnp.zeros((m, 2 * m), F32) for _ in range(zs)),
        hist_ref[...],
    )
    if cfg["source"]:
        for first in range(0, bands, per):
            carry = step(first, carry)
    else:
        carry = lax.fori_loop(0, bands // per, lambda i, c: step(i * per, c), carry)
    dens, energy = carry
    row_ref[...] = energy
    pk, xr, gz = cfg["pk"], cfg["xr"], cfg["gz"]
    merged = []
    for zp in range(zs // pk):
        folded = []
        for half in range(pk):
            value = dens[zp * pk + half]
            folded.append(value[:, :m] + value[:, m:])
        merged.append(jnp.concatenate(folded, axis=1) if pk > 1 else folded[0])
    high, low = split(jnp.concatenate(merged, axis=1))
    rows_x = dot(ix_ref[...], jnp.concatenate([high, high, low], axis=0))
    for zp in range(zs // pk):
        for g in range(gz):
            at = (cfg["dest"][g] * (zs // pk) + zp) * xr
            out_ref[at : at + xr, :] = rows_x[g * xr : (g + 1) * xr, zp * pk * m : (zp + 1) * pk * m]


def cells_kernel(cfg, in_ref, row_ref, iy_ref, rho_ref, resid_ref, dens_ref, send_ref, work):
    pk, xr, ng = cfg["pk"], cfg["xr"], cfg["ng"]
    count = in_ref.shape[0] // xr
    high, low = split(in_ref[...])
    cells = dot(jnp.concatenate([high, high, low], axis=1), iy_ref[...])
    each = count // cfg["gz"]
    for at in range(count):
        for half in range(pk):
            to = ((cfg["band_order"][at // each] * each + at % each) * pk + half) * xr
            work[to : to + xr, :] = cells[at * xr : (at + 1) * xr, half * ng : (half + 1) * ng]
    hist = resid_ref.shape[0]
    sums = [None] * (hist + 1)
    for x in range(xr):
        at = slice(x * ng, (x + 1) * ng)
        value = work[pl.ds(x, count * pk, stride=xr), :]
        dens_ref[:, at] = value
        last = value - rho_ref[:, at]
        for i in range(hist + 1):
            term = last * (resid_ref[i, :, at] if i < hist else last)
            sums[i] = term if x == 0 else sums[i] + term
    lane = lax.broadcasted_iota(jnp.int32, row_ref.shape, 1)
    row = row_ref[...]
    for i in range(hist + 1):
        value = jnp.sum(jnp.sum(sums[i], axis=0, keepdims=True), axis=1, keepdims=True)
        row = row + jnp.where(lane == i * (hist + 1) + hist, value, 0.0)
    send_ref[...] = jnp.broadcast_to(row, send_ref.shape)


def mix_kernel(
    cfg, in_ref, dens_ref, rho_ref, rho_hist_ref, resid_ref, occ_ref,
    dens_hbm, mixed_hbm, energy_hbm, norm_hbm, mixed_ref, energy_ref, norm_ref, sems,
):
    dens_copy = pltpu.make_async_copy(dens_ref, dens_hbm, sems.at[2])
    dens_copy.start()
    hist = resid_ref.shape[0]
    size = hist + 1
    row = jnp.sum(in_ref[...], axis=0, keepdims=True) * (1.0 / cfg["ng"] ** 3)
    lane = lax.broadcasted_iota(jnp.int32, row.shape, 1)

    def pick(at):
        return jnp.sum(jnp.where(lane == at, row, 0.0), axis=1, keepdims=True)

    gram = {(i, j): pick(i * size + j) for i in range(size) for j in range(i, size)}
    low = {}
    for j in range(size):
        value = gram[(j, j)]
        for k in range(j):
            value = value - low[(j, k)] * low[(j, k)]
        low[(j, j)] = jnp.sqrt(value)
        for i in range(j + 1, size):
            value = gram[(j, i)]
            for k in range(j):
                value = value - low[(i, k)] * low[(j, k)]
            low[(i, j)] = value / low[(j, j)]
    half = []
    for i in range(size):
        value = jnp.ones((1, 1), F32)
        for k in range(i):
            value = value - low[(i, k)] * half[k]
        half.append(value / low[(i, i)])
    solved = [None] * size
    for i in reversed(range(size)):
        value = half[i]
        for k in range(i + 1, size):
            value = value - low[(k, i)] * solved[k]
        solved[i] = value / low[(i, i)]
    total = solved[0]
    for value in solved[1:]:
        total = total + value
    coef = [value / total for value in solved]
    norm_ref[...] = jnp.sqrt(gram[(hist, hist)])
    weight = occ_ref[0].astype(F32) * (1.0 / cfg["bands"])
    energy_ref[...] = pick(cfg["row"] + lax.axis_index("band")) / jnp.full((1, 1), weight, F32)
    planes, width = mixed_ref.shape
    copies = fetch(((energy_ref, energy_hbm), (norm_ref, norm_hbm)), sems) + [dens_copy]
    step = 8
    for at in range(0, planes, step):
        rows = slice(at, at + step)
        for first in range(0, width, 4 * LANES):
            lanes = slice(first, min(first + 4 * LANES, width))
            rho = rho_ref[rows, lanes]
            mixed = coef[hist] * (rho + 0.8 * (dens_ref[rows, lanes] - rho))
            for i in range(hist):
                mixed = mixed + coef[i] * (rho_hist_ref[i, rows, lanes] + 0.8 * resid_ref[i, rows, lanes])
            mixed_ref[rows, lanes] = mixed
        copy = pltpu.make_async_copy(mixed_ref.at[rows, :], mixed_hbm.at[rows, :], sems.at[3 + at // step])
        copy.start()
        copies.append(copy)
    for copy in copies:
        copy.wait()


SPACES = {"u": pltpu.HBM, "v": pltpu.VMEM, "p": pltpu.VMEM, "s": pltpu.SMEM, "h": pltpu.HBM}


def call(kernel, cfg, outs, spaces, out_spaces, scratch, copies, name, limit):
    sems = [pltpu.SemaphoreType.DMA((copies,))] if copies else []
    run = pl.pallas_call(
        lambda *refs: kernel(cfg, *refs),
        out_shape=tuple(
            SPACES[space](out.shape, out.dtype) if space in "hp" else out
            for out, space in zip(outs, out_spaces, strict=True)
        ),
        in_specs=[pl.BlockSpec(memory_space=SPACES[space]) for space in spaces],
        out_specs=tuple(pl.BlockSpec(memory_space=SPACES[space]) for space in out_spaces),
        scratch_shapes=list(scratch) + sems,
        compiler_params=pltpu.CompilerParams(vmem_limit_bytes=limit),
        name=name,
    )

    def placed(*args):
        return run(*(
            pltpu.with_memory_space_constraint(arg, SPACES[space]) if space in "hp" else arg
            for arg, space in zip(args, spaces, strict=True)
        ))

    return placed


def held(*arrays):
    return [pltpu.VMEM(array.shape, array.dtype) for array in arrays]


def slice_x(table, axis, gx, gz, xs):
    if gx == 1:
        return table
    return lax.dynamic_slice_in_dim(table, lax.axis_index("band") // gz * xs, xs, axis)


def build(mesh):
    nband, npw = mesh.shape["band"], mesh.shape["pw"]
    both = ("band", "pw")

    def local(coefficients, pw_index, col_index, occupation, v_local, rho_in, rho_hist, resid_hist):
        bands_dev, _, count = coefficients.shape
        planes, cells = v_local.shape
        ng = planes * npw
        ncol = col_index.shape[0]
        cols = ncol // npw
        hist = resid_hist.shape[0]
        assert bands_dev == 1 and ng * ng == cells and ng == LANES
        bands = nband
        gz = math.gcd(planes, nband)
        gx = nband // gz
        zs, xs, xr = planes // gz, ng // gx, ng // nband
        kz_radius = line_radius(ng, cols, count)
        k_radius = plane_radius(ng, ncol)
        m = ng
        while m % 2 == 0 and m // 2 > 4 * k_radius and zs % (2 * ng // m) == 0:
            m //= 2
        pk = ng // m
        kz_vals, _ = box(ng, kz_radius, 16)
        kz_rows, kz_rest, kz_extra = kz_split(len(kz_vals))
        k_vals, k_rows = box(ng, k_radius, 16)
        if k_rows % 32:
            k_rows = up(k_rows, 32)
        chunk_bands = bands
        while chunk_bands % 2 == 0 and chunk_bands * zs * k_rows > 1024:
            chunk_bands //= 2
        cfg = dict(
            ng=ng, ncol=ncol, cols=cols, bands=bands, npw=npw, gz=gz, zs=zs, xs=xs, xr=xr, m=m, pk=pk,
            kz_radius=kz_radius, k_radius=k_radius, kz_real=len(kz_vals), k_rows=k_rows, chunk_bands=chunk_bands,
            row=(hist + 1) ** 2,
        )
        unrolled = bands // chunk_bands <= 2
        all_order = snake(nband, npw) if unrolled else list(range(nband * npw))
        band_order = shuffled(gz)
        cfg.update(source=inverse(all_order) if unrolled else None, dest=inverse(band_order), band_order=band_order)
        turn = 2.0 * math.pi / ng
        z_of = (
            np.arange(npw)[None, :, None] * planes
            + (np.arange(nband) % gz)[:, None, None] * zs
            + np.arange(zs)[None, None, :]
        )
        angle = turn * (z_of[..., None] * kz_vals % ng)
        cz, sz = np.cos(angle), np.sin(angle)
        z_table = np.stack([np.stack([cz, -sz], -2), np.stack([sz, cz], -2)], axis=2)
        z_table = z_table.reshape((nband * npw,) + z_table.shape[2:])[all_order]
        z_high, z_low = split_np(z_table.reshape(-1, 2, len(kz_vals)))
        flat = lambda table: table.reshape(table.shape[0], -1)
        main = [flat(table[:, :, :kz_rows]) for table in (z_high, z_low)]
        spare = [flat(table[:, :, kz_rows:]) for table in (z_high, z_low)]
        pad = [np.zeros((z_high.shape[0], kz_extra - 2 * k * kz_rest), z_high.dtype) for k in (2, 1)]
        z_table = jnp.asarray(np.concatenate(
            [main[0], main[0], spare[0], spare[0], pad[0], main[1], spare[1], pad[1]], axis=1
        ))
        angle = turn * pk * (k_vals[:, None] * np.arange(m)[None, :])
        cy, sy = np.zeros((2, k_rows, m))
        cy[: len(k_vals)], sy[: len(k_vals)] = np.cos(angle), np.sin(angle)
        real = split_np(np.concatenate([cy, sy], axis=1))
        imag = split_np(np.concatenate([-sy, cy], axis=1))
        y_table = jnp.asarray(np.concatenate([*real, *imag], axis=1))
        x_high, x_low = split_np(np.concatenate([cy.T, sy.T], axis=1))
        x_table = jnp.asarray(np.concatenate([x_high, x_high, x_low], axis=1))
        inter = interpolation(ng, m)
        iy_twice = jnp.asarray(np.stack(split_np(np.concatenate([inter, inter], axis=1))))
        wide = np.zeros((pk * m, pk * ng))
        for half in range(pk):
            wide[half * m : (half + 1) * m, half * ng : (half + 1) * ng] = inter.T
        w_high, w_low = split_np(wide)
        iy_wide = jnp.asarray(np.concatenate([w_high, w_low, w_high], axis=0))
        x_high, x_low = split_np(inter)
        ix_full = jnp.asarray(np.concatenate([x_high, x_low, x_high], axis=1))
        ixt_full = jnp.asarray(np.stack(split_np(inter.T)))

        index = pw_index.reshape(1, count)
        col = col_index.reshape(1, ncol)
        shape = jax.ShapeDtypeStruct
        width = up(cfg["row"] + bands, LANES)
        mib = 1024 * 1024

        sent_shape = shape((nband * npw * 2 * zs, cols), F32)
        (sent,) = call(
            columns_kernel, cfg, (sent_shape,), "shhh", "h",
            held(index, coefficients, z_table, sent_shape) + [pltpu.SemaphoreType.DMA((3,)), pltpu.SemaphoreType.DMA],
            0, "columns", 40 * mib,
        )(occupation, index, coefficients, z_table)
        everyone = [all_order] if unrolled else None
        received = lax.all_to_all(sent, both, 0, 0, axis_index_groups=everyone, tiled=True)
        block = max(zs, 8)
        assert planes % block == 0 and xs % 8 == 0
        v_block = shape((block, xs * ng), F32)
        ix = slice_x(ix_full, 0, gx, gz, xs)
        e_table, hot, v_grid, hist_row, tx, ix, iy = call(
            tables_kernel, cfg,
            (
                shape((2 * ncol, 4 * m), BF16), shape((k_rows, ncol), BF16), shape((zs * m, 2 * m), F32), shape((1, width), F32),
                x_table, ix, iy_wide,
            ),
            "h" * 9, "ppppppp",
            held(
                col, y_table, iy_twice, ixt_full[:, :, :xs], v_block, resid_hist,
                shape((block * xs, ng), F32),
            ),
            9, "tables", 40 * mib,
        )(col, y_table, iy_twice, slice_x(ixt_full, 2, gx, gz, xs), v_local, resid_hist, x_table, ix, iy_wide)
        to_cells, row = call(
            planes_kernel, cfg, (shape((gz * (zs // pk) * xr, pk * m), F32), shape((1, width), F32)),
            "vpppppp", "pp", held(shape((2, received.shape[0] + 8, cols), F32)), 0, "planes", 40 * mib,
        )(received, hot, e_table, tx, ix, v_grid, hist_row)
        groups = [[g * gz + k for k in band_order] for g in range(gx)]
        mine = lax.all_to_all(to_cells, "band", 0, 0, axis_index_groups=groups, tiled=True)
        dens, rows = call(
            cells_kernel, cfg, (shape(rho_in.shape, F32), shape((nband * npw, width), F32)),
            "vppvv", "pp", [pltpu.VMEM((mine.shape[0] * pk, ng), F32)], 0, "cells", 16 * mib,
        )(mine, row, iy, rho_in, resid_hist)
        rows = lax.all_to_all(rows, both, 0, 0, axis_index_groups=everyone, tiled=True)
        one = shape((1, 1), F32)
        density, mixed, energy, norm = call(
            mix_kernel, cfg, (shape(rho_in.shape, F32), shape(rho_in.shape, F32), one, one),
            "vpvvvs", "hhuu", held(rho_in, one, one), 3 + planes // 8, "mix", 16 * mib,
        )(rows, dens, rho_in, rho_hist, resid_hist, occupation)
        return density, mixed, energy.reshape(1), norm.reshape(())

    return local


def solution(mesh):
    in_specs = (
        P("band", None, "pw"),
        P("pw"),
        P(),
        P("band"),
        P("pw", None),
        P("pw", "band"),
        P(None, "pw", "band"),
        P(None, "pw", "band"),
    )
    out_specs = (P("pw", "band"), P("pw", "band"), P("band"), P())
    return jax.shard_map(build(mesh), mesh=mesh, in_specs=in_specs, out_specs=out_specs, check_vma=False)
```

```python
import math

import jax
import jax.numpy as jnp
import numpy as np
from jax import lax
from jax.experimental import pallas as pl
from jax.experimental.pallas import tpu as pltpu
from jax.sharding import PartitionSpec as P

F32 = jnp.float32
BF16 = jnp.bfloat16
LANES = 128


def up(value, multiple):
    return -(-value // multiple) * multiple


def split_np(table):
    high = table.astype(np.float32).astype(jnp.bfloat16)
    low = (table - high.astype(np.float64)).astype(np.float32).astype(jnp.bfloat16)
    return high, low


def split(value):
    high = value.astype(BF16)
    low = (value - high.astype(F32)).astype(BF16)
    return high, low


def dot(left, right):
    return jnp.dot(left, right, preferred_element_type=F32)


def dot_t(left, right):
    return lax.dot_general(left, right, (((1,), (1,)), ((), ())), preferred_element_type=F32)


def dot3(left, right_high, right_low):
    high, low = split(left)
    return dot(high, right_high) + dot(high, right_low) + dot(low, right_high)


def signed(length):
    index = np.arange(length)
    return np.where(index > length // 2, index - length, index)


def plane_radius(length, count):
    freq = signed(length)
    norm = np.sort((freq[:, None] ** 2 + freq[None, :] ** 2).reshape(-1))
    return max(1, math.isqrt(int(norm[count - 1])))


def line_radius(length, columns, count):
    norm = np.sort(np.repeat(np.abs(signed(length)), columns))
    return max(1, int(norm[count - 1]))


def box(length, radius, multiple):
    real = min(length, 2 * radius + 1)
    rows = up(real, multiple)
    return (np.arange(real) - radius) % length, rows


def row_freq(shape, length, radius):
    row = lax.broadcasted_iota(jnp.int32, shape, 0)
    real = min(length, 2 * radius + 1)
    freq = jnp.where(row < radius, row - radius + length, row - radius)
    return jnp.where(row < real, freq, -1)


def interpolation(length, samples):
    if samples == length:
        return np.eye(length)
    shift = np.arange(length)[:, None] - np.arange(samples)[None, :] * (length // samples)
    total = np.cos(math.pi * samples * shift / length)
    for k in range(samples // 2):
        total = total + (2.0 if k else 1.0) * np.cos(2.0 * math.pi * k * shift / length)
    return total / samples


def kz_split(real):
    rows = real // 16 * 16
    return rows, real - rows, up(4 * (real - rows), 16)


def pair_snake(size):
    pairs = size // 2
    members = []
    for i in range(pairs):
        k = (i + 1) % pairs
        members += [2 * k + 1, 2 * k] if i % 2 else [2 * k, 2 * k + 1]
    return members + list(range(2 * pairs, size))


def inverse(members):
    return [members.index(k) for k in range(len(members))]


def fetch(pairs, sems):
    copies = [pltpu.make_async_copy(src, dst, sems.at[i]) for i, (src, dst) in enumerate(pairs)]
    for copy in copies:
        copy.start()
    return copies


def columns_kernel(
    cfg, occ_ref, index_hbm, coef_hbm, table_hbm, out_hbm, index_ref, coef_ref, table_ref, out_ref, sems, out_sem
):
    copies = fetch(((index_hbm, index_ref), (coef_hbm, coef_ref), (table_hbm, table_ref)), sems)
    real, cols, ng, radius = cfg["kz_real"], cfg["cols"], cfg["ng"], cfg["kz_radius"]
    rows, rest, extra = kz_split(real)
    count = index_ref.shape[1]
    chunk = math.gcd(count, 1024)
    row = lax.broadcasted_iota(jnp.int32, (rows, chunk), 0)
    freq_k = jnp.where(row < radius, row - radius + ng, row - radius).astype(F32).astype(BF16)
    if extra:
        row = lax.broadcasted_iota(jnp.int32, (extra, chunk), 0)
        freq_e = jnp.where(row < 4 * rest, lax.rem(row, rest) + (rows - radius), -1).astype(F32).astype(BF16)
    freq_s = lax.broadcasted_iota(jnp.int32, (cols, chunk), 0).astype(F32).astype(BF16)
    weight = occ_ref[0].astype(F32) * (1.0 / cfg["bands"])
    scale = jnp.sqrt(jnp.full((1, chunk), weight, F32))
    total = jnp.zeros((4 * rows + extra, cols), F32)
    for copy in copies[:2]:
        copy.wait()
    for at in range(0, count, chunk):
        index = index_ref[:, at : at + chunk].astype(F32)
        kz = jnp.floor((index + 0.5) * (1.0 / cols))
        slot = index - kz * cols
        pieces = [None] * 4
        for comp in range(2):
            value = coef_ref[0, comp : comp + 1, at : at + chunk] * scale
            high = value.astype(BF16).astype(F32)
            pieces[comp], pieces[2 + comp] = high, value - high
        hit = jnp.broadcast_to(kz, (rows, chunk)).astype(BF16) == freq_k
        parts = []
        for piece in pieces:
            wide = jnp.broadcast_to(piece, (rows, chunk)).astype(BF16)
            parts.append(jnp.where(hit, wide, jnp.zeros_like(wide)))
        if extra:
            wide = jnp.broadcast_to(pieces[3], (extra, chunk))
            for k in (2, 1, 0):
                wide = jnp.where(row < (k + 1) * rest, jnp.broadcast_to(pieces[k], (extra, chunk)), wide)
            wide = wide.astype(BF16)
            hit = jnp.broadcast_to(kz, (extra, chunk)).astype(BF16) == freq_e
            parts.append(jnp.where(hit, wide, jnp.zeros_like(wide)))
        where = jnp.broadcast_to(slot, (cols, chunk)).astype(BF16) == freq_s
        pick = jnp.where(where, jnp.ones((cols, chunk), BF16), jnp.zeros((cols, chunk), BF16))
        total = total + dot_t(jnp.concatenate(parts, axis=0), pick)
    line = total.astype(BF16)
    both = jnp.concatenate([line, line[: 2 * rows]] + ([line[4 * rows :]] if extra else []), axis=0)
    copies[2].wait()
    out_ref[...] = dot(table_ref[...], both)
    copy = pltpu.make_async_copy(out_ref, out_hbm, out_sem)
    copy.start()
    copy.wait()


def tables_kernel(
    cfg, col_hbm, yt_hbm, iy_hbm, ix_hbm, v_hbm, resid_hbm, tx_hbm, x_hbm, wide_hbm,
    e_ref, hot_ref, v_out_ref, hist_ref, tx_ref, x_ref, wide_ref,
    col_ref, yt_ref, iy_ref, ix_ref, v_ref, resid_ref, v_work, sems,
):
    ncol, rows, m, zs, xs, ng = (cfg[k] for k in ("ncol", "k_rows", "m", "zs", "xs", "ng"))
    block = v_ref.shape[0]
    band = lax.axis_index("band")
    first = lax.rem(band, cfg["gz"]) * zs
    base = pl.multiple_of(lax.div(first, block) * block, 8)
    offset = first - base
    lanes = pl.multiple_of(lax.div(band, cfg["gz"]) * (xs * ng), LANES)
    v_mine = v_hbm.at[pl.ds(base, block), pl.ds(lanes, xs * ng)]
    copies = fetch(
        (
            (col_hbm, col_ref), (yt_hbm, yt_ref), (v_mine, v_ref), (iy_hbm, iy_ref), (ix_hbm, ix_ref), (resid_hbm, resid_ref),
            (tx_hbm, tx_ref), (x_hbm, x_ref), (wide_hbm, wide_ref),
        ),
        sems,
    )
    copies[0].wait()
    col = col_ref[...].astype(F32)
    kx = jnp.floor((col + 0.5) * (1.0 / ng))
    ky = col - kx * ng
    freq = row_freq((rows, ncol), ng, cfg["k_radius"]).astype(F32)
    hot_ref[...] = jnp.where(jnp.broadcast_to(kx, (rows, ncol)) == freq, 1.0, 0.0).astype(BF16)
    hot = jnp.where(jnp.broadcast_to(ky, (rows, ncol)) == freq, 1.0, 0.0)
    hot = hot.T.astype(BF16)
    copies[1].wait()
    width = 4 * m
    e_ref[:ncol] = dot(hot, yt_ref[:, :width]).astype(BF16)
    e_ref[ncol:] = dot(hot, yt_ref[:, width:]).astype(BF16)
    copies[2].wait()
    for x in range(xs):
        v_work[pl.ds(x, block, stride=xs), :] = v_ref[:, x * ng : (x + 1) * ng]
    copies[3].wait()
    copies[4].wait()
    for z in range(zs):
        at = pl.multiple_of((offset + z) * xs, 8)
        along = dot3(v_work[pl.ds(at, xs), :], iy_ref[0], iy_ref[1])
        high, low = split(along)
        v_out_ref[z * m : (z + 1) * m, :] = (
            dot(ix_ref[0], high) + dot(ix_ref[1], high) + dot(ix_ref[0], low)
        )
    copies[5].wait()
    hist = resid_ref.shape[0]
    lane = lax.broadcasted_iota(jnp.int32, hist_ref.shape, 1)
    row = jnp.zeros(hist_ref.shape, F32)
    for i in range(hist):
        left = resid_ref[i]
        for j in range(i, hist):
            value = jnp.sum(left * resid_ref[j], axis=0, keepdims=True)
            value = jnp.sum(value, axis=1, keepdims=True)
            row = row + jnp.where(lane == i * (hist + 1) + j, value, 0.0)
    hist_ref[...] = row
    for copy in copies[6:]:
        copy.wait()


def turned(value, m):
    if 2 * m > LANES:
        return jnp.concatenate([-value[:, m:], value[:, :m]], axis=1)
    lane = lax.broadcasted_iota(jnp.int32, value.shape, 1)
    moved = pltpu.roll(value, m, 1)
    return jnp.where(lane < m, -moved, moved)


def planes_kernel(
    cfg, in_ref, hot_ref, e_ref, tx_ref, ix_ref, v_ref, hist_ref, out_ref, row_ref, piece_ref
):
    ncol, rows, m, zs, cols = cfg["ncol"], cfg["k_rows"], cfg["m"], cfg["zs"], cfg["cols"]
    npw, bands, per = cfg["npw"], cfg["bands"], cfg["chunk_bands"]
    value = in_ref[...]
    high = value.astype(BF16).astype(F32)
    count = value.shape[0]
    piece_ref[0, :count] = high
    piece_ref[1, :count] = value - high
    hits = [hot_ref[:, p * cols : (p + 1) * cols] > 0 for p in range(npw)]
    none = jnp.zeros((rows, cols), BF16)
    lane = lax.broadcasted_iota(jnp.int32, row_ref.shape, 1)

    def left(part, first):
        lanes = []
        for comp in range(2):
            for p in range(npw):
                column = []
                for b in range(per):
                    for z in range(zs):
                        at = ((first + b) * npw + p) * 2 * zs + comp * zs + z
                        line = piece_ref[part, pl.ds(at, 8, stride=0), :]
                        line = jnp.concatenate([line, line], axis=0).astype(BF16)
                        column.append(jnp.where(hits[p], jnp.concatenate([line] * (rows // 16), axis=0), none))
                lanes.append(jnp.concatenate(column, axis=0))
        return jnp.concatenate(lanes, axis=1)

    def step(first, carry):
        dens, energy = carry
        dens = list(dens)
        grid = dot(left(0, first), e_ref[...])
        grid = grid[:, : 2 * m] + grid[:, 2 * m :] + dot(left(1, first), e_ref[:, : 2 * m])
        grids = [part for value in (grid, turned(grid, m)) for part in split(value)]

        def stack(b, z):
            at = (b * zs + z) * rows
            parts = [grids[k][at : at + rows] for k in (0, 2, 1, 3, 0, 2)]
            return jnp.concatenate(parts, axis=0)

        group = 2 if zs % 2 == 0 else 1
        for b in range(per):
            acc = jnp.zeros((m, 2 * m), F32)
            for z in range(0, zs, group):
                both = jnp.concatenate([stack(b, z + k) for k in range(group)], axis=1)
                psi = dot(tx_ref[...], both)
                for k in range(group):
                    square = psi[:, k * 2 * m : (k + 1) * 2 * m]
                    square = square * square
                    dens[z + k] = dens[z + k] + square
                    acc = acc + square * v_ref[(z + k) * m : (z + k + 1) * m, :]
            part = jnp.sum(jnp.sum(acc, axis=0, keepdims=True), axis=1, keepdims=True)
            energy = energy + jnp.where(lane == cfg["row"] + first + b, part, 0.0)
        return tuple(dens), energy

    carry = (
        tuple(jnp.zeros((m, 2 * m), F32) for _ in range(zs)),
        hist_ref[...],
    )
    if bands // per <= 2:
        for first in range(0, bands, per):
            carry = step(first, carry)
    else:
        carry = lax.fori_loop(0, bands // per, lambda i, c: step(i * per, c), carry)
    dens, energy = carry
    row_ref[...] = energy
    pk, xr, gz = cfg["pk"], cfg["xr"], cfg["gz"]
    merged = []
    for zp in range(zs // pk):
        folded = []
        for half in range(pk):
            value = dens[zp * pk + half]
            folded.append(value[:, :m] + value[:, m:])
        merged.append(jnp.concatenate(folded, axis=1) if pk > 1 else folded[0])
    high, low = split(jnp.concatenate(merged, axis=1))
    rows_x = dot(ix_ref[...], jnp.concatenate([high, high, low], axis=0))
    for zp in range(zs // pk):
        for g in range(gz):
            at = (cfg["dest"][g] * (zs // pk) + zp) * xr
            out_ref[at : at + xr, :] = rows_x[g * xr : (g + 1) * xr, zp * pk * m : (zp + 1) * pk * m]


def cells_kernel(cfg, in_ref, row_ref, iy_ref, rho_ref, resid_ref, dens_ref, send_ref, work):
    pk, xr, ng = cfg["pk"], cfg["xr"], cfg["ng"]
    count = in_ref.shape[0] // xr
    high, low = split(in_ref[...])
    cells = dot(jnp.concatenate([high, high, low], axis=1), iy_ref[...])
    each = count // cfg["gz"]
    for at in range(count):
        for half in range(pk):
            to = ((cfg["band_order"][at // each] * each + at % each) * pk + half) * xr
            work[to : to + xr, :] = cells[at * xr : (at + 1) * xr, half * ng : (half + 1) * ng]
    hist = resid_ref.shape[0]
    sums = [None] * (hist + 1)
    for x in range(xr):
        at = slice(x * ng, (x + 1) * ng)
        value = work[pl.ds(x, count * pk, stride=xr), :]
        dens_ref[:, at] = value
        last = value - rho_ref[:, at]
        for i in range(hist + 1):
            term = last * (resid_ref[i, :, at] if i < hist else last)
            sums[i] = term if x == 0 else sums[i] + term
    lane = lax.broadcasted_iota(jnp.int32, row_ref.shape, 1)
    row = row_ref[...]
    for i in range(hist + 1):
        value = jnp.sum(jnp.sum(sums[i], axis=0, keepdims=True), axis=1, keepdims=True)
        row = row + jnp.where(lane == i * (hist + 1) + hist, value, 0.0)
    send_ref[...] = jnp.broadcast_to(row, send_ref.shape)


def mix_kernel(
    cfg, in_ref, dens_ref, rho_ref, rho_hist_ref, resid_ref, occ_ref,
    dens_hbm, mixed_hbm, energy_hbm, norm_hbm, mixed_ref, energy_ref, norm_ref, sems,
):
    dens_copy = pltpu.make_async_copy(dens_ref, dens_hbm, sems.at[2])
    dens_copy.start()
    hist = resid_ref.shape[0]
    size = hist + 1
    row = jnp.sum(in_ref[...], axis=0, keepdims=True) * (1.0 / cfg["ng"] ** 3)
    lane = lax.broadcasted_iota(jnp.int32, row.shape, 1)

    def pick(at):
        return jnp.sum(jnp.where(lane == at, row, 0.0), axis=1, keepdims=True)

    gram = {(i, j): pick(i * size + j) for i in range(size) for j in range(i, size)}
    low = {}
    for j in range(size):
        value = gram[(j, j)]
        for k in range(j):
            value = value - low[(j, k)] * low[(j, k)]
        low[(j, j)] = jnp.sqrt(value)
        for i in range(j + 1, size):
            value = gram[(j, i)]
            for k in range(j):
                value = value - low[(i, k)] * low[(j, k)]
            low[(i, j)] = value / low[(j, j)]
    half = []
    for i in range(size):
        value = jnp.ones((1, 1), F32)
        for k in range(i):
            value = value - low[(i, k)] * half[k]
        half.append(value / low[(i, i)])
    solved = [None] * size
    for i in reversed(range(size)):
        value = half[i]
        for k in range(i + 1, size):
            value = value - low[(k, i)] * solved[k]
        solved[i] = value / low[(i, i)]
    total = solved[0]
    for value in solved[1:]:
        total = total + value
    coef = [value / total for value in solved]
    norm_ref[...] = jnp.sqrt(gram[(hist, hist)])
    weight = occ_ref[0].astype(F32) * (1.0 / cfg["bands"])
    energy_ref[...] = pick(cfg["row"] + lax.axis_index("band")) / jnp.full((1, 1), weight, F32)
    planes, width = mixed_ref.shape
    copies = fetch(((energy_ref, energy_hbm), (norm_ref, norm_hbm)), sems) + [dens_copy]
    step = 8
    for at in range(0, planes, step):
        rows = slice(at, at + step)
        for first in range(0, width, 4 * LANES):
            lanes = slice(first, min(first + 4 * LANES, width))
            rho = rho_ref[rows, lanes]
            mixed = coef[hist] * (rho + 0.8 * (dens_ref[rows, lanes] - rho))
            for i in range(hist):
                mixed = mixed + coef[i] * (rho_hist_ref[i, rows, lanes] + 0.8 * resid_ref[i, rows, lanes])
            mixed_ref[rows, lanes] = mixed
        copy = pltpu.make_async_copy(mixed_ref.at[rows, :], mixed_hbm.at[rows, :], sems.at[3 + at // step])
        copy.start()
        copies.append(copy)
    for copy in copies:
        copy.wait()


SPACES = {"u": pltpu.HBM, "v": pltpu.VMEM, "p": pltpu.VMEM, "s": pltpu.SMEM, "h": pltpu.HBM}


def call(kernel, cfg, outs, spaces, out_spaces, scratch, copies, name, limit):
    sems = [pltpu.SemaphoreType.DMA((copies,))] if copies else []
    run = pl.pallas_call(
        lambda *refs: kernel(cfg, *refs),
        out_shape=tuple(
            SPACES[space](out.shape, out.dtype) if space in "hp" else out
            for out, space in zip(outs, out_spaces, strict=True)
        ),
        in_specs=[pl.BlockSpec(memory_space=SPACES[space]) for space in spaces],
        out_specs=tuple(pl.BlockSpec(memory_space=SPACES[space]) for space in out_spaces),
        scratch_shapes=list(scratch) + sems,
        compiler_params=pltpu.CompilerParams(vmem_limit_bytes=limit),
        name=name,
    )

    def placed(*args):
        return run(*(
            pltpu.with_memory_space_constraint(arg, SPACES[space]) if space in "hp" else arg
            for arg, space in zip(args, spaces, strict=True)
        ))

    return placed


def held(*arrays):
    return [pltpu.VMEM(array.shape, array.dtype) for array in arrays]


def slice_x(table, axis, gx, gz, xs):
    if gx == 1:
        return table
    return lax.dynamic_slice_in_dim(table, lax.axis_index("band") // gz * xs, xs, axis)


def build(mesh):
    nband, npw = mesh.shape["band"], mesh.shape["pw"]
    both = ("band", "pw")

    def local(coefficients, pw_index, col_index, occupation, v_local, rho_in, rho_hist, resid_hist):
        bands_dev, _, count = coefficients.shape
        planes, cells = v_local.shape
        ng = planes * npw
        ncol = col_index.shape[0]
        cols = ncol // npw
        hist = resid_hist.shape[0]
        assert bands_dev == 1 and ng * ng == cells and ng == LANES
        bands = nband
        gz = math.gcd(planes, nband)
        gx = nband // gz
        zs, xs, xr = planes // gz, ng // gx, ng // nband
        kz_radius = line_radius(ng, cols, count)
        k_radius = plane_radius(ng, ncol)
        m = ng
        while m % 2 == 0 and m // 2 > 4 * k_radius and zs % (2 * ng // m) == 0:
            m //= 2
        pk = ng // m
        kz_vals, _ = box(ng, kz_radius, 16)
        kz_rows, kz_rest, kz_extra = kz_split(len(kz_vals))
        k_vals, k_rows = box(ng, k_radius, 16)
        if k_rows % 32:
            k_rows = up(k_rows, 32)
        chunk_bands = bands
        while chunk_bands % 2 == 0 and chunk_bands * zs * k_rows > 1024:
            chunk_bands //= 2
        cfg = dict(
            ng=ng, ncol=ncol, cols=cols, bands=bands, npw=npw, gz=gz, zs=zs, xs=xs, xr=xr, m=m, pk=pk,
            kz_radius=kz_radius, k_radius=k_radius, kz_real=len(kz_vals), k_rows=k_rows, chunk_bands=chunk_bands,
            row=(hist + 1) ** 2,
        )
        band_order = pair_snake(gz)
        cfg.update(dest=inverse(band_order), band_order=band_order)
        turn = 2.0 * math.pi / ng
        z_of = (
            np.arange(npw)[None, :, None] * planes
            + (np.arange(nband) % gz)[:, None, None] * zs
            + np.arange(zs)[None, None, :]
        )
        angle = turn * (z_of[..., None] * kz_vals % ng)
        cz, sz = np.cos(angle), np.sin(angle)
        z_table = np.stack([np.stack([cz, -sz], -2), np.stack([sz, cz], -2)], axis=2)
        z_high, z_low = split_np(z_table.reshape(-1, 2, len(kz_vals)))
        flat = lambda table: table.reshape(table.shape[0], -1)
        main = [flat(table[:, :, :kz_rows]) for table in (z_high, z_low)]
        spare = [flat(table[:, :, kz_rows:]) for table in (z_high, z_low)]
        pad = [np.zeros((z_high.shape[0], kz_extra - 2 * k * kz_rest), z_high.dtype) for k in (2, 1)]
        z_table = jnp.asarray(np.concatenate(
            [main[0], main[0], spare[0], spare[0], pad[0], main[1], spare[1], pad[1]], axis=1
        ))
        angle = turn * pk * (k_vals[:, None] * np.arange(m)[None, :])
        cy, sy = np.zeros((2, k_rows, m))
        cy[: len(k_vals)], sy[: len(k_vals)] = np.cos(angle), np.sin(angle)
        real = split_np(np.concatenate([cy, sy], axis=1))
        imag = split_np(np.concatenate([-sy, cy], axis=1))
        y_table = jnp.asarray(np.concatenate([*real, *imag], axis=1))
        x_high, x_low = split_np(np.concatenate([cy.T, sy.T], axis=1))
        x_table = jnp.asarray(np.concatenate([x_high, x_high, x_low], axis=1))
        inter = interpolation(ng, m)
        iy_twice = jnp.asarray(np.stack(split_np(np.concatenate([inter, inter], axis=1))))
        wide = np.zeros((pk * m, pk * ng))
        for half in range(pk):
            wide[half * m : (half + 1) * m, half * ng : (half + 1) * ng] = inter.T
        w_high, w_low = split_np(wide)
        iy_wide = jnp.asarray(np.concatenate([w_high, w_low, w_high], axis=0))
        x_high, x_low = split_np(inter)
        ix_full = jnp.asarray(np.concatenate([x_high, x_low, x_high], axis=1))
        ixt_full = jnp.asarray(np.stack(split_np(inter.T)))

        index = pw_index.reshape(1, count)
        col = col_index.reshape(1, ncol)
        shape = jax.ShapeDtypeStruct
        width = up(cfg["row"] + bands, LANES)
        mib = 1024 * 1024

        sent_shape = shape((nband * npw * 2 * zs, cols), F32)
        (sent,) = call(
            columns_kernel, cfg, (sent_shape,), "shhh", "h",
            held(index, coefficients, z_table, sent_shape) + [pltpu.SemaphoreType.DMA((3,)), pltpu.SemaphoreType.DMA],
            0, "columns", 40 * mib,
        )(occupation, index, coefficients, z_table)
        received = lax.all_to_all(sent, both, 0, 0, tiled=True)
        block = max(zs, 8)
        assert planes % block == 0 and xs % 8 == 0
        v_block = shape((block, xs * ng), F32)
        ix = slice_x(ix_full, 0, gx, gz, xs)
        e_table, hot, v_grid, hist_row, tx, ix, iy = call(
            tables_kernel, cfg,
            (
                shape((2 * ncol, 4 * m), BF16), shape((k_rows, ncol), BF16), shape((zs * m, 2 * m), F32), shape((1, width), F32),
                x_table, ix, iy_wide,
            ),
            "h" * 9, "ppppppp",
            held(
                col, y_table, iy_twice, ixt_full[:, :, :xs], v_block, resid_hist,
                shape((block * xs, ng), F32),
            ),
            9, "tables", 40 * mib,
        )(col, y_table, iy_twice, slice_x(ixt_full, 2, gx, gz, xs), v_local, resid_hist, x_table, ix, iy_wide)
        to_cells, row = call(
            planes_kernel, cfg, (shape((gz * (zs // pk) * xr, pk * m), F32), shape((1, width), F32)),
            "vpppppp", "pp", held(shape((2, received.shape[0] + 8, cols), F32)), 0, "planes", 40 * mib,
        )(received, hot, e_table, tx, ix, v_grid, hist_row)
        groups = [[g * gz + k for k in band_order] for g in range(gx)]
        mine = lax.all_to_all(to_cells, "band", 0, 0, axis_index_groups=groups, tiled=True)
        dens, rows = call(
            cells_kernel, cfg, (shape(rho_in.shape, F32), shape((nband * npw, width), F32)),
            "vppvv", "pp", [pltpu.VMEM((mine.shape[0] * pk, ng), F32)], 0, "cells", 16 * mib,
        )(mine, row, iy, rho_in, resid_hist)
        rows = lax.all_to_all(rows, both, 0, 0, tiled=True)
        one = shape((1, 1), F32)
        density, mixed, energy, norm = call(
            mix_kernel, cfg, (shape(rho_in.shape, F32), shape(rho_in.shape, F32), one, one),
            "vpvvvs", "hhuu", held(rho_in, one, one), 3 + planes // 8, "mix", 16 * mib,
        )(rows, dens, rho_in, rho_hist, resid_hist, occupation)
        return density, mixed, energy.reshape(1), norm.reshape(())

    return local


def solution(mesh):
    in_specs = (
        P("band", None, "pw"),
        P("pw"),
        P(),
        P("band"),
        P("pw", None),
        P("pw", "band"),
        P(None, "pw", "band"),
        P(None, "pw", "band"),
    )
    out_specs = (P("pw", "band"), P("pw", "band"), P("band"), P())
    return jax.shard_map(build(mesh), mesh=mesh, in_specs=in_specs, out_specs=out_specs, check_vma=False)
```

```python
import math

import jax
import jax.numpy as jnp
import numpy as np
from jax import lax
from jax.experimental import pallas as pl
from jax.experimental.pallas import tpu as pltpu
from jax.sharding import PartitionSpec as P

F32 = jnp.float32
BF16 = jnp.bfloat16
LANES = 128


def up(value, multiple):
    return -(-value // multiple) * multiple


def split_np(table):
    high = table.astype(np.float32).astype(jnp.bfloat16)
    low = (table - high.astype(np.float64)).astype(np.float32).astype(jnp.bfloat16)
    return high, low


def split(value):
    high = value.astype(BF16)
    low = (value - high.astype(F32)).astype(BF16)
    return high, low


def dot(left, right):
    return jnp.dot(left, right, preferred_element_type=F32)


def dot_t(left, right):
    return lax.dot_general(left, right, (((1,), (1,)), ((), ())), preferred_element_type=F32)


def dot3(left, right_high, right_low):
    high, low = split(left)
    return dot(high, right_high) + dot(high, right_low) + dot(low, right_high)


def signed(length):
    index = np.arange(length)
    return np.where(index > length // 2, index - length, index)


def plane_radius(length, count):
    freq = signed(length)
    norm = np.sort((freq[:, None] ** 2 + freq[None, :] ** 2).reshape(-1))
    return max(1, math.isqrt(int(norm[count - 1])))


def line_radius(length, columns, count):
    norm = np.sort(np.repeat(np.abs(signed(length)), columns))
    return max(1, int(norm[count - 1]))


def box(length, radius, multiple):
    real = min(length, 2 * radius + 1)
    rows = up(real, multiple)
    return (np.arange(real) - radius) % length, rows


def row_freq(shape, length, radius):
    row = lax.broadcasted_iota(jnp.int32, shape, 0)
    real = min(length, 2 * radius + 1)
    freq = jnp.where(row < radius, row - radius + length, row - radius)
    return jnp.where(row < real, freq, -1)


def interpolation(length, samples):
    if samples == length:
        return np.eye(length)
    shift = np.arange(length)[:, None] - np.arange(samples)[None, :] * (length // samples)
    total = np.cos(math.pi * samples * shift / length)
    for k in range(samples // 2):
        total = total + (2.0 if k else 1.0) * np.cos(2.0 * math.pi * k * shift / length)
    return total / samples


def kz_split(real):
    rows = real // 16 * 16
    return rows, real - rows, up(4 * (real - rows), 16)


def pair_snake(size):
    pairs = size // 2
    members = []
    for i in range(pairs):
        k = (i + 1) % pairs
        members += [2 * k + 1, 2 * k] if i % 2 else [2 * k, 2 * k + 1]
    return members + list(range(2 * pairs, size))


def inverse(members):
    return [members.index(k) for k in range(len(members))]


def fetch(pairs, sems):
    copies = [pltpu.make_async_copy(src, dst, sems.at[i]) for i, (src, dst) in enumerate(pairs)]
    for copy in copies:
        copy.start()
    return copies


def columns_kernel(
    cfg, occ_ref, index_hbm, coef_hbm, table_hbm, out_hbm, index_ref, coef_ref, table_ref, out_ref, sems, out_sem
):
    count = index_ref.shape[1]
    chunk = math.gcd(count, 1024)
    pairs = []
    for part in (slice(0, chunk), slice(chunk, count)):
        pairs.append((index_hbm.at[:, part], index_ref.at[:, part]))
        pairs.append((coef_hbm.at[:, :, part], coef_ref.at[:, :, part]))
    copies = fetch((*pairs, (table_hbm, table_ref)), sems)
    real, cols, ng, radius = cfg["kz_real"], cfg["cols"], cfg["ng"], cfg["kz_radius"]
    rows, rest, extra = kz_split(real)
    row = lax.broadcasted_iota(jnp.int32, (rows, chunk), 0)
    freq_k = jnp.where(row < radius, row - radius + ng, row - radius).astype(F32).astype(BF16)
    if extra:
        row = lax.broadcasted_iota(jnp.int32, (extra, chunk), 0)
        freq_e = jnp.where(row < 4 * rest, lax.rem(row, rest) + (rows - radius), -1).astype(F32).astype(BF16)
    freq_s = lax.broadcasted_iota(jnp.int32, (cols, chunk), 0).astype(F32).astype(BF16)
    weight = occ_ref[0].astype(F32) * (1.0 / cfg["bands"])
    scale = jnp.sqrt(jnp.full((1, chunk), weight, F32))
    total = jnp.zeros((4 * rows + extra, cols), F32)
    for copy in copies[:2]:
        copy.wait()
    for at in range(0, count, chunk):
        if at == chunk:
            copies[2].wait()
            copies[3].wait()
        index = index_ref[:, at : at + chunk].astype(F32)
        kz = jnp.floor((index + 0.5) * (1.0 / cols))
        slot = index - kz * cols
        pieces = [None] * 4
        for comp in range(2):
            value = coef_ref[0, comp : comp + 1, at : at + chunk] * scale
            high = value.astype(BF16).astype(F32)
            pieces[comp], pieces[2 + comp] = high, value - high
        hit = jnp.broadcast_to(kz, (rows, chunk)).astype(BF16) == freq_k
        parts = []
        for piece in pieces:
            wide = jnp.broadcast_to(piece, (rows, chunk)).astype(BF16)
            parts.append(jnp.where(hit, wide, jnp.zeros_like(wide)))
        if extra:
            wide = jnp.broadcast_to(pieces[3], (extra, chunk))
            for k in (2, 1, 0):
                wide = jnp.where(row < (k + 1) * rest, jnp.broadcast_to(pieces[k], (extra, chunk)), wide)
            wide = wide.astype(BF16)
            hit = jnp.broadcast_to(kz, (extra, chunk)).astype(BF16) == freq_e
            parts.append(jnp.where(hit, wide, jnp.zeros_like(wide)))
        where = jnp.broadcast_to(slot, (cols, chunk)).astype(BF16) == freq_s
        pick = jnp.where(where, jnp.ones((cols, chunk), BF16), jnp.zeros((cols, chunk), BF16))
        total = total + dot_t(jnp.concatenate(parts, axis=0), pick)
    line = total.astype(BF16)
    both = jnp.concatenate([line, line[: 2 * rows]] + ([line[4 * rows :]] if extra else []), axis=0)
    copies[4].wait()
    out_ref[...] = dot(table_ref[...], both)
    copy = pltpu.make_async_copy(out_ref, out_hbm, out_sem)
    copy.start()
    copy.wait()


def tables_kernel(
    cfg, col_hbm, yt_hbm, iy_hbm, ix_hbm, v_hbm, resid_hbm, tx_hbm, x_hbm, wide_hbm,
    e_ref, hot_ref, v_out_ref, hist_ref, tx_ref, x_ref, wide_ref,
    col_ref, yt_ref, iy_ref, ix_ref, v_ref, resid_ref, v_work, sems,
):
    ncol, rows, m, zs, xs, ng = (cfg[k] for k in ("ncol", "k_rows", "m", "zs", "xs", "ng"))
    block = v_ref.shape[0]
    band = lax.axis_index("band")
    first = lax.rem(band, cfg["gz"]) * zs
    base = pl.multiple_of(lax.div(first, block) * block, 8)
    offset = first - base
    lanes = pl.multiple_of(lax.div(band, cfg["gz"]) * (xs * ng), LANES)
    v_mine = v_hbm.at[pl.ds(base, block), pl.ds(lanes, xs * ng)]
    copies = fetch(
        (
            (col_hbm, col_ref), (yt_hbm, yt_ref), (v_mine, v_ref), (iy_hbm, iy_ref), (ix_hbm, ix_ref), (resid_hbm, resid_ref),
            (tx_hbm, tx_ref), (x_hbm, x_ref), (wide_hbm, wide_ref),
        ),
        sems,
    )
    copies[0].wait()
    col = col_ref[...].astype(F32)
    kx = jnp.floor((col + 0.5) * (1.0 / ng))
    ky = col - kx * ng
    freq = row_freq((rows, ncol), ng, cfg["k_radius"]).astype(F32)
    hot_ref[...] = jnp.where(jnp.broadcast_to(kx, (rows, ncol)) == freq, 1.0, 0.0).astype(BF16)
    hot = jnp.where(jnp.broadcast_to(ky, (rows, ncol)) == freq, 1.0, 0.0)
    hot = hot.T.astype(BF16)
    copies[1].wait()
    width = 4 * m
    e_ref[:ncol] = dot(hot, yt_ref[:, :width]).astype(BF16)
    e_ref[ncol:] = dot(hot, yt_ref[:, width:]).astype(BF16)
    copies[2].wait()
    for x in range(xs):
        v_work[pl.ds(x, block, stride=xs), :] = v_ref[:, x * ng : (x + 1) * ng]
    copies[3].wait()
    copies[4].wait()
    for z in range(zs):
        at = pl.multiple_of((offset + z) * xs, 8)
        along = dot3(v_work[pl.ds(at, xs), :], iy_ref[0], iy_ref[1])
        high, low = split(along)
        v_out_ref[z * m : (z + 1) * m, :] = (
            dot(ix_ref[0], high) + dot(ix_ref[1], high) + dot(ix_ref[0], low)
        )
    copies[5].wait()
    hist = resid_ref.shape[0]
    lane = lax.broadcasted_iota(jnp.int32, hist_ref.shape, 1)
    row = jnp.zeros(hist_ref.shape, F32)
    for i in range(hist):
        left = resid_ref[i]
        for j in range(i, hist):
            value = jnp.sum(left * resid_ref[j], axis=0, keepdims=True)
            value = jnp.sum(value, axis=1, keepdims=True)
            row = row + jnp.where(lane == i * (hist + 1) + j, value, 0.0)
    hist_ref[...] = row
    for copy in copies[6:]:
        copy.wait()


def turned(value, m):
    if 2 * m > LANES:
        return jnp.concatenate([-value[:, m:], value[:, :m]], axis=1)
    lane = lax.broadcasted_iota(jnp.int32, value.shape, 1)
    moved = pltpu.roll(value, m, 1)
    return jnp.where(lane < m, -moved, moved)


def planes_kernel(
    cfg, in_ref, hot_ref, e_ref, tx_ref, ix_ref, v_ref, hist_ref, out_ref, row_ref, piece_ref
):
    ncol, rows, m, zs, cols = cfg["ncol"], cfg["k_rows"], cfg["m"], cfg["zs"], cfg["cols"]
    npw, bands, per = cfg["npw"], cfg["bands"], cfg["chunk_bands"]
    value = in_ref[...]
    high = value.astype(BF16).astype(F32)
    count = value.shape[0]
    piece_ref[0, :count] = high
    piece_ref[1, :count] = value - high
    hits = [hot_ref[:, p * cols : (p + 1) * cols] > 0 for p in range(npw)]
    none = jnp.zeros((rows, cols), BF16)
    lane = lax.broadcasted_iota(jnp.int32, row_ref.shape, 1)

    def left(part, first):
        lanes = []
        for comp in range(2):
            for p in range(npw):
                column = []
                for b in range(per):
                    for z in range(zs):
                        at = ((first + b) * npw + p) * 2 * zs + comp * zs + z
                        line = piece_ref[part, pl.ds(at, 8, stride=0), :]
                        line = jnp.concatenate([line, line], axis=0).astype(BF16)
                        column.append(jnp.where(hits[p], jnp.concatenate([line] * (rows // 16), axis=0), none))
                lanes.append(jnp.concatenate(column, axis=0))
        return jnp.concatenate(lanes, axis=1)

    def step(first, carry):
        dens, energy = carry
        dens = list(dens)
        grid = dot(left(0, first), e_ref[...])
        grid = grid[:, : 2 * m] + grid[:, 2 * m :] + dot(left(1, first), e_ref[:, : 2 * m])
        grids = [part for value in (grid, turned(grid, m)) for part in split(value)]

        def stack(b, z):
            at = (b * zs + z) * rows
            parts = [grids[k][at : at + rows] for k in (0, 2, 1, 3, 0, 2)]
            return jnp.concatenate(parts, axis=0)

        group = 2 if zs % 2 == 0 else 1
        for b in range(per):
            acc = jnp.zeros((m, 2 * m), F32)
            for z in range(0, zs, group):
                both = jnp.concatenate([stack(b, z + k) for k in range(group)], axis=1)
                psi = dot(tx_ref[...], both)
                for k in range(group):
                    square = psi[:, k * 2 * m : (k + 1) * 2 * m]
                    square = square * square
                    dens[z + k] = dens[z + k] + square
                    acc = acc + square * v_ref[(z + k) * m : (z + k + 1) * m, :]
            part = jnp.sum(jnp.sum(acc, axis=0, keepdims=True), axis=1, keepdims=True)
            energy = energy + jnp.where(lane == cfg["row"] + first + b, part, 0.0)
        return tuple(dens), energy

    carry = (
        tuple(jnp.zeros((m, 2 * m), F32) for _ in range(zs)),
        hist_ref[...],
    )
    if bands // per <= 2:
        for first in range(0, bands, per):
            carry = step(first, carry)
    else:
        carry = lax.fori_loop(0, bands // per, lambda i, c: step(i * per, c), carry)
    dens, energy = carry
    row_ref[...] = energy
    pk, xr, gz = cfg["pk"], cfg["xr"], cfg["gz"]
    merged = []
    for zp in range(zs // pk):
        if pk == 2 and 2 * m == LANES:
            low, high = dens[zp * pk], dens[zp * pk + 1]
            side = lax.broadcasted_iota(jnp.int32, low.shape, 1) < m
            merged.append(jnp.where(side, low, high) + pltpu.roll(jnp.where(side, high, low), m, 1))
            continue
        folded = []
        for half in range(pk):
            value = dens[zp * pk + half]
            folded.append(value[:, :m] + value[:, m:])
        merged.append(jnp.concatenate(folded, axis=1) if pk > 1 else folded[0])
    high, low = split(jnp.concatenate(merged, axis=1))
    rows_x = dot(ix_ref[...], jnp.concatenate([high, high, low], axis=0))
    for zp in range(zs // pk):
        for g in range(gz):
            at = (cfg["dest"][g] * (zs // pk) + zp) * xr
            out_ref[at : at + xr, :] = rows_x[g * xr : (g + 1) * xr, zp * pk * m : (zp + 1) * pk * m]


def cells_kernel(cfg, in_ref, row_ref, iy_ref, rho_ref, resid_ref, dens_ref, send_ref, work):
    pk, xr, ng = cfg["pk"], cfg["xr"], cfg["ng"]
    count = in_ref.shape[0] // xr
    high, low = split(in_ref[...])
    cells = dot(jnp.concatenate([high, high, low], axis=1), iy_ref[...])
    each = count // cfg["gz"]
    for at in range(count):
        for half in range(pk):
            to = ((cfg["band_order"][at // each] * each + at % each) * pk + half) * xr
            work[to : to + xr, :] = cells[at * xr : (at + 1) * xr, half * ng : (half + 1) * ng]
    hist = resid_ref.shape[0]
    sums = [None] * (hist + 1)
    for x in range(xr):
        at = slice(x * ng, (x + 1) * ng)
        value = work[pl.ds(x, count * pk, stride=xr), :]
        dens_ref[:, at] = value
        last = value - rho_ref[:, at]
        for i in range(hist + 1):
            term = last * (resid_ref[i, :, at] if i < hist else last)
            sums[i] = term if x == 0 else sums[i] + term
    lane = lax.broadcasted_iota(jnp.int32, row_ref.shape, 1)
    row = row_ref[...]
    for i in range(hist + 1):
        value = jnp.sum(jnp.sum(sums[i], axis=0, keepdims=True), axis=1, keepdims=True)
        row = row + jnp.where(lane == i * (hist + 1) + hist, value, 0.0)
    send_ref[...] = jnp.broadcast_to(row, send_ref.shape)


def mix_kernel(
    cfg, in_ref, dens_ref, rho_ref, rho_hist_ref, resid_ref, occ_ref,
    dens_hbm, mixed_hbm, energy_hbm, norm_hbm, mixed_ref, energy_ref, norm_ref, sems,
):
    dens_copy = pltpu.make_async_copy(dens_ref, dens_hbm, sems.at[2])
    dens_copy.start()
    hist = resid_ref.shape[0]
    size = hist + 1
    row = jnp.sum(in_ref[...], axis=0, keepdims=True) * (1.0 / cfg["ng"] ** 3)
    lane = lax.broadcasted_iota(jnp.int32, row.shape, 1)

    def pick(at):
        return jnp.sum(jnp.where(lane == at, row, 0.0), axis=1, keepdims=True)

    gram = {(i, j): pick(i * size + j) for i in range(size) for j in range(i, size)}
    low = {}
    for j in range(size):
        value = gram[(j, j)]
        for k in range(j):
            value = value - low[(j, k)] * low[(j, k)]
        low[(j, j)] = jnp.sqrt(value)
        for i in range(j + 1, size):
            value = gram[(j, i)]
            for k in range(j):
                value = value - low[(i, k)] * low[(j, k)]
            low[(i, j)] = value / low[(j, j)]
    half = []
    for i in range(size):
        value = jnp.ones((1, 1), F32)
        for k in range(i):
            value = value - low[(i, k)] * half[k]
        half.append(value / low[(i, i)])
    solved = [None] * size
    for i in reversed(range(size)):
        value = half[i]
        for k in range(i + 1, size):
            value = value - low[(k, i)] * solved[k]
        solved[i] = value / low[(i, i)]
    total = solved[0]
    for value in solved[1:]:
        total = total + value
    coef = [value / total for value in solved]
    norm_ref[...] = jnp.sqrt(gram[(hist, hist)])
    weight = occ_ref[0].astype(F32) * (1.0 / cfg["bands"])
    energy_ref[...] = pick(cfg["row"] + lax.axis_index("band")) / jnp.full((1, 1), weight, F32)
    planes, width = mixed_ref.shape
    copies = fetch(((energy_ref, energy_hbm), (norm_ref, norm_hbm)), sems) + [dens_copy]
    step = 8
    for at in range(0, planes, step):
        rows = slice(at, at + step)
        for first in range(0, width, 4 * LANES):
            lanes = slice(first, min(first + 4 * LANES, width))
            rho = rho_ref[rows, lanes]
            mixed = coef[hist] * (rho + 0.8 * (dens_ref[rows, lanes] - rho))
            for i in range(hist):
                mixed = mixed + coef[i] * (rho_hist_ref[i, rows, lanes] + 0.8 * resid_ref[i, rows, lanes])
            mixed_ref[rows, lanes] = mixed
        copy = pltpu.make_async_copy(mixed_ref.at[rows, :], mixed_hbm.at[rows, :], sems.at[3 + at // step])
        copy.start()
        copies.append(copy)
    for copy in copies:
        copy.wait()


SPACES = {"u": pltpu.HBM, "v": pltpu.VMEM, "p": pltpu.VMEM, "s": pltpu.SMEM, "h": pltpu.HBM}


def call(kernel, cfg, outs, spaces, out_spaces, scratch, copies, name, limit):
    sems = [pltpu.SemaphoreType.DMA((copies,))] if copies else []
    run = pl.pallas_call(
        lambda *refs: kernel(cfg, *refs),
        out_shape=tuple(
            SPACES[space](out.shape, out.dtype) if space in "hp" else out
            for out, space in zip(outs, out_spaces, strict=True)
        ),
        in_specs=[pl.BlockSpec(memory_space=SPACES[space]) for space in spaces],
        out_specs=tuple(pl.BlockSpec(memory_space=SPACES[space]) for space in out_spaces),
        scratch_shapes=list(scratch) + sems,
        compiler_params=pltpu.CompilerParams(vmem_limit_bytes=limit),
        name=name,
    )

    def placed(*args):
        return run(*(
            pltpu.with_memory_space_constraint(arg, SPACES[space]) if space in "hp" else arg
            for arg, space in zip(args, spaces, strict=True)
        ))

    return placed


def held(*arrays):
    return [pltpu.VMEM(array.shape, array.dtype) for array in arrays]


def slice_x(table, axis, gx, gz, xs):
    if gx == 1:
        return table
    return lax.dynamic_slice_in_dim(table, lax.axis_index("band") // gz * xs, xs, axis)


def build(mesh):
    nband, npw = mesh.shape["band"], mesh.shape["pw"]
    both = ("band", "pw")

    def local(coefficients, pw_index, col_index, occupation, v_local, rho_in, rho_hist, resid_hist):
        bands_dev, _, count = coefficients.shape
        planes, cells = v_local.shape
        ng = planes * npw
        ncol = col_index.shape[0]
        cols = ncol // npw
        hist = resid_hist.shape[0]
        assert bands_dev == 1 and ng * ng == cells and ng == LANES
        bands = nband
        gz = math.gcd(planes, nband)
        gx = nband // gz
        zs, xs, xr = planes // gz, ng // gx, ng // nband
        kz_radius = line_radius(ng, cols, count)
        k_radius = plane_radius(ng, ncol)
        m = ng
        while m % 2 == 0 and m // 2 > 4 * k_radius and zs % (2 * ng // m) == 0:
            m //= 2
        pk = ng // m
        kz_vals, _ = box(ng, kz_radius, 16)
        kz_rows, kz_rest, kz_extra = kz_split(len(kz_vals))
        k_vals, k_rows = box(ng, k_radius, 16)
        if k_rows % 32:
            k_rows = up(k_rows, 32)
        assert count > 1024 and count % 1024 == 0
        chunk_bands = bands
        while chunk_bands % 2 == 0 and chunk_bands * zs * k_rows > 1024:
            chunk_bands //= 2
        cfg = dict(
            ng=ng, ncol=ncol, cols=cols, bands=bands, npw=npw, gz=gz, zs=zs, xs=xs, xr=xr, m=m, pk=pk,
            kz_radius=kz_radius, k_radius=k_radius, kz_real=len(kz_vals), k_rows=k_rows, chunk_bands=chunk_bands,
            row=(hist + 1) ** 2,
        )
        band_order = pair_snake(gz)
        cfg.update(dest=inverse(band_order), band_order=band_order)
        turn = 2.0 * math.pi / ng
        z_of = (
            np.arange(npw)[None, :, None] * planes
            + (np.arange(nband) % gz)[:, None, None] * zs
            + np.arange(zs)[None, None, :]
        )
        angle = turn * (z_of[..., None] * kz_vals % ng)
        cz, sz = np.cos(angle), np.sin(angle)
        z_table = np.stack([np.stack([cz, -sz], -2), np.stack([sz, cz], -2)], axis=2)
        z_high, z_low = split_np(z_table.reshape(-1, 2, len(kz_vals)))
        flat = lambda table: table.reshape(table.shape[0], -1)
        main = [flat(table[:, :, :kz_rows]) for table in (z_high, z_low)]
        spare = [flat(table[:, :, kz_rows:]) for table in (z_high, z_low)]
        pad = [np.zeros((z_high.shape[0], kz_extra - 2 * k * kz_rest), z_high.dtype) for k in (2, 1)]
        z_table = jnp.asarray(np.concatenate(
            [main[0], main[0], spare[0], spare[0], pad[0], main[1], spare[1], pad[1]], axis=1
        ))
        angle = turn * pk * (k_vals[:, None] * np.arange(m)[None, :])
        cy, sy = np.zeros((2, k_rows, m))
        cy[: len(k_vals)], sy[: len(k_vals)] = np.cos(angle), np.sin(angle)
        real = split_np(np.concatenate([cy, sy], axis=1))
        imag = split_np(np.concatenate([-sy, cy], axis=1))
        y_table = jnp.asarray(np.concatenate([*real, *imag], axis=1))
        x_high, x_low = split_np(np.concatenate([cy.T, sy.T], axis=1))
        x_table = jnp.asarray(np.concatenate([x_high, x_high, x_low], axis=1))
        inter = interpolation(ng, m)
        iy_twice = jnp.asarray(np.stack(split_np(np.concatenate([inter, inter], axis=1))))
        wide = np.zeros((pk * m, pk * ng))
        for half in range(pk):
            wide[half * m : (half + 1) * m, half * ng : (half + 1) * ng] = inter.T
        w_high, w_low = split_np(wide)
        iy_wide = jnp.asarray(np.concatenate([w_high, w_low, w_high], axis=0))
        x_high, x_low = split_np(inter)
        ix_full = jnp.asarray(np.concatenate([x_high, x_low, x_high], axis=1))
        ixt_full = jnp.asarray(np.stack(split_np(inter.T)))

        index = pw_index.reshape(1, count)
        col = col_index.reshape(1, ncol)
        shape = jax.ShapeDtypeStruct
        width = up(cfg["row"] + bands, LANES)
        mib = 1024 * 1024

        sent_shape = shape((nband * npw * 2 * zs, cols), F32)
        (sent,) = call(
            columns_kernel, cfg, (sent_shape,), "shhh", "h",
            held(index, coefficients, z_table, sent_shape) + [pltpu.SemaphoreType.DMA((5,)), pltpu.SemaphoreType.DMA],
            0, "columns", 40 * mib,
        )(occupation, index, coefficients, z_table)
        received = lax.all_to_all(sent, both, 0, 0, tiled=True)
        block = max(zs, 8)
        assert planes % block == 0 and xs % 8 == 0
        v_block = shape((block, xs * ng), F32)
        ix = slice_x(ix_full, 0, gx, gz, xs)
        e_table, hot, v_grid, hist_row, tx, ix, iy = call(
            tables_kernel, cfg,
            (
                shape((2 * ncol, 4 * m), BF16), shape((k_rows, ncol), BF16), shape((zs * m, 2 * m), F32), shape((1, width), F32),
                x_table, ix, iy_wide,
            ),
            "h" * 9, "ppppppp",
            held(
                col, y_table, iy_twice, ixt_full[:, :, :xs], v_block, resid_hist,
                shape((block * xs, ng), F32),
            ),
            9, "tables", 40 * mib,
        )(col, y_table, iy_twice, slice_x(ixt_full, 2, gx, gz, xs), v_local, resid_hist, x_table, ix, iy_wide)
        to_cells, row = call(
            planes_kernel, cfg, (shape((gz * (zs // pk) * xr, pk * m), F32), shape((1, width), F32)),
            "vpppppp", "pp", held(shape((2, received.shape[0] + 8, cols), F32)), 0, "planes", 40 * mib,
        )(received, hot, e_table, tx, ix, v_grid, hist_row)
        groups = [[g * gz + k for k in band_order] for g in range(gx)]
        mine = lax.all_to_all(to_cells, "band", 0, 0, axis_index_groups=groups, tiled=True)
        dens, rows = call(
            cells_kernel, cfg, (shape(rho_in.shape, F32), shape((nband * npw, width), F32)),
            "vppvv", "pp", [pltpu.VMEM((mine.shape[0] * pk, ng), F32)], 0, "cells", 16 * mib,
        )(mine, row, iy, rho_in, resid_hist)
        rows = lax.all_to_all(rows, both, 0, 0, tiled=True)
        one = shape((1, 1), F32)
        density, mixed, energy, norm = call(
            mix_kernel, cfg, (shape(rho_in.shape, F32), shape(rho_in.shape, F32), one, one),
            "vpvvvs", "hhuu", held(rho_in, one, one), 3 + planes // 8, "mix", 16 * mib,
        )(rows, dens, rho_in, rho_hist, resid_hist, occupation)
        return density, mixed, energy.reshape(1), norm.reshape(())

    return local


def solution(mesh):
    in_specs = (
        P("band", None, "pw"),
        P("pw"),
        P(),
        P("band"),
        P("pw", None),
        P("pw", "band"),
        P(None, "pw", "band"),
        P(None, "pw", "band"),
    )
    out_specs = (P("pw", "band"), P("pw", "band"), P("band"), P())
    return jax.shard_map(build(mesh), mesh=mesh, in_specs=in_specs, out_specs=out_specs, check_vma=False)
```

```python
import math

import jax
import jax.numpy as jnp
import numpy as np
from jax import lax
from jax.experimental import pallas as pl
from jax.experimental.pallas import tpu as pltpu
from jax.sharding import PartitionSpec as P

F32 = jnp.float32
BF16 = jnp.bfloat16
LANES = 128


def up(value, multiple):
    return -(-value // multiple) * multiple


def split_np(table):
    high = table.astype(np.float32).astype(jnp.bfloat16)
    low = (table - high.astype(np.float64)).astype(np.float32).astype(jnp.bfloat16)
    return high, low


def split(value):
    high = value.astype(BF16)
    low = (value - high.astype(F32)).astype(BF16)
    return high, low


def dot(left, right):
    return jnp.dot(left, right, preferred_element_type=F32)


def dot_t(left, right):
    return lax.dot_general(left, right, (((1,), (1,)), ((), ())), preferred_element_type=F32)


def dot3(left, right_high, right_low):
    high, low = split(left)
    return dot(high, right_high) + dot(high, right_low) + dot(low, right_high)


def signed(length):
    index = np.arange(length)
    return np.where(index > length // 2, index - length, index)


def plane_radius(length, count):
    freq = signed(length)
    norm = np.sort((freq[:, None] ** 2 + freq[None, :] ** 2).reshape(-1))
    return max(1, math.isqrt(int(norm[count - 1])))


def line_radius(length, columns, count):
    norm = np.sort(np.repeat(np.abs(signed(length)), columns))
    return max(1, int(norm[count - 1]))


def box(length, radius, multiple):
    real = min(length, 2 * radius + 1)
    rows = up(real, multiple)
    return (np.arange(real) - radius) % length, rows


def row_freq(shape, length, radius):
    row = lax.broadcasted_iota(jnp.int32, shape, 0)
    real = min(length, 2 * radius + 1)
    freq = jnp.where(row < radius, row - radius + length, row - radius)
    return jnp.where(row < real, freq, -1)


def interpolation(length, samples):
    if samples == length:
        return np.eye(length)
    shift = np.arange(length)[:, None] - np.arange(samples)[None, :] * (length // samples)
    total = np.cos(math.pi * samples * shift / length)
    for k in range(samples // 2):
        total = total + (2.0 if k else 1.0) * np.cos(2.0 * math.pi * k * shift / length)
    return total / samples


def kz_split(real):
    rows = real // 16 * 16
    return rows, real - rows, up(4 * (real - rows), 16)


def turned_order(size):
    return [(k + size // 4) % size for k in range(size)]


def inverse(members):
    return [members.index(k) for k in range(len(members))]


def fetch(pairs, sems):
    copies = [pltpu.make_async_copy(src, dst, sems.at[i]) for i, (src, dst) in enumerate(pairs)]
    for copy in copies:
        copy.start()
    return copies


def columns_kernel(
    cfg, occ_ref, index_hbm, coef_hbm, table_hbm, out_hbm, index_ref, coef_ref, table_ref, out_ref, sems, out_sem
):
    count = index_ref.shape[1]
    chunk = math.gcd(count, 1024)
    pairs = []
    for part in (slice(0, chunk), slice(chunk, count)):
        pairs.append((index_hbm.at[:, part], index_ref.at[:, part]))
        pairs.append((coef_hbm.at[:, :, part], coef_ref.at[:, :, part]))
    copies = fetch((*pairs, (table_hbm, table_ref)), sems)
    real, cols, ng, radius = cfg["kz_real"], cfg["cols"], cfg["ng"], cfg["kz_radius"]
    rows, rest, extra = kz_split(real)
    row = lax.broadcasted_iota(jnp.int32, (rows, chunk), 0)
    freq_k = jnp.where(row < radius, row - radius + ng, row - radius).astype(F32).astype(BF16)
    if extra:
        row = lax.broadcasted_iota(jnp.int32, (extra, chunk), 0)
        freq_e = jnp.where(row < 4 * rest, lax.rem(row, rest) + (rows - radius), -1).astype(F32).astype(BF16)
    freq_s = lax.broadcasted_iota(jnp.int32, (cols, chunk), 0).astype(F32).astype(BF16)
    weight = occ_ref[0].astype(F32) * (1.0 / cfg["bands"])
    scale = jnp.sqrt(jnp.full((1, chunk), weight, F32))
    total = jnp.zeros((4 * rows + extra, cols), F32)
    for copy in copies[:2]:
        copy.wait()
    for at in range(0, count, chunk):
        if at == chunk:
            copies[2].wait()
            copies[3].wait()
        index = index_ref[:, at : at + chunk].astype(F32)
        kz = jnp.floor((index + 0.5) * (1.0 / cols))
        slot = index - kz * cols
        pieces = [None] * 4
        for comp in range(2):
            value = coef_ref[0, comp : comp + 1, at : at + chunk] * scale
            high = value.astype(BF16).astype(F32)
            pieces[comp], pieces[2 + comp] = high, value - high
        hit = jnp.broadcast_to(kz, (rows, chunk)).astype(BF16) == freq_k
        parts = []
        for piece in pieces:
            wide = jnp.broadcast_to(piece, (rows, chunk)).astype(BF16)
            parts.append(jnp.where(hit, wide, jnp.zeros_like(wide)))
        if extra:
            wide = jnp.broadcast_to(pieces[3], (extra, chunk))
            for k in (2, 1, 0):
                wide = jnp.where(row < (k + 1) * rest, jnp.broadcast_to(pieces[k], (extra, chunk)), wide)
            wide = wide.astype(BF16)
            hit = jnp.broadcast_to(kz, (extra, chunk)).astype(BF16) == freq_e
            parts.append(jnp.where(hit, wide, jnp.zeros_like(wide)))
        where = jnp.broadcast_to(slot, (cols, chunk)).astype(BF16) == freq_s
        pick = jnp.where(where, jnp.ones((cols, chunk), BF16), jnp.zeros((cols, chunk), BF16))
        total = total + dot_t(jnp.concatenate(parts, axis=0), pick)
    line = total.astype(BF16)
    both = jnp.concatenate([line, line[: 2 * rows]] + ([line[4 * rows :]] if extra else []), axis=0)
    copies[4].wait()
    out_ref[...] = dot(table_ref[...], both)
    copy = pltpu.make_async_copy(out_ref, out_hbm, out_sem)
    copy.start()
    copy.wait()


def tables_kernel(
    cfg, col_hbm, yt_hbm, iy_hbm, ix_hbm, v_hbm, resid_hbm, tx_hbm, x_hbm, wide_hbm,
    e_ref, hot_ref, v_out_ref, hist_ref, tx_ref, x_ref, wide_ref,
    col_ref, yt_ref, iy_ref, ix_ref, v_ref, resid_ref, v_work, sems,
):
    ncol, rows, m, zs, xs, ng = (cfg[k] for k in ("ncol", "k_rows", "m", "zs", "xs", "ng"))
    block = v_ref.shape[0]
    band = lax.axis_index("band")
    first = lax.rem(band, cfg["gz"]) * zs
    base = pl.multiple_of(lax.div(first, block) * block, 8)
    offset = first - base
    lanes = pl.multiple_of(lax.div(band, cfg["gz"]) * (xs * ng), LANES)
    v_mine = v_hbm.at[pl.ds(base, block), pl.ds(lanes, xs * ng)]
    copies = fetch(
        (
            (col_hbm, col_ref), (yt_hbm, yt_ref), (v_mine, v_ref), (iy_hbm, iy_ref), (ix_hbm, ix_ref), (resid_hbm, resid_ref),
            (tx_hbm, tx_ref), (x_hbm, x_ref), (wide_hbm, wide_ref),
        ),
        sems,
    )
    copies[0].wait()
    col = col_ref[...].astype(F32)
    kx = jnp.floor((col + 0.5) * (1.0 / ng))
    ky = col - kx * ng
    freq = row_freq((rows, ncol), ng, cfg["k_radius"]).astype(F32)
    hot_ref[...] = jnp.where(jnp.broadcast_to(kx, (rows, ncol)) == freq, 1.0, 0.0).astype(BF16)
    hot = jnp.where(jnp.broadcast_to(ky, (rows, ncol)) == freq, 1.0, 0.0)
    hot = hot.T.astype(BF16)
    copies[1].wait()
    width = 4 * m
    e_ref[:ncol] = dot(hot, yt_ref[:, :width]).astype(BF16)
    e_ref[ncol:] = dot(hot, yt_ref[:, width:]).astype(BF16)
    copies[2].wait()
    for x in range(xs):
        v_work[pl.ds(x, block, stride=xs), :] = v_ref[:, x * ng : (x + 1) * ng]
    copies[3].wait()
    copies[4].wait()
    for z in range(zs):
        at = pl.multiple_of((offset + z) * xs, 8)
        along = dot3(v_work[pl.ds(at, xs), :], iy_ref[0], iy_ref[1])
        high, low = split(along)
        v_out_ref[z * m : (z + 1) * m, :] = (
            dot(ix_ref[0], high) + dot(ix_ref[1], high) + dot(ix_ref[0], low)
        )
    copies[5].wait()
    hist = resid_ref.shape[0]
    lane = lax.broadcasted_iota(jnp.int32, hist_ref.shape, 1)
    row = jnp.zeros(hist_ref.shape, F32)
    for i in range(hist):
        left = resid_ref[i]
        for j in range(i, hist):
            value = jnp.sum(left * resid_ref[j], axis=0, keepdims=True)
            value = jnp.sum(value, axis=1, keepdims=True)
            row = row + jnp.where(lane == i * (hist + 1) + j, value, 0.0)
    hist_ref[...] = row
    for copy in copies[6:]:
        copy.wait()


def turned(value, m):
    if 2 * m > LANES:
        return jnp.concatenate([-value[:, m:], value[:, :m]], axis=1)
    lane = lax.broadcasted_iota(jnp.int32, value.shape, 1)
    moved = pltpu.roll(value, m, 1)
    return jnp.where(lane < m, -moved, moved)


def planes_kernel(
    cfg, in_ref, hot_ref, e_ref, tx_ref, ix_ref, v_ref, hist_ref, out_ref, row_ref, piece_ref
):
    ncol, rows, m, zs, cols = cfg["ncol"], cfg["k_rows"], cfg["m"], cfg["zs"], cfg["cols"]
    npw, bands, per = cfg["npw"], cfg["bands"], cfg["chunk_bands"]
    value = in_ref[...]
    high = value.astype(BF16).astype(F32)
    count = value.shape[0]
    piece_ref[0, :count] = high
    piece_ref[1, :count] = value - high
    hits = [hot_ref[:, p * cols : (p + 1) * cols] > 0 for p in range(npw)]
    none = jnp.zeros((rows, cols), BF16)
    lane = lax.broadcasted_iota(jnp.int32, row_ref.shape, 1)

    def left(part, first):
        lanes = []
        for comp in range(2):
            for p in range(npw):
                column = []
                for b in range(per):
                    for z in range(zs):
                        at = ((first + b) * npw + p) * 2 * zs + comp * zs + z
                        line = piece_ref[part, pl.ds(at, 8, stride=0), :]
                        line = jnp.concatenate([line, line], axis=0).astype(BF16)
                        column.append(jnp.where(hits[p], jnp.concatenate([line] * (rows // 16), axis=0), none))
                lanes.append(jnp.concatenate(column, axis=0))
        return jnp.concatenate(lanes, axis=1)

    def step(first, carry):
        dens, energy = carry
        dens = list(dens)
        grid = dot(left(0, first), e_ref[...])
        grid = grid[:, : 2 * m] + grid[:, 2 * m :] + dot(left(1, first), e_ref[:, : 2 * m])
        grids = [part for value in (grid, turned(grid, m)) for part in split(value)]

        def stack(b, z):
            at = (b * zs + z) * rows
            parts = [grids[k][at : at + rows] for k in (0, 2, 1, 3, 0, 2)]
            return jnp.concatenate(parts, axis=0)

        group = 2 if zs % 2 == 0 else 1
        for b in range(per):
            acc = jnp.zeros((m, 2 * m), F32)
            for z in range(0, zs, group):
                both = jnp.concatenate([stack(b, z + k) for k in range(group)], axis=1)
                psi = dot(tx_ref[...], both)
                for k in range(group):
                    square = psi[:, k * 2 * m : (k + 1) * 2 * m]
                    square = square * square
                    dens[z + k] = dens[z + k] + square
                    acc = acc + square * v_ref[(z + k) * m : (z + k + 1) * m, :]
            part = jnp.sum(jnp.sum(acc, axis=0, keepdims=True), axis=1, keepdims=True)
            energy = energy + jnp.where(lane == cfg["row"] + first + b, part, 0.0)
        return tuple(dens), energy

    carry = (
        tuple(jnp.zeros((m, 2 * m), F32) for _ in range(zs)),
        hist_ref[...],
    )
    if bands // per <= 2:
        for first in range(0, bands, per):
            carry = step(first, carry)
    else:
        carry = lax.fori_loop(0, bands // per, lambda i, c: step(i * per, c), carry)
    dens, energy = carry
    row_ref[...] = energy
    pk, xr, gz = cfg["pk"], cfg["xr"], cfg["gz"]
    merged = []
    for zp in range(zs // pk):
        if pk == 2 and 2 * m == LANES:
            low, high = dens[zp * pk], dens[zp * pk + 1]
            side = lax.broadcasted_iota(jnp.int32, low.shape, 1) < m
            merged.append(jnp.where(side, low, high) + pltpu.roll(jnp.where(side, high, low), m, 1))
            continue
        folded = []
        for half in range(pk):
            value = dens[zp * pk + half]
            folded.append(value[:, :m] + value[:, m:])
        merged.append(jnp.concatenate(folded, axis=1) if pk > 1 else folded[0])
    high, low = split(jnp.concatenate(merged, axis=1))
    rows_x = dot(ix_ref[...], jnp.concatenate([high, high, low], axis=0))
    for zp in range(zs // pk):
        for g in range(gz):
            at = (cfg["dest"][g] * (zs // pk) + zp) * xr
            out_ref[at : at + xr, :] = rows_x[g * xr : (g + 1) * xr, zp * pk * m : (zp + 1) * pk * m]


def cells_kernel(cfg, in_ref, row_ref, iy_ref, rho_ref, resid_ref, dens_ref, send_ref, work):
    pk, xr, ng = cfg["pk"], cfg["xr"], cfg["ng"]
    count = in_ref.shape[0] // xr
    high, low = split(in_ref[...])
    cells = dot(jnp.concatenate([high, high, low], axis=1), iy_ref[...])
    each = count // cfg["gz"]
    for at in range(count):
        for half in range(pk):
            to = ((cfg["band_order"][at // each] * each + at % each) * pk + half) * xr
            work[to : to + xr, :] = cells[at * xr : (at + 1) * xr, half * ng : (half + 1) * ng]
    hist = resid_ref.shape[0]
    sums = [None] * (hist + 1)
    for x in range(xr):
        at = slice(x * ng, (x + 1) * ng)
        value = work[pl.ds(x, count * pk, stride=xr), :]
        dens_ref[:, at] = value
        last = value - rho_ref[:, at]
        for i in range(hist + 1):
            term = last * (resid_ref[i, :, at] if i < hist else last)
            sums[i] = term if x == 0 else sums[i] + term
    lane = lax.broadcasted_iota(jnp.int32, row_ref.shape, 1)
    row = row_ref[...]
    for i in range(hist + 1):
        value = jnp.sum(jnp.sum(sums[i], axis=0, keepdims=True), axis=1, keepdims=True)
        row = row + jnp.where(lane == i * (hist + 1) + hist, value, 0.0)
    send_ref[...] = jnp.broadcast_to(row, send_ref.shape)


def mix_kernel(
    cfg, in_ref, dens_ref, rho_ref, rho_hist_ref, resid_ref, occ_ref,
    dens_hbm, mixed_hbm, energy_hbm, norm_hbm, mixed_ref, energy_ref, norm_ref, sems,
):
    dens_copy = pltpu.make_async_copy(dens_ref, dens_hbm, sems.at[2])
    dens_copy.start()
    hist = resid_ref.shape[0]
    size = hist + 1
    row = jnp.sum(in_ref[...], axis=0, keepdims=True) * (1.0 / cfg["ng"] ** 3)
    lane = lax.broadcasted_iota(jnp.int32, row.shape, 1)

    def pick(at):
        return jnp.sum(jnp.where(lane == at, row, 0.0), axis=1, keepdims=True)

    gram = {(i, j): pick(i * size + j) for i in range(size) for j in range(i, size)}
    low = {}
    for j in range(size):
        value = gram[(j, j)]
        for k in range(j):
            value = value - low[(j, k)] * low[(j, k)]
        low[(j, j)] = jnp.sqrt(value)
        for i in range(j + 1, size):
            value = gram[(j, i)]
            for k in range(j):
                value = value - low[(i, k)] * low[(j, k)]
            low[(i, j)] = value / low[(j, j)]
    half = []
    for i in range(size):
        value = jnp.ones((1, 1), F32)
        for k in range(i):
            value = value - low[(i, k)] * half[k]
        half.append(value / low[(i, i)])
    solved = [None] * size
    for i in reversed(range(size)):
        value = half[i]
        for k in range(i + 1, size):
            value = value - low[(k, i)] * solved[k]
        solved[i] = value / low[(i, i)]
    total = solved[0]
    for value in solved[1:]:
        total = total + value
    coef = [value / total for value in solved]
    norm_ref[...] = jnp.sqrt(gram[(hist, hist)])
    weight = occ_ref[0].astype(F32) * (1.0 / cfg["bands"])
    energy_ref[...] = pick(cfg["row"] + lax.axis_index("band")) / jnp.full((1, 1), weight, F32)
    planes, width = mixed_ref.shape
    copies = fetch(((energy_ref, energy_hbm), (norm_ref, norm_hbm)), sems) + [dens_copy]
    step = 8
    for at in range(0, planes, step):
        rows = slice(at, at + step)
        for first in range(0, width, 4 * LANES):
            lanes = slice(first, min(first + 4 * LANES, width))
            rho = rho_ref[rows, lanes]
            mixed = coef[hist] * (rho + 0.8 * (dens_ref[rows, lanes] - rho))
            for i in range(hist):
                mixed = mixed + coef[i] * (rho_hist_ref[i, rows, lanes] + 0.8 * resid_ref[i, rows, lanes])
            mixed_ref[rows, lanes] = mixed
        copy = pltpu.make_async_copy(mixed_ref.at[rows, :], mixed_hbm.at[rows, :], sems.at[3 + at // step])
        copy.start()
        copies.append(copy)
    for copy in copies:
        copy.wait()


SPACES = {"u": pltpu.HBM, "v": pltpu.VMEM, "p": pltpu.VMEM, "s": pltpu.SMEM, "h": pltpu.HBM}


def call(kernel, cfg, outs, spaces, out_spaces, scratch, copies, name, limit):
    sems = [pltpu.SemaphoreType.DMA((copies,))] if copies else []
    run = pl.pallas_call(
        lambda *refs: kernel(cfg, *refs),
        out_shape=tuple(
            SPACES[space](out.shape, out.dtype) if space in "hp" else out
            for out, space in zip(outs, out_spaces, strict=True)
        ),
        in_specs=[pl.BlockSpec(memory_space=SPACES[space]) for space in spaces],
        out_specs=tuple(pl.BlockSpec(memory_space=SPACES[space]) for space in out_spaces),
        scratch_shapes=list(scratch) + sems,
        compiler_params=pltpu.CompilerParams(vmem_limit_bytes=limit),
        name=name,
    )

    def placed(*args):
        return run(*(
            pltpu.with_memory_space_constraint(arg, SPACES[space]) if space in "hp" else arg
            for arg, space in zip(args, spaces, strict=True)
        ))

    return placed


def held(*arrays):
    return [pltpu.VMEM(array.shape, array.dtype) for array in arrays]


def slice_x(table, axis, gx, gz, xs):
    if gx == 1:
        return table
    return lax.dynamic_slice_in_dim(table, lax.axis_index("band") // gz * xs, xs, axis)


def build(mesh):
    nband, npw = mesh.shape["band"], mesh.shape["pw"]
    both = ("band", "pw")

    def local(coefficients, pw_index, col_index, occupation, v_local, rho_in, rho_hist, resid_hist):
        bands_dev, _, count = coefficients.shape
        planes, cells = v_local.shape
        ng = planes * npw
        ncol = col_index.shape[0]
        cols = ncol // npw
        hist = resid_hist.shape[0]
        assert bands_dev == 1 and ng * ng == cells and ng == LANES
        bands = nband
        gz = math.gcd(planes, nband)
        gx = nband // gz
        zs, xs, xr = planes // gz, ng // gx, ng // nband
        kz_radius = line_radius(ng, cols, count)
        k_radius = plane_radius(ng, ncol)
        m = ng
        while m % 2 == 0 and m // 2 > 4 * k_radius and zs % (2 * ng // m) == 0:
            m //= 2
        pk = ng // m
        kz_vals, _ = box(ng, kz_radius, 16)
        kz_rows, kz_rest, kz_extra = kz_split(len(kz_vals))
        k_vals, k_rows = box(ng, k_radius, 16)
        if k_rows % 32:
            k_rows = up(k_rows, 32)
        assert count > 1024 and count % 1024 == 0
        chunk_bands = bands
        while chunk_bands % 2 == 0 and chunk_bands * zs * k_rows > 1024:
            chunk_bands //= 2
        cfg = dict(
            ng=ng, ncol=ncol, cols=cols, bands=bands, npw=npw, gz=gz, zs=zs, xs=xs, xr=xr, m=m, pk=pk,
            kz_radius=kz_radius, k_radius=k_radius, kz_real=len(kz_vals), k_rows=k_rows, chunk_bands=chunk_bands,
            row=(hist + 1) ** 2,
        )
        band_order = turned_order(gz)
        cfg.update(dest=inverse(band_order), band_order=band_order)
        turn = 2.0 * math.pi / ng
        z_of = (
            np.arange(npw)[None, :, None] * planes
            + (np.arange(nband) % gz)[:, None, None] * zs
            + np.arange(zs)[None, None, :]
        )
        angle = turn * (z_of[..., None] * kz_vals % ng)
        cz, sz = np.cos(angle), np.sin(angle)
        z_table = np.stack([np.stack([cz, -sz], -2), np.stack([sz, cz], -2)], axis=2)
        z_high, z_low = split_np(z_table.reshape(-1, 2, len(kz_vals)))
        flat = lambda table: table.reshape(table.shape[0], -1)
        main = [flat(table[:, :, :kz_rows]) for table in (z_high, z_low)]
        spare = [flat(table[:, :, kz_rows:]) for table in (z_high, z_low)]
        pad = [np.zeros((z_high.shape[0], kz_extra - 2 * k * kz_rest), z_high.dtype) for k in (2, 1)]
        z_table = jnp.asarray(np.concatenate(
            [main[0], main[0], spare[0], spare[0], pad[0], main[1], spare[1], pad[1]], axis=1
        ))
        angle = turn * pk * (k_vals[:, None] * np.arange(m)[None, :])
        cy, sy = np.zeros((2, k_rows, m))
        cy[: len(k_vals)], sy[: len(k_vals)] = np.cos(angle), np.sin(angle)
        real = split_np(np.concatenate([cy, sy], axis=1))
        imag = split_np(np.concatenate([-sy, cy], axis=1))
        y_table = jnp.asarray(np.concatenate([*real, *imag], axis=1))
        x_high, x_low = split_np(np.concatenate([cy.T, sy.T], axis=1))
        x_table = jnp.asarray(np.concatenate([x_high, x_high, x_low], axis=1))
        inter = interpolation(ng, m)
        iy_twice = jnp.asarray(np.stack(split_np(np.concatenate([inter, inter], axis=1))))
        wide = np.zeros((pk * m, pk * ng))
        for half in range(pk):
            wide[half * m : (half + 1) * m, half * ng : (half + 1) * ng] = inter.T
        w_high, w_low = split_np(wide)
        iy_wide = jnp.asarray(np.concatenate([w_high, w_low, w_high], axis=0))
        x_high, x_low = split_np(inter)
        ix_full = jnp.asarray(np.concatenate([x_high, x_low, x_high], axis=1))
        ixt_full = jnp.asarray(np.stack(split_np(inter.T)))

        index = pw_index.reshape(1, count)
        col = col_index.reshape(1, ncol)
        shape = jax.ShapeDtypeStruct
        width = up(cfg["row"] + bands, LANES)
        mib = 1024 * 1024

        sent_shape = shape((nband * npw * 2 * zs, cols), F32)
        (sent,) = call(
            columns_kernel, cfg, (sent_shape,), "shhh", "h",
            held(index, coefficients, z_table, sent_shape) + [pltpu.SemaphoreType.DMA((5,)), pltpu.SemaphoreType.DMA],
            0, "columns", 40 * mib,
        )(occupation, index, coefficients, z_table)
        received = lax.all_to_all(sent, both, 0, 0, tiled=True)
        block = max(zs, 8)
        assert planes % block == 0 and xs % 8 == 0
        v_block = shape((block, xs * ng), F32)
        ix = slice_x(ix_full, 0, gx, gz, xs)
        e_table, hot, v_grid, hist_row, tx, ix, iy = call(
            tables_kernel, cfg,
            (
                shape((2 * ncol, 4 * m), BF16), shape((k_rows, ncol), BF16), shape((zs * m, 2 * m), F32), shape((1, width), F32),
                x_table, ix, iy_wide,
            ),
            "h" * 9, "ppppppp",
            held(
                col, y_table, iy_twice, ixt_full[:, :, :xs], v_block, resid_hist,
                shape((block * xs, ng), F32),
            ),
            9, "tables", 40 * mib,
        )(col, y_table, iy_twice, slice_x(ixt_full, 2, gx, gz, xs), v_local, resid_hist, x_table, ix, iy_wide)
        to_cells, row = call(
            planes_kernel, cfg, (shape((gz * (zs // pk) * xr, pk * m), F32), shape((1, width), F32)),
            "vpppppp", "pp", held(shape((2, received.shape[0] + 8, cols), F32)), 0, "planes", 40 * mib,
        )(received, hot, e_table, tx, ix, v_grid, hist_row)
        groups = [[g * gz + k for k in band_order] for g in range(gx)]
        mine = lax.all_to_all(to_cells, "band", 0, 0, axis_index_groups=groups, tiled=True)
        dens, rows = call(
            cells_kernel, cfg, (shape(rho_in.shape, F32), shape((nband * npw, width), F32)),
            "vppvv", "pp", [pltpu.VMEM((mine.shape[0] * pk, ng), F32)], 0, "cells", 16 * mib,
        )(mine, row, iy, rho_in, resid_hist)
        rows = lax.all_to_all(rows, both, 0, 0, tiled=True)
        one = shape((1, 1), F32)
        density, mixed, energy, norm = call(
            mix_kernel, cfg, (shape(rho_in.shape, F32), shape(rho_in.shape, F32), one, one),
            "vpvvvs", "hhuu", held(rho_in, one, one), 3 + planes // 8, "mix", 16 * mib,
        )(rows, dens, rho_in, rho_hist, resid_hist, occupation)
        return density, mixed, energy.reshape(1), norm.reshape(())

    return local


def solution(mesh):
    in_specs = (
        P("band", None, "pw"),
        P("pw"),
        P(),
        P("band"),
        P("pw", None),
        P("pw", "band"),
        P(None, "pw", "band"),
        P(None, "pw", "band"),
    )
    out_specs = (P("pw", "band"), P("pw", "band"), P("band"), P())
    return jax.shard_map(build(mesh), mesh=mesh, in_specs=in_specs, out_specs=out_specs, check_vma=False)
```
